256 devices in a mesh: gx: 8 (over y, x_lo), gy: 8 (over z), wa: 4 (over x_hi, core).
Axes of the slice: x: 4 (x_hi: 2, x_lo: 2; x = x_hi * 2 + x_lo), y: 4, z: 8, core: 2. Of those that a mesh axis runs over, the one named last changes fastest.
Arguments:
- adjoint_init: float32 [5, 64, 128, 512], P(None, 'gx', 'gy', 'wa'), may hold values from -6 to 6
- objective_grad: float32 [5, 64, 128, 512], P(None, 'gx', 'gy', 'wa'), may hold values from -6 to 6
- diag_term: float32 [64, 128, 512], P('gx', 'gy', 'wa'), may hold values from 1.5 to 3
- face_metric: float32 [12, 64, 128, 512], P(None, 'gx', 'gy', 'wa'), may hold values from 0.05 to 0.3
- flux_jacobian: bfloat16 [5, 5, 64, 128, 512], P(None, None, 'gx', 'gy', 'wa'), may hold values from -2 to 2
- wall_coef: float32 [3, 10, 64, 128], P(None, None, 'gx', 'gy'), may hold values from -2 to 2
- ffd_ids: int32 [4, 64, 128], P(None, 'gx', 'gy'), may hold values from 0 to 4095
- ffd_weight: float32 [4, 64, 128], P(None, 'gx', 'gy'), may hold values from 0.1 to 1
Outputs:
- adjoint: float32 [5, 64, 128, 512], P(None, 'gx', 'gy', 'wa')
- shape_grad: float32 [3, 4096], P(None, ('gx', 'gy', 'wa'))
The draws below stay inside these ranges and needn't reach their ends.
All inputs are finite; a program needn't handle non-finite values.
Results may differ from the reference program's by a relative error of at most 0.0003.
Values sent between devices are 32-bit elements; how exact they have to be, the bound alone decides.
No kernel may reach another device: no remote copies, remote signals or barrier semaphores. Data moves between devices by JAX's collectives and lax.ppermute only.
A program may use at most 192 MiB of HBM per device.

```python
import math
import jax
import jax.numpy as jnp

FIELDS = 5
OFFS = 12
SWEEPS = 4
POINTS = 4096
NX = 64
NY = 128
NZ = 512


def with_ends(entries, own_key, least, largest):
    extent = entries.shape
    spot = [jax.random.randint(jax.random.fold_in(own_key, axis), (), 0, extent[axis]) for axis in range(len(extent))]
    entries = entries.at[tuple(spot)].set(least)
    longest = extent.index(max(extent))
    spot[longest] = (spot[longest] + 1) % extent[longest]
    return entries.at[tuple(spot)].set(largest)


def steps_of(key, shape, shards, least, high):
    def one(position, shards_of):
        heights = jax.random.uniform(jax.random.fold_in(jax.random.fold_in(key, 6), position), (shards_of,), jnp.float32, least / len(shards), high / len(shards))
        return jnp.repeat(jnp.exp(heights), shape[position] // shards_of).reshape((-1,) + (1,) * (len(shape) - position - 1))

    factor_of = one(*shards[0])
    for cut in shards[1:]:
        factor_of = factor_of * one(*cut)
    return factor_of


def bell_draw(own_key, shape, spread, most, shards=(), dtype=jnp.bfloat16):
    result = spread * jax.random.normal(own_key, shape, jnp.float32)
    if shards:
        result = result * steps_of(own_key, shape, shards, -0.22, 0.18)
    return jnp.clip(result, -most, most).astype(dtype)


def setup_inputs(seed: int = 0) -> dict:
    splits = jax.random.split(jax.random.key(seed), 9)
    adjoint_init = bell_draw(splits[0], (FIELDS, NX, NY, NZ), 1.0, 6.0, ((1, 8), (2, 8), (3, 4)), jnp.float32)
    objective_grad = bell_draw(splits[1], (FIELDS, NX, NY, NZ), 1.0, 6.0, ((1, 8), (2, 8), (3, 4)), jnp.float32)
    diag_term = jnp.clip(1.5 + 1.5 * jax.random.uniform(splits[2], (NX, NY, NZ), jnp.float32) ** steps_of(splits[2], (NX, NY, NZ), ((0, 8), (1, 8), (2, 4)), -0.2, 0.2), 1.5, 3.0)
    face_metric = jnp.clip(jnp.exp(math.log(0.3) - 1.7917595 * jax.random.uniform(splits[3], (OFFS, NX, NY, NZ), jnp.float32) ** steps_of(splits[3], (OFFS, NX, NY, NZ), ((1, 8), (2, 8), (3, 4)), -0.2, 0.2)), 0.05, 0.3)
    flux_jacobian = bell_draw(splits[4], (FIELDS, FIELDS, NX, NY, NZ), 0.5, 2.0, ((2, 8), (3, 8), (4, 4)))
    wall_coef = bell_draw(splits[5], (3, 2 * FIELDS, NX, NY), 0.3, 2.0, ((2, 8), (3, 8)), jnp.float32)
    ffd_ids = with_ends(jax.random.randint(splits[6], (4, NX, NY), 0, POINTS), jax.random.fold_in(splits[6], 1), 0, POINTS - 1).astype(jnp.int32)
    ffd_weight = jnp.clip(0.1 + 0.9 * jax.random.uniform(splits[7], (4, NX, NY), jnp.float32) ** steps_of(splits[7], (4, NX, NY), ((1, 8), (2, 8)), -0.2, 0.2), 0.1, 1.0)
    return {"adjoint_init": adjoint_init, "objective_grad": objective_grad, "diag_term": diag_term, "face_metric": face_metric, "flux_jacobian": flux_jacobian, "wall_coef": wall_coef, "ffd_ids": ffd_ids, "ffd_weight": ffd_weight}


OMEGA = 0.6
OFFSET_LIST = [(1, 1), (1, -1), (1, 2), (1, -2), (2, 1), (2, -1), (2, 2), (2, -2), (3, 1), (3, -1), (3, 2), (3, -2)]


def take_shifted(field, dim, step):
    starts = [0, 2, 2, 2]
    starts[dim] = 2 - step
    limits = [field.shape[0]] + [starts[d] + field.shape[d] - 4 for d in (1, 2, 3)]
    return jax.lax.slice(field, starts, limits)


def sweep(padded_psi, padded_coef, diag, rhs, jac):
    total = jnp.zeros((padded_psi.shape[0],) + tuple(s - 4 for s in padded_psi.shape[1:]), jnp.float32)
    for index, (dim, step) in enumerate(OFFSET_LIST):
        total = total + take_shifted(padded_coef[index][None] * padded_psi, dim, step)
    centre = padded_psi[:, 2:-2, 2:-2, 2:-2]
    coupled = (jac * total[:, None]).sum(0)
    return centre + OMEGA * (rhs - diag * centre + coupled) / diag


def wall_terms(psi, wall_coef, ffd_ids, ffd_weight):
    sens = jnp.zeros(wall_coef.shape[:1] + wall_coef.shape[2:], jnp.float32)
    for field in range(psi.shape[0]):
        for layer in range(2):
            sens = sens + wall_coef[:, 2 * field + layer] * psi[field, :, :, layer][None]
    values = ffd_weight[None] * sens[:, None]
    flat = values.reshape(values.shape[0], -1).T
    summed = jax.ops.segment_sum(flat, ffd_ids.reshape(-1), num_segments=POINTS)
    return summed.T


def reference(adjoint_init, objective_grad, diag_term, face_metric, flux_jacobian, wall_coef, ffd_ids, ffd_weight):
    pad_spec = ((0, 0), (2, 2), (2, 2), (2, 2))
    padded_coef = jnp.pad(face_metric, pad_spec)
    psi = adjoint_init
    for sweep_index in range(SWEEPS):
        psi = sweep(jnp.pad(psi, pad_spec), padded_coef, diag_term[None], objective_grad, flux_jacobian)
    grad = wall_terms(psi, wall_coef, ffd_ids, ffd_weight)
    return psi, grad
```

```python
import jax
import jax.numpy as jnp
from jax import lax
from jax.sharding import PartitionSpec as P

SWEEPS = 4
POINTS = 4096
OMEGA = 0.6
AXES = ("gx", "gy", "wa")


def pairs(count, odd):
    table = {}
    for i in range(0, count, 2):
        a, b = (i + odd) % count, (i + 1 + odd) % count
        table[a], table[b] = b, a
    return sorted(table.items())


def send(high, low, axis):
    count = lax.axis_size(axis)
    even = lax.axis_index(axis) % 2 == 0
    first = lax.ppermute(jnp.where(even, high, low), axis, pairs(count, 0))
    second = lax.ppermute(jnp.where(even, low, high), axis, pairs(count, 1))
    return first, second


def receive(first, second, axis):
    count = lax.axis_size(axis)
    index = lax.axis_index(axis)
    even = index % 2 == 0
    below = jnp.where(even, second, first) * (index > 0).astype(jnp.float32)
    above = jnp.where(even, first, second) * (index < count - 1).astype(jnp.float32)
    return below, above


def part(a, dim, start, stop):
    return lax.slice_in_dim(a, start, stop, axis=dim)


def padded(a, dim, before, after):
    widths = [(0, 0)] * a.ndim
    widths[dim] = (before, after)
    return jnp.pad(a, widths)


def sweep(psi, metric, diag, rhs, jac):
    flights = []
    for axis, dim, base in (("wa", 3, 8), ("gy", 2, 4), ("gx", 1, 0)):
        n = psi.shape[dim]
        def term(o, start, stop):
            return part(metric[base + o][None], dim, start, stop) * part(psi, dim, start, stop)
        high = jnp.concatenate([term(0, n - 1, n) + term(2, n - 2, n - 1), term(2, n - 1, n)], axis=dim)
        low = jnp.concatenate([term(3, 0, 1), term(1, 0, 1) + term(3, 1, 2)], axis=dim)
        flights.append(send(high, low, axis))
    z = jnp.zeros_like(psi)
    for dim, base in ((1, 0), (2, 4), (3, 8)):
        n = psi.shape[dim]
        for o, step in enumerate((1, -1, 2, -2)):
            p = metric[base + o][None] * psi
            if step > 0:
                z = z + padded(part(p, dim, 0, n - step), dim, step, 0)
            else:
                z = z + padded(part(p, dim, -step, n), dim, 0, -step)
    for (first, second), (axis, dim) in zip(flights, (("wa", 3), ("gy", 2), ("gx", 1))):
        n = psi.shape[dim]
        below, above = receive(first, second, axis)
        z = z + padded(below, dim, 0, n - 2) + padded(above, dim, n - 2, 0)
    coupled = (jac * z[:, None]).sum(0)
    return psi + OMEGA * (rhs - diag * psi + coupled) / diag


def local(adjoint_init, objective_grad, diag_term, face_metric, flux_jacobian, wall_coef, ffd_ids, ffd_weight):
    psi = adjoint_init
    for _ in range(SWEEPS):
        psi = sweep(psi, face_metric, diag_term[None], objective_grad, flux_jacobian)
    wall_on = (lax.axis_index("wa") == 0).astype(jnp.float32)
    sens = jnp.zeros(wall_coef.shape[:1] + wall_coef.shape[2:], jnp.float32)
    for field in range(psi.shape[0]):
        for layer in range(2):
            sens = sens + wall_coef[:, 2 * field + layer] * psi[field, :, :, layer][None]
    values = ffd_weight[None] * sens[:, None] * wall_on
    flat = values.reshape(values.shape[0], -1).T
    summed = jax.ops.segment_sum(flat, ffd_ids.reshape(-1), num_segments=POINTS)
    owners = lax.axis_size(AXES)
    slots = jnp.swapaxes(summed.reshape(owners, POINTS // owners, -1), 1, 2).reshape(owners, 1, -1)
    got = lax.all_to_all(slots, AXES, 0, 0)
    return psi, got.sum((0, 1)).reshape(wall_coef.shape[0], -1)


def solution(mesh):
    in_specs = (
        P(None, "gx", "gy", "wa"),
        P(None, "gx", "gy", "wa"),
        P("gx", "gy", "wa"),
        P(None, "gx", "gy", "wa"),
        P(None, None, "gx", "gy", "wa"),
        P(None, None, "gx", "gy"),
        P(None, "gx", "gy"),
        P(None, "gx", "gy"),
    )
    out_specs = (P(None, "gx", "gy", "wa"), P(None, AXES))
    return jax.shard_map(local, mesh=mesh, in_specs=in_specs, out_specs=out_specs, check_vma=False)
```

```python
import jax
import jax.numpy as jnp
from jax import lax
from jax.experimental import pallas as pl
from jax.experimental.pallas import tpu as pltpu
from jax.sharding import PartitionSpec as P

SWEEPS = 4
OMEGA = 0.6
AXES = ("gx", "gy", "wa")
FIELDS, NX, NY, NZ = 5, 8, 16, 128
ROWS = NX * NY
F32 = jnp.float32
VMEM = pl.BlockSpec(memory_space=pltpu.VMEM)


def pairs(count, odd):
    table = {}
    for i in range(0, count, 2):
        a, b = (i + odd) % count, (i + 1 + odd) % count
        table[a], table[b] = b, a
    return sorted(table.items())


def iota(shape, dim):
    return lax.broadcasted_iota(jnp.int32, shape, dim)


def lane_roll(v, shift):
    return pltpu.roll(v, shift % NZ, axis=1) if shift % NZ else v


def row_roll(v, shift):
    return pltpu.roll(v, shift % v.shape[0], axis=0)


def is_even(axis):
    return lax.axis_index(axis) % 2 == 0


def slab(x):
    return slice(NY * x, NY * (x + 1))


def edge_rows(y):
    return pl.ds(y, NX, stride=NY)


def tile_rows(x, t):
    return slice(NY * x + 8 * t, NY * x + 8 * t + 8)


def pack_edges(psi_ref):
    lane = iota((8, NZ), 1)
    edge = (lane < 2) | (lane >= NZ - 2)
    groups = []
    for g in range((FIELDS + 1) // 2):
        total = jnp.zeros((8, NZ), F32)
        for e in range(2 * g, min(2 * g + 2, FIELDS)):
            for x in range(NX):
                for t in range(2):
                    v = jnp.where(edge, psi_ref[e, tile_rows(x, t), :], 0.0)
                    total = total + lane_roll(v, 2 + 64 * (e % 2) + 4 * (2 * x + t))
        groups.append(total)
    return groups


def pack_metric(metric_ref, out_ref):
    lane = iota((8, NZ), 1)
    same = jnp.zeros((8, NZ), F32)
    after = jnp.zeros((8, NZ), F32)
    before = jnp.zeros((8, NZ), F32)
    for x in range(NX):
        for t in range(2):
            j, rows = 4 * (2 * x + t), tile_rows(x, t)
            v = jnp.where(lane >= NZ - 2, metric_ref[10, rows, :], jnp.where(lane < 2, metric_ref[11, rows, :], 0.0))
            same = same + lane_roll(v, 2 + j)
            after = after + lane_roll(jnp.where(lane == NZ - 1, metric_ref[8, rows, :], 0.0), 1 + j)
            before = before + lane_roll(jnp.where(lane == 0, metric_ref[9, rows, :], 0.0), 3 + j)
    for i, v in enumerate((same, after, before)):
        out_ref[8 * i : 8 * i + 8, :] = v + lane_roll(v, 64)


def emit_sends(psi_ref, metric_ref, packed_metric, groups, sends):
    x0, x1, y0, y1, zz = sends
    lane = iota((8, NZ), 1)
    same, after, before = (packed_metric[8 * i : 8 * i + 8, :] for i in range(3))
    for g, p in enumerate(groups):
        v = same * p + after * lane_roll(p, -1) + before * lane_roll(p, 1)
        zz[8 * g : 8 * g + 8, :] = jnp.where(lane % 4 < 2, lane_roll(v, -2), lane_roll(v, 2))
    even = is_even("gy")
    m4, m6a, m6b = metric_ref[4, edge_rows(15), :], metric_ref[6, edge_rows(14), :], metric_ref[6, edge_rows(15), :]
    m5, m7a, m7b = metric_ref[5, edge_rows(0), :], metric_ref[7, edge_rows(0), :], metric_ref[7, edge_rows(1), :]
    for e in range(FIELDS):
        q14, q15 = psi_ref[e, edge_rows(14), :], psi_ref[e, edge_rows(15), :]
        q0, q1 = psi_ref[e, edge_rows(0), :], psi_ref[e, edge_rows(1), :]
        high = (m4 * q15 + m6a * q14, m6b * q15)
        low = (m7a * q0, m5 * q0 + m7b * q1)
        for r in range(2):
            y0[e, r] = jnp.where(even, high[r], low[r])
            y1[e, r] = jnp.where(even, low[r], high[r])
    even = is_even("gx")
    last, near = slab(NX - 1), slab(NX - 2)
    m0, m2a, m2b = metric_ref[0, last, :], metric_ref[2, near, :], metric_ref[2, last, :]
    m1, m3a, m3b = metric_ref[1, slab(0), :], metric_ref[3, slab(0), :], metric_ref[3, slab(1), :]
    for e in range(FIELDS):
        q6, q7, q0, q1 = psi_ref[e, near, :], psi_ref[e, last, :], psi_ref[e, slab(0), :], psi_ref[e, slab(1), :]
        high = (m0 * q7 + m2a * q6, m2b * q7)
        low = (m3a * q0, m1 * q0 + m3b * q1)
        for r in range(2):
            x0[e, r] = jnp.where(even, high[r], low[r])
            x1[e, r] = jnp.where(even, low[r], high[r])


def first_body(psi_ref, metric_ref, x0, x1, y0, y1, zz, packed_metric):
    pack_metric(metric_ref, packed_metric)
    emit_sends(psi_ref, metric_ref, packed_metric, pack_edges(psi_ref), (x0, x1, y0, y1, zz))


def inner_body(psi_ref, metric_ref, z_ref):
    lane, row = iota((NY, NZ), 1), iota((NY, NZ), 0)
    for x in range(NX):
        s = slab(x)
        ms = []
        for o, keep in (
            (4, row < NY - 1), (5, row >= 1), (6, row < NY - 2), (7, row >= 2),
            (8, lane < NZ - 1), (9, lane >= 1), (10, lane < NZ - 2), (11, lane >= 2),
        ):
            ms.append(jnp.where(keep, metric_ref[o, s, :], 0.0))
        for e in range(FIELDS):
            q = psi_ref[e, s, :]
            total = row_roll(ms[0] * q, 1) + row_roll(ms[1] * q, -1)
            total = total + (row_roll(ms[2] * q, 2) + row_roll(ms[3] * q, -2))
            total = total + (lane_roll(ms[4] * q, 1) + lane_roll(ms[5] * q, -1))
            total = total + (lane_roll(ms[6] * q, 2) + lane_roll(ms[7] * q, -2))
            for o, step in enumerate((1, -1, 2, -2)):
                if 0 <= x - step < NX:
                    total = total + metric_ref[o, slab(x - step), :] * psi_ref[e, slab(x - step), :]
            z_ref[e, s, :] = total


def from_sides(axis, first, second):
    index = lax.axis_index(axis)
    even = index % 2 == 0
    below = jnp.where(even, second, first)
    above = jnp.where(even, first, second)
    return jnp.where(index > 0, below, 0.0), jnp.where(index < lax.axis_size(axis) - 1, above, 0.0)


def update(psi_ref, z_ref, received, diag_ref, rhs_ref, jac_ref, new_ref, total_ref):
    x0, x1, y0, y1, z0, z1 = received
    lane8 = iota((8, NZ), 1)
    edge = (lane8 < 2) | (lane8 >= NZ - 2)
    for g in range((FIELDS + 1) // 2):
        rows = slice(8 * g, 8 * g + 8)
        below, above = from_sides("wa", z0[rows, :], z1[rows, :])
        both = jnp.where(lane8 % 4 >= 2, below, above)
        for e in range(2 * g, min(2 * g + 2, FIELDS)):
            for x in range(NX):
                for t in range(2):
                    shift = -(2 + 64 * (e % 2) + 4 * (2 * x + t))
                    total_ref[e, tile_rows(x, t), :] = z_ref[e, tile_rows(x, t), :] + jnp.where(edge, lane_roll(both, shift), 0.0)
    for e in range(FIELDS):
        for r in range(2):
            below, above = from_sides("gx", x0[e, r], x1[e, r])
            total_ref[e, slab(r), :] += below
            total_ref[e, slab(NX - 2 + r), :] += above
        for r in range(2):
            below, above = from_sides("gy", y0[e, r], y1[e, r])
            total_ref[e, edge_rows(r), :] += below
            total_ref[e, edge_rows(NY - 2 + r), :] += above
    for x in range(NX):
        s = slab(x)
        d = diag_ref[s, :]
        scale = OMEGA / d
        zs = [total_ref[e, s, :] for e in range(FIELDS)]
        for f in range(FIELDS):
            c = jac_ref[f, s, :].astype(F32) * zs[0]
            for e in range(1, FIELDS):
                c = c + jac_ref[FIELDS * e + f, s, :].astype(F32) * zs[e]
            q = psi_ref[f, s, :]
            new_ref[f, s, :] = q + (rhs_ref[f, s, :] - d * q + c) * scale


def middle_body(psi_ref, z_ref, r0, r1, r2, r3, r4, r5, diag_ref, rhs_ref, jac_ref, metric_ref, packed_metric,
                new_ref, x0, x1, y0, y1, zz, total_ref):
    update(psi_ref, z_ref, (r0, r1, r2, r3, r4, r5), diag_ref, rhs_ref, jac_ref, new_ref, total_ref)
    emit_sends(new_ref, metric_ref, packed_metric, pack_edges(new_ref), (x0, x1, y0, y1, zz))


def wall_body(coef_ref, ids_ref, weight_ref, coef_out, weight_out, hot_out, low_out):
    def spread(rows, place):
        at = lax.broadcasted_iota(jnp.int32, (rows, 2 * NZ), 1)
        r = lax.broadcasted_iota(jnp.int32, (rows, 2 * NZ), 0)
        return (at % NZ == place(r) + 4 * (at // NZ)).astype(F32)

    def packed(table, chooser):
        v = lax.dot_general(table, chooser, (((0,), (0,)), ((), ())), precision=lax.Precision.HIGHEST,
                            preferred_element_type=F32)
        return v[:8, :NZ] + v[8:, NZ:]

    chooser = spread(4 * NX, lambda r: 64 * (r // 16) + 8 * (r % NX) + 2 + (r // NX) % 2)
    for c in range(3):
        for g in range((FIELDS + 1) // 2):
            count = 4 * NX if g < FIELDS // 2 else 2 * NX
            start = c * 10 * NX + g * 4 * NX
            coef_out[c, 8 * g : 8 * g + 8, :] = packed(coef_ref[start : start + count, :], chooser[:count])
    chooser = spread(4 * NX, lambda r: 8 * (r % NX) + r // NX)
    lane, row = iota((8, NZ), 1), iota((8, NZ), 0)

    def halves(v):
        return jnp.where(lane < 64, v, lane_roll(row_roll(v, 4), 64))

    on = jnp.where(lax.axis_index("wa") == 0, 1.0, 0.0)
    weight_out[...] = halves(packed(weight_ref[...], chooser)) * on
    ids = halves(packed(ids_ref[...].astype(F32), chooser)).astype(jnp.int32)
    low_out[...] = ids % 16
    owner = ids // 16
    slot = iota((256, NZ), 0)
    for s in range(4):
        hit = slot == jnp.broadcast_to(owner[s : s + 1, :], (256, NZ))
        hot_out[:, NZ * s : NZ * s + NZ] = jnp.where(hit, 1.0, 0.0).astype(jnp.bfloat16)


def last_body(psi_ref, z_ref, r0, r1, r2, r3, r4, r5, diag_ref, rhs_ref, jac_ref, coef_ref, weight_ref, hot_ref, low_ref,
              new_ref, slots_ref, total_ref, high_part, low_part):
    update(psi_ref, z_ref, (r0, r1, r2, r3, r4, r5), diag_ref, rhs_ref, jac_ref, new_ref, total_ref)
    lane = iota((8, NZ), 1)
    groups = pack_edges(new_ref)
    low = low_ref[...]
    point = iota((16, NZ), 0)
    for c in range(3):
        v = coef_ref[c, 0:8, :] * groups[0]
        for g in range(1, len(groups)):
            v = v + coef_ref[c, 8 * g : 8 * g + 8, :] * groups[g]
        v = v + lane_roll(v, 64)
        v = jnp.where(lane % 4 == 3, v + lane_roll(v, 1), 0.0)
        v = v + lane_roll(v, -1)
        v = v + lane_roll(v, -2)
        v = jnp.where(lane < 64, v, row_roll(v, 4)) * weight_ref[...]
        for s in range(4):
            here = point == jnp.broadcast_to(low[s : s + 1, :], (16, NZ))
            w = jnp.where(here, jnp.broadcast_to(v[s : s + 1, :], (16, NZ)), 0.0)
            top = w.astype(jnp.bfloat16)
            at = (slice(16 * c, 16 * c + 16), slice(NZ * s, NZ * s + NZ))
            high_part[at] = top
            low_part[at] = (w - top.astype(F32)).astype(jnp.bfloat16)
    high_part[48:, :] = jnp.zeros((NZ - 48, 512), jnp.bfloat16)
    low_part[48:, :] = jnp.zeros((NZ - 48, 512), jnp.bfloat16)
    hot = hot_ref[...]
    dims = (((1,), (1,)), ((), ()))
    slots_ref[...] = lax.dot_general(hot, high_part[...], dims, preferred_element_type=F32) + lax.dot_general(
        hot, low_part[...], dims, preferred_element_type=F32
    )


def sum_body(got_ref, out_ref):
    v = got_ref[...].sum(axis=0, keepdims=True)
    v = jnp.broadcast_to(v, (8, NZ))
    for c in range(3):
        out_ref[c : c + 1, :] = lane_roll(v, -16 * c)[0:1, :16]


def run(body, args, *rest, **kw):
    shapes = [jax.ShapeDtypeStruct(s, d) for s, d in rest[0]]
    return pl.pallas_call(
        body,
        out_shape=shapes,
        in_specs=[VMEM] * len(args),
        out_specs=[VMEM] * len(shapes),
        scratch_shapes=[pltpu.VMEM(s, d) for s, d in kw.get("scratch", ())],
        compiler_params=pltpu.CompilerParams(vmem_limit_bytes=24 << 20),
        cost_estimate=pl.CostEstimate(flops=kw.get("flops", 1000000), bytes_accessed=kw.get("traffic", 1000000), transcendentals=0),
    )(*args)


EDGE_X = ((FIELDS, 2, NY, NZ), F32)
EDGE_Y = ((FIELDS, 2, NX, NZ), F32)
EDGE_Z = ((24, NZ), F32)
SENDS = [EDGE_X, EDGE_X, EDGE_Y, EDGE_Y, EDGE_Z]
FIELD = ((FIELDS, ROWS, NZ), F32)


def exchange(sends):
    x0, x1, y0, y1, zz = sends
    def swap(v, axis, odd):
        return lax.ppermute(v, axis, pairs(lax.axis_size(axis), odd))
    z = swap(zz, "wa", 0), swap(zz, "wa", 1)
    y = swap(y0, "gy", 0), swap(y1, "gy", 1)
    x = swap(x0, "gx", 0), swap(x1, "gx", 1)
    return (*x, *y, *z)


def local(adjoint_init, objective_grad, diag_term, face_metric, flux_jacobian, wall_coef, ffd_ids, ffd_weight):
    psi = adjoint_init.reshape(FIELDS, ROWS, NZ)
    rhs = objective_grad.reshape(FIELDS, ROWS, NZ)
    diag = diag_term.reshape(ROWS, NZ)
    metric = face_metric.reshape(12, ROWS, NZ)
    jac = flux_jacobian.reshape(FIELDS * FIELDS, ROWS, NZ)
    *sends, packed_metric = run(first_body, (psi, metric), SENDS + [((24, NZ), F32)])
    wall = run(
        wall_body,
        (wall_coef.reshape(30 * NX, NY), ffd_ids.reshape(4 * NX, NY), ffd_weight.reshape(4 * NX, NY)),
        [((3, 24, NZ), F32), ((8, NZ), F32), ((256, 512), jnp.bfloat16), ((8, NZ), jnp.int32)],
    )
    for step in range(SWEEPS):
        received = exchange(sends)
        (z,) = run(inner_body, (psi, metric), [FIELD])
        if step < SWEEPS - 1:
            psi, *sends = run(
                middle_body, (psi, z, *received, diag, rhs, jac, metric, packed_metric), [FIELD] + SENDS, scratch=[FIELD]
            )
        else:
            psi, slots = run(
                last_body, (psi, z, *received, diag, rhs, jac, *wall), [FIELD, ((256, NZ), F32)],
                scratch=[FIELD, ((NZ, 512), jnp.bfloat16), ((NZ, 512), jnp.bfloat16)],
            )
    got = lax.all_to_all(slots.reshape(256, 1, NZ), AXES, 0, 0).reshape(256, NZ)
    (grad,) = run(sum_body, (got,), [((3, 16), F32)])
    return psi.reshape(adjoint_init.shape), grad


def solution(mesh):
    in_specs = (
        P(None, "gx", "gy", "wa"),
        P(None, "gx", "gy", "wa"),
        P("gx", "gy", "wa"),
        P(None, "gx", "gy", "wa"),
        P(None, None, "gx", "gy", "wa"),
        P(None, None, "gx", "gy"),
        P(None, "gx", "gy"),
        P(None, "gx", "gy"),
    )
    out_specs = (P(None, "gx", "gy", "wa"), P(None, AXES))
    return jax.shard_map(local, mesh=mesh, in_specs=in_specs, out_specs=out_specs, check_vma=False)
```

```python
import jax
import jax.numpy as jnp
from jax import lax
from jax.experimental import pallas as pl
from jax.experimental.pallas import tpu as pltpu
from jax.sharding import PartitionSpec as P

SWEEPS = 4
OMEGA = 0.6
AXES = ("gx", "gy", "wa")
FIELDS, NX, NY, NZ = 5, 8, 16, 128
ROWS = NX * NY
F32 = jnp.float32
VMEM = pl.BlockSpec(memory_space=pltpu.VMEM)


def pairs(count, odd):
    table = {}
    for i in range(0, count, 2):
        a, b = (i + odd) % count, (i + 1 + odd) % count
        table[a], table[b] = b, a
    return sorted(table.items())


def iota(shape, dim):
    return lax.broadcasted_iota(jnp.int32, shape, dim)


def lane_roll(v, shift):
    return pltpu.roll(v, shift % NZ, axis=1) if shift % NZ else v


def row_roll(v, shift):
    return pltpu.roll(v, shift % v.shape[0], axis=0)


def is_even(axis):
    return lax.axis_index(axis) % 2 == 0


def slab(x):
    return slice(NY * x, NY * (x + 1))


def edge_rows(y):
    return pl.ds(y, NX, stride=NY)


def tile_rows(x, t):
    return slice(NY * x + 8 * t, NY * x + 8 * t + 8)


def pack_edges(psi_ref):
    lane = iota((8, NZ), 1)
    edge = (lane < 2) | (lane >= NZ - 2)
    groups = []
    for g in range((FIELDS + 1) // 2):
        total = jnp.zeros((8, NZ), F32)
        for e in range(2 * g, min(2 * g + 2, FIELDS)):
            for x in range(NX):
                for t in range(2):
                    v = jnp.where(edge, psi_ref[e, tile_rows(x, t), :], 0.0)
                    total = total + lane_roll(v, 2 + 64 * (e % 2) + 4 * (2 * x + t))
        groups.append(total)
    return groups


def pack_metric(metric_ref, out_ref):
    lane = iota((8, NZ), 1)
    same = jnp.zeros((8, NZ), F32)
    after = jnp.zeros((8, NZ), F32)
    before = jnp.zeros((8, NZ), F32)
    for x in range(NX):
        for t in range(2):
            j, rows = 4 * (2 * x + t), tile_rows(x, t)
            v = jnp.where(lane >= NZ - 2, metric_ref[10, rows, :], jnp.where(lane < 2, metric_ref[11, rows, :], 0.0))
            same = same + lane_roll(v, 2 + j)
            after = after + lane_roll(jnp.where(lane == NZ - 1, metric_ref[8, rows, :], 0.0), 1 + j)
            before = before + lane_roll(jnp.where(lane == 0, metric_ref[9, rows, :], 0.0), 3 + j)
    for i, v in enumerate((same, after, before)):
        out_ref[8 * i : 8 * i + 8, :] = v + lane_roll(v, 64)


def emit_sends(psi_ref, metric_ref, packed_metric, groups, sends):
    x0, x1, y0, y1, zz = sends
    lane = iota((8, NZ), 1)
    same, after, before = (packed_metric[8 * i : 8 * i + 8, :] for i in range(3))
    for g, p in enumerate(groups):
        v = same * p + after * lane_roll(p, -1) + before * lane_roll(p, 1)
        zz[8 * g : 8 * g + 8, :] = jnp.where(lane % 4 < 2, lane_roll(v, -2), lane_roll(v, 2))
    even = is_even("gy")
    m4, m6a, m6b = metric_ref[4, edge_rows(15), :], metric_ref[6, edge_rows(14), :], metric_ref[6, edge_rows(15), :]
    m5, m7a, m7b = metric_ref[5, edge_rows(0), :], metric_ref[7, edge_rows(0), :], metric_ref[7, edge_rows(1), :]
    for e in range(FIELDS):
        q14, q15 = psi_ref[e, edge_rows(14), :], psi_ref[e, edge_rows(15), :]
        q0, q1 = psi_ref[e, edge_rows(0), :], psi_ref[e, edge_rows(1), :]
        high = (m4 * q15 + m6a * q14, m6b * q15)
        low = (m7a * q0, m5 * q0 + m7b * q1)
        for r in range(2):
            y0[e, r] = jnp.where(even, high[r], low[r])
            y1[e, r] = jnp.where(even, low[r], high[r])
    even = is_even("gx")
    last, near = slab(NX - 1), slab(NX - 2)
    m0, m2a, m2b = metric_ref[0, last, :], metric_ref[2, near, :], metric_ref[2, last, :]
    m1, m3a, m3b = metric_ref[1, slab(0), :], metric_ref[3, slab(0), :], metric_ref[3, slab(1), :]
    for e in range(FIELDS):
        q6, q7, q0, q1 = psi_ref[e, near, :], psi_ref[e, last, :], psi_ref[e, slab(0), :], psi_ref[e, slab(1), :]
        high = (m0 * q7 + m2a * q6, m2b * q7)
        low = (m3a * q0, m1 * q0 + m3b * q1)
        for r in range(2):
            x0[e, r] = jnp.where(even, high[r], low[r])
            x1[e, r] = jnp.where(even, low[r], high[r])


def first_body(psi_ref, metric_ref, x0, x1, y0, y1, zz, packed_metric):
    pack_metric(metric_ref, packed_metric)
    emit_sends(psi_ref, metric_ref, packed_metric, pack_edges(psi_ref), (x0, x1, y0, y1, zz))


def inner_body(psi_ref, metric_ref, z_ref):
    lane, row = iota((NY, NZ), 1), iota((NY, NZ), 0)
    for x in range(NX):
        s = slab(x)
        ms = []
        for o, keep in (
            (4, row < NY - 1), (5, row >= 1), (6, row < NY - 2), (7, row >= 2),
            (8, lane < NZ - 1), (9, lane >= 1), (10, lane < NZ - 2), (11, lane >= 2),
        ):
            ms.append(jnp.where(keep, metric_ref[o, s, :], 0.0))
        for e in range(FIELDS):
            q = psi_ref[e, s, :]
            total = row_roll(ms[0] * q, 1) + row_roll(ms[1] * q, -1)
            total = total + (row_roll(ms[2] * q, 2) + row_roll(ms[3] * q, -2))
            total = total + (lane_roll(ms[4] * q, 1) + lane_roll(ms[5] * q, -1))
            total = total + (lane_roll(ms[6] * q, 2) + lane_roll(ms[7] * q, -2))
            for o, step in enumerate((1, -1, 2, -2)):
                if 0 <= x - step < NX:
                    total = total + metric_ref[o, slab(x - step), :] * psi_ref[e, slab(x - step), :]
            z_ref[e, s, :] = total


def from_sides(axis, first, second):
    index = lax.axis_index(axis)
    even = index % 2 == 0
    below = jnp.where(even, second, first)
    above = jnp.where(even, first, second)
    return jnp.where(index > 0, below, 0.0), jnp.where(index < lax.axis_size(axis) - 1, above, 0.0)


def update(psi_ref, z_ref, received, diag_ref, rhs_ref, jac_ref, new_ref, total_ref):
    x0, x1, y0, y1, z0, z1 = received
    lane8 = iota((8, NZ), 1)
    edge = (lane8 < 2) | (lane8 >= NZ - 2)
    for g in range((FIELDS + 1) // 2):
        rows = slice(8 * g, 8 * g + 8)
        below, above = from_sides("wa", z0[rows, :], z1[rows, :])
        both = jnp.where(lane8 % 4 >= 2, below, above)
        for e in range(2 * g, min(2 * g + 2, FIELDS)):
            for x in range(NX):
                for t in range(2):
                    shift = -(2 + 64 * (e % 2) + 4 * (2 * x + t))
                    total_ref[e, tile_rows(x, t), :] = z_ref[e, tile_rows(x, t), :] + jnp.where(edge, lane_roll(both, shift), 0.0)
    for e in range(FIELDS):
        for r in range(2):
            below, above = from_sides("gx", x0[e, r], x1[e, r])
            total_ref[e, slab(r), :] += below
            total_ref[e, slab(NX - 2 + r), :] += above
        for r in range(2):
            below, above = from_sides("gy", y0[e, r], y1[e, r])
            total_ref[e, edge_rows(r), :] += below
            total_ref[e, edge_rows(NY - 2 + r), :] += above
    for x in range(NX):
        s = slab(x)
        d = diag_ref[s, :]
        scale = OMEGA / d
        zs = [total_ref[e, s, :] for e in range(FIELDS)]
        for f in range(FIELDS):
            c = jac_ref[f, s, :].astype(F32) * zs[0]
            for e in range(1, FIELDS):
                c = c + jac_ref[FIELDS * e + f, s, :].astype(F32) * zs[e]
            q = psi_ref[f, s, :]
            new_ref[f, s, :] = q + (rhs_ref[f, s, :] - d * q + c) * scale


def middle_body(psi_ref, z_ref, r0, r1, r2, r3, r4, r5, diag_ref, rhs_ref, jac_ref, metric_ref, packed_metric,
                new_ref, x0, x1, y0, y1, zz, total_ref):
    update(psi_ref, z_ref, (r0, r1, r2, r3, r4, r5), diag_ref, rhs_ref, jac_ref, new_ref, total_ref)
    emit_sends(new_ref, metric_ref, packed_metric, pack_edges(new_ref), (x0, x1, y0, y1, zz))


def wall_body(coef_ref, ids_ref, weight_ref, coef_out, weight_out, hot_out, low_out):
    def spread(rows, place):
        at = lax.broadcasted_iota(jnp.int32, (rows, 2 * NZ), 1)
        r = lax.broadcasted_iota(jnp.int32, (rows, 2 * NZ), 0)
        return (at % NZ == place(r) + 4 * (at // NZ)).astype(F32)

    def packed(table, chooser):
        v = lax.dot_general(table, chooser, (((0,), (0,)), ((), ())), precision=lax.Precision.HIGHEST,
                            preferred_element_type=F32)
        return v[:8, :NZ] + v[8:, NZ:]

    chooser = spread(4 * NX, lambda r: 64 * (r // 16) + 8 * (r % NX) + 2 + (r // NX) % 2)
    for c in range(3):
        for g in range((FIELDS + 1) // 2):
            count = 4 * NX if g < FIELDS // 2 else 2 * NX
            start = c * 10 * NX + g * 4 * NX
            coef_out[c, 8 * g : 8 * g + 8, :] = packed(coef_ref[start : start + count, :], chooser[:count])
    chooser = spread(4 * NX, lambda r: 8 * (r % NX) + r // NX)
    lane, row = iota((8, NZ), 1), iota((8, NZ), 0)

    def halves(v):
        return jnp.where(lane < 64, v, lane_roll(row_roll(v, 4), 64))

    on = jnp.where(lax.axis_index("wa") == 0, 1.0, 0.0)
    weight_out[...] = halves(packed(weight_ref[...], chooser)) * on
    ids = halves(packed(ids_ref[...].astype(F32), chooser)).astype(jnp.int32)
    low_out[...] = ids % 16
    owner = ids // 16
    slot = iota((256, NZ), 0)
    for s in range(4):
        hit = slot == jnp.broadcast_to(owner[s : s + 1, :], (256, NZ))
        hot_out[:, NZ * s : NZ * s + NZ] = jnp.where(hit, 1.0, 0.0).astype(jnp.bfloat16)


def last_body(psi_ref, z_ref, r0, r1, r2, r3, r4, r5, diag_ref, rhs_ref, jac_ref, coef_ref, weight_ref, hot_ref, low_ref,
              new_ref, slots_ref, total_ref, high_part, low_part):
    update(psi_ref, z_ref, (r0, r1, r2, r3, r4, r5), diag_ref, rhs_ref, jac_ref, new_ref, total_ref)
    lane = iota((8, NZ), 1)
    groups = pack_edges(new_ref)
    low = low_ref[...]
    point = iota((16, NZ), 0)
    for c in range(3):
        v = coef_ref[c, 0:8, :] * groups[0]
        for g in range(1, len(groups)):
            v = v + coef_ref[c, 8 * g : 8 * g + 8, :] * groups[g]
        v = v + lane_roll(v, 64)
        v = jnp.where(lane % 4 == 3, v + lane_roll(v, 1), 0.0)
        v = v + lane_roll(v, -1)
        v = v + lane_roll(v, -2)
        v = jnp.where(lane < 64, v, row_roll(v, 4)) * weight_ref[...]
        for s in range(4):
            here = point == jnp.broadcast_to(low[s : s + 1, :], (16, NZ))
            w = jnp.where(here, jnp.broadcast_to(v[s : s + 1, :], (16, NZ)), 0.0)
            top = w.astype(jnp.bfloat16)
            at = (slice(16 * c, 16 * c + 16), slice(NZ * s, NZ * s + NZ))
            high_part[at] = top
            low_part[at] = (w - top.astype(F32)).astype(jnp.bfloat16)
    high_part[48:, :] = jnp.zeros((NZ - 48, 512), jnp.bfloat16)
    low_part[48:, :] = jnp.zeros((NZ - 48, 512), jnp.bfloat16)
    hot = hot_ref[...]
    dims = (((1,), (1,)), ((), ()))
    slots_ref[...] = lax.dot_general(hot, high_part[...], dims, preferred_element_type=F32) + lax.dot_general(
        hot, low_part[...], dims, preferred_element_type=F32
    )


def sum_body(got_ref, out_ref):
    v = got_ref[...].sum(axis=0, keepdims=True)
    v = jnp.broadcast_to(v, (8, NZ))
    for c in range(3):
        out_ref[c : c + 1, :] = lane_roll(v, -16 * c)[0:1, :16]


def run(body, args, *rest, **kw):
    shapes = [jax.ShapeDtypeStruct(s, d) for s, d in rest[0]]
    return pl.pallas_call(
        body,
        out_shape=shapes,
        in_specs=[VMEM] * len(args),
        out_specs=[VMEM] * len(shapes),
        scratch_shapes=[pltpu.VMEM(s, d) for s, d in kw.get("scratch", ())],
        compiler_params=pltpu.CompilerParams(vmem_limit_bytes=24 << 20),
        cost_estimate=pl.CostEstimate(flops=kw.get("flops", 1000000), bytes_accessed=kw.get("traffic", 1000000), transcendentals=0),
    )(*args)


EDGE_X = ((FIELDS, 2, NY, NZ), F32)
EDGE_Y = ((FIELDS, 2, NX, NZ), F32)
EDGE_Z = ((24, NZ), F32)
SENDS = [EDGE_X, EDGE_X, EDGE_Y, EDGE_Y, EDGE_Z]
FIELD = ((FIELDS, ROWS, NZ), F32)


def exchange(sends):
    x0, x1, y0, y1, zz = sends
    def swap(v, axis, odd):
        return lax.ppermute(v, axis, pairs(lax.axis_size(axis), odd))
    x = swap(x0, "gx", 0), swap(x1, "gx", 1)
    y = swap(y0, "gy", 0), swap(y1, "gy", 1)
    far = swap(zz, "wa", 1)
    zz, first = lax.optimization_barrier((zz, x[0]))
    x = first, x[1]
    z = swap(zz, "wa", 0), far
    return (*x, *y, *z)


def local(adjoint_init, objective_grad, diag_term, face_metric, flux_jacobian, wall_coef, ffd_ids, ffd_weight):
    psi = adjoint_init.reshape(FIELDS, ROWS, NZ)
    rhs = objective_grad.reshape(FIELDS, ROWS, NZ)
    diag = diag_term.reshape(ROWS, NZ)
    metric = face_metric.reshape(12, ROWS, NZ)
    jac = flux_jacobian.reshape(FIELDS * FIELDS, ROWS, NZ)
    *sends, packed_metric = run(first_body, (psi, metric), SENDS + [((24, NZ), F32)])
    wall = run(
        wall_body,
        (wall_coef.reshape(30 * NX, NY), ffd_ids.reshape(4 * NX, NY), ffd_weight.reshape(4 * NX, NY)),
        [((3, 24, NZ), F32), ((8, NZ), F32), ((256, 512), jnp.bfloat16), ((8, NZ), jnp.int32)],
    )
    for step in range(SWEEPS):
        received = exchange(sends)
        (z,) = run(inner_body, (psi, metric), [FIELD])
        if step < SWEEPS - 1:
            psi, *sends = run(
                middle_body, (psi, z, *received, diag, rhs, jac, metric, packed_metric), [FIELD] + SENDS, scratch=[FIELD]
            )
        else:
            psi, slots = run(
                last_body, (psi, z, *received, diag, rhs, jac, *wall), [FIELD, ((256, NZ), F32)],
                scratch=[FIELD, ((NZ, 512), jnp.bfloat16), ((NZ, 512), jnp.bfloat16)],
            )
    got = lax.all_to_all(slots.reshape(256, 1, NZ), AXES, 0, 0).reshape(256, NZ)
    (grad,) = run(sum_body, (got,), [((3, 16), F32)])
    return psi.reshape(adjoint_init.shape), grad


def solution(mesh):
    in_specs = (
        P(None, "gx", "gy", "wa"),
        P(None, "gx", "gy", "wa"),
        P("gx", "gy", "wa"),
        P(None, "gx", "gy", "wa"),
        P(None, None, "gx", "gy", "wa"),
        P(None, None, "gx", "gy"),
        P(None, "gx", "gy"),
        P(None, "gx", "gy"),
    )
    out_specs = (P(None, "gx", "gy", "wa"), P(None, AXES))
    return jax.shard_map(local, mesh=mesh, in_specs=in_specs, out_specs=out_specs, check_vma=False)
```

```python
import jax
import jax.numpy as jnp
from jax import lax
from jax.experimental import pallas as pl
from jax.experimental.pallas import tpu as pltpu
from jax.sharding import PartitionSpec as P

SWEEPS = 4
OMEGA = 0.6
AXES = ("gx", "gy", "wa")
FIELDS, NX, NY, NZ = 5, 8, 16, 128
ROWS = NX * NY
F32 = jnp.float32
VMEM = pl.BlockSpec(memory_space=pltpu.VMEM)


def pairs(count, odd):
    table = {}
    for i in range(0, count, 2):
        a, b = (i + odd) % count, (i + 1 + odd) % count
        table[a], table[b] = b, a
    return sorted(table.items())


def iota(shape, dim):
    return lax.broadcasted_iota(jnp.int32, shape, dim)


def lane_roll(v, shift):
    return pltpu.roll(v, shift % NZ, axis=1) if shift % NZ else v


def row_roll(v, shift):
    return pltpu.roll(v, shift % v.shape[0], axis=0)


def is_even(axis):
    return lax.axis_index(axis) % 2 == 0


def slab(x):
    return slice(NY * x, NY * (x + 1))


def edge_rows(y):
    return pl.ds(y, NX, stride=NY)


def tile_rows(x, t):
    return slice(NY * x + 8 * t, NY * x + 8 * t + 8)


def pack_edges(psi_ref):
    lane = iota((8, NZ), 1)
    edge = (lane < 2) | (lane >= NZ - 2)
    groups = []
    for g in range((FIELDS + 1) // 2):
        total = jnp.zeros((8, NZ), F32)
        for e in range(2 * g, min(2 * g + 2, FIELDS)):
            for x in range(NX):
                for t in range(2):
                    v = jnp.where(edge, psi_ref[e, tile_rows(x, t), :], 0.0)
                    total = total + lane_roll(v, 2 + 64 * (e % 2) + 4 * (2 * x + t))
        groups.append(total)
    return groups


def pack_metric(metric_ref, out_ref):
    lane = iota((8, NZ), 1)
    same = jnp.zeros((8, NZ), F32)
    after = jnp.zeros((8, NZ), F32)
    before = jnp.zeros((8, NZ), F32)
    for x in range(NX):
        for t in range(2):
            j, rows = 4 * (2 * x + t), tile_rows(x, t)
            v = jnp.where(lane >= NZ - 2, metric_ref[10, rows, :], jnp.where(lane < 2, metric_ref[11, rows, :], 0.0))
            same = same + lane_roll(v, 2 + j)
            after = after + lane_roll(jnp.where(lane == NZ - 1, metric_ref[8, rows, :], 0.0), 1 + j)
            before = before + lane_roll(jnp.where(lane == 0, metric_ref[9, rows, :], 0.0), 3 + j)
    for i, v in enumerate((same, after, before)):
        out_ref[8 * i : 8 * i + 8, :] = v + lane_roll(v, 64)


def emit_sends(psi_ref, metric_ref, packed_metric, groups, sends):
    x0, x1, y0, y1, zz = sends
    lane = iota((8, NZ), 1)
    same, after, before = (packed_metric[8 * i : 8 * i + 8, :] for i in range(3))
    for g, p in enumerate(groups):
        v = same * p + after * lane_roll(p, -1) + before * lane_roll(p, 1)
        zz[8 * g : 8 * g + 8, :] = jnp.where(lane % 4 < 2, lane_roll(v, -2), lane_roll(v, 2))
    even = is_even("gy")
    m4, m6a, m6b = metric_ref[4, edge_rows(15), :], metric_ref[6, edge_rows(14), :], metric_ref[6, edge_rows(15), :]
    m5, m7a, m7b = metric_ref[5, edge_rows(0), :], metric_ref[7, edge_rows(0), :], metric_ref[7, edge_rows(1), :]
    for e in range(FIELDS):
        q14, q15 = psi_ref[e, edge_rows(14), :], psi_ref[e, edge_rows(15), :]
        q0, q1 = psi_ref[e, edge_rows(0), :], psi_ref[e, edge_rows(1), :]
        high = (m4 * q15 + m6a * q14, m6b * q15)
        low = (m7a * q0, m5 * q0 + m7b * q1)
        for r in range(2):
            y0[e, r] = jnp.where(even, high[r], low[r])
            y1[e, r] = jnp.where(even, low[r], high[r])
    even = is_even("gx")
    last, near = slab(NX - 1), slab(NX - 2)
    m0, m2a, m2b = metric_ref[0, last, :], metric_ref[2, near, :], metric_ref[2, last, :]
    m1, m3a, m3b = metric_ref[1, slab(0), :], metric_ref[3, slab(0), :], metric_ref[3, slab(1), :]
    for e in range(FIELDS):
        q6, q7, q0, q1 = psi_ref[e, near, :], psi_ref[e, last, :], psi_ref[e, slab(0), :], psi_ref[e, slab(1), :]
        high = (m0 * q7 + m2a * q6, m2b * q7)
        low = (m3a * q0, m1 * q0 + m3b * q1)
        for r in range(2):
            x0[e, r] = jnp.where(even, high[r], low[r])
            x1[e, r] = jnp.where(even, low[r], high[r])


def first_body(psi_hbm, metric_hbm, x0, x1, y0, y1, zz, packed_metric, psi_ref, metric_ref, sems):
    copies = [
        pltpu.make_async_copy(metric_hbm.at[8:12], metric_ref.at[8:12], sems.at[0]),
        pltpu.make_async_copy(psi_hbm, psi_ref, sems.at[1]),
        pltpu.make_async_copy(metric_hbm.at[4:8], metric_ref.at[4:8], sems.at[2]),
        pltpu.make_async_copy(metric_hbm.at[0:4], metric_ref.at[0:4], sems.at[3]),
    ]
    for copy in copies:
        copy.start()
    copies[0].wait()
    pack_metric(metric_ref, packed_metric)
    copies[1].wait()
    groups = pack_edges(psi_ref)
    copies[2].wait()
    copies[3].wait()
    emit_sends(psi_ref, metric_ref, packed_metric, groups, (x0, x1, y0, y1, zz))


def inner_body(psi_ref, metric_ref, z_ref):
    lane, row = iota((NY, NZ), 1), iota((NY, NZ), 0)
    for x in range(NX):
        s = slab(x)
        ms = []
        for o, keep in (
            (4, row < NY - 1), (5, row >= 1), (6, row < NY - 2), (7, row >= 2),
            (8, lane < NZ - 1), (9, lane >= 1), (10, lane < NZ - 2), (11, lane >= 2),
        ):
            ms.append(jnp.where(keep, metric_ref[o, s, :], 0.0))
        for e in range(FIELDS):
            q = psi_ref[e, s, :]
            total = row_roll(ms[0] * q, 1) + row_roll(ms[1] * q, -1)
            total = total + (row_roll(ms[2] * q, 2) + row_roll(ms[3] * q, -2))
            total = total + (lane_roll(ms[4] * q, 1) + lane_roll(ms[5] * q, -1))
            total = total + (lane_roll(ms[6] * q, 2) + lane_roll(ms[7] * q, -2))
            for o, step in enumerate((1, -1, 2, -2)):
                if 0 <= x - step < NX:
                    total = total + metric_ref[o, slab(x - step), :] * psi_ref[e, slab(x - step), :]
            z_ref[e, s, :] = total


def from_sides(axis, first, second):
    index = lax.axis_index(axis)
    even = index % 2 == 0
    below = jnp.where(even, second, first)
    above = jnp.where(even, first, second)
    return jnp.where(index > 0, below, 0.0), jnp.where(index < lax.axis_size(axis) - 1, above, 0.0)


def update(psi_ref, z_ref, received, diag_ref, rhs_ref, jac_ref, new_ref, total_ref):
    x0, x1, y0, y1, z0, z1 = received
    lane8 = iota((8, NZ), 1)
    edge = (lane8 < 2) | (lane8 >= NZ - 2)
    for g in range((FIELDS + 1) // 2):
        rows = slice(8 * g, 8 * g + 8)
        below, above = from_sides("wa", z0[rows, :], z1[rows, :])
        both = jnp.where(lane8 % 4 >= 2, below, above)
        for e in range(2 * g, min(2 * g + 2, FIELDS)):
            for x in range(NX):
                for t in range(2):
                    shift = -(2 + 64 * (e % 2) + 4 * (2 * x + t))
                    total_ref[e, tile_rows(x, t), :] = z_ref[e, tile_rows(x, t), :] + jnp.where(edge, lane_roll(both, shift), 0.0)
    for e in range(FIELDS):
        for r in range(2):
            below, above = from_sides("gx", x0[e, r], x1[e, r])
            total_ref[e, slab(r), :] += below
            total_ref[e, slab(NX - 2 + r), :] += above
        for r in range(2):
            below, above = from_sides("gy", y0[e, r], y1[e, r])
            total_ref[e, edge_rows(r), :] += below
            total_ref[e, edge_rows(NY - 2 + r), :] += above
    for x in range(NX):
        s = slab(x)
        d = diag_ref[s, :]
        scale = OMEGA / d
        zs = [total_ref[e, s, :] for e in range(FIELDS)]
        for f in range(FIELDS):
            c = jac_ref[f, s, :].astype(F32) * zs[0]
            for e in range(1, FIELDS):
                c = c + jac_ref[FIELDS * e + f, s, :].astype(F32) * zs[e]
            q = psi_ref[f, s, :]
            new_ref[f, s, :] = q + (rhs_ref[f, s, :] - d * q + c) * scale


def middle_body(psi_ref, z_ref, r0, r1, r2, r3, r4, r5, diag_ref, rhs_ref, jac_ref, metric_ref, packed_metric,
                new_ref, x0, x1, y0, y1, zz, total_ref):
    update(psi_ref, z_ref, (r0, r1, r2, r3, r4, r5), diag_ref, rhs_ref, jac_ref, new_ref, total_ref)
    emit_sends(new_ref, metric_ref, packed_metric, pack_edges(new_ref), (x0, x1, y0, y1, zz))


def wall_body(coef_ref, ids_ref, weight_ref, coef_out, weight_out, hot_out, low_out):
    def spread(rows, place):
        at = lax.broadcasted_iota(jnp.int32, (rows, 2 * NZ), 1)
        r = lax.broadcasted_iota(jnp.int32, (rows, 2 * NZ), 0)
        return (at % NZ == place(r) + 4 * (at // NZ)).astype(F32)

    def packed(table, chooser):
        v = lax.dot_general(table, chooser, (((0,), (0,)), ((), ())), precision=lax.Precision.HIGHEST,
                            preferred_element_type=F32)
        return v[:8, :NZ] + v[8:, NZ:]

    chooser = spread(4 * NX, lambda r: 64 * (r // 16) + 8 * (r % NX) + 2 + (r // NX) % 2)
    for c in range(3):
        for g in range((FIELDS + 1) // 2):
            count = 4 * NX if g < FIELDS // 2 else 2 * NX
            start = c * 10 * NX + g * 4 * NX
            coef_out[c, 8 * g : 8 * g + 8, :] = packed(coef_ref[start : start + count, :], chooser[:count])
    chooser = spread(4 * NX, lambda r: 8 * (r % NX) + r // NX)
    lane, row = iota((8, NZ), 1), iota((8, NZ), 0)

    def halves(v):
        return jnp.where(lane < 64, v, lane_roll(row_roll(v, 4), 64))

    on = jnp.where(lax.axis_index("wa") == 0, 1.0, 0.0)
    weight_out[...] = halves(packed(weight_ref[...], chooser)) * on
    ids = halves(packed(ids_ref[...].astype(F32), chooser)).astype(jnp.int32)
    low_out[...] = ids % 16
    owner = ids // 16
    slot = iota((256, NZ), 0)
    for s in range(4):
        hit = slot == jnp.broadcast_to(owner[s : s + 1, :], (256, NZ))
        hot_out[:, NZ * s : NZ * s + NZ] = jnp.where(hit, 1.0, 0.0).astype(jnp.bfloat16)


def last_body(psi_ref, z_ref, r0, r1, r2, r3, r4, r5, diag_ref, rhs_ref, jac_ref, coef_ref, weight_ref, hot_ref, low_ref,
              out_hbm, slots_ref, new_ref, total_ref, high_part, low_part, sem):
    update(psi_ref, z_ref, (r0, r1, r2, r3, r4, r5), diag_ref, rhs_ref, jac_ref, new_ref, total_ref)
    copy = pltpu.make_async_copy(new_ref, out_hbm, sem)
    copy.start()
    lane = iota((8, NZ), 1)
    groups = pack_edges(new_ref)
    low = low_ref[...]
    point = iota((16, NZ), 0)
    for c in range(3):
        v = coef_ref[c, 0:8, :] * groups[0]
        for g in range(1, len(groups)):
            v = v + coef_ref[c, 8 * g : 8 * g + 8, :] * groups[g]
        v = v + lane_roll(v, 64)
        v = jnp.where(lane % 4 == 3, v + lane_roll(v, 1), 0.0)
        v = v + lane_roll(v, -1)
        v = v + lane_roll(v, -2)
        v = jnp.where(lane < 64, v, row_roll(v, 4)) * weight_ref[...]
        for s in range(4):
            here = point == jnp.broadcast_to(low[s : s + 1, :], (16, NZ))
            w = jnp.where(here, jnp.broadcast_to(v[s : s + 1, :], (16, NZ)), 0.0)
            top = w.astype(jnp.bfloat16)
            at = (slice(16 * c, 16 * c + 16), slice(NZ * s, NZ * s + NZ))
            high_part[at] = top
            low_part[at] = (w - top.astype(F32)).astype(jnp.bfloat16)
    hot = hot_ref[...]
    dims = (((1,), (1,)), ((), ()))
    slots_ref[...] = lax.dot_general(hot, high_part[...], dims, preferred_element_type=F32) + lax.dot_general(
        hot, low_part[...], dims, preferred_element_type=F32
    )
    copy.wait()


def sum_body(got_ref, out_ref):
    v = got_ref[...].sum(axis=0, keepdims=True)
    for c in range(3):
        out_ref[c : c + 1, :] = v[:, 16 * c : 16 * c + 16]


def run(body, args, outs, scratch=(), sems=(), far=(), far_outs=()):
    hbm = pl.BlockSpec(memory_space=pltpu.HBM)
    args = [pltpu.with_memory_space_constraint(v, pltpu.HBM) if i in far else v for i, v in enumerate(args)]
    return pl.pallas_call(
        body,
        out_shape=[jax.ShapeDtypeStruct(s, d) for s, d in outs],
        in_specs=[hbm if i in far else VMEM for i in range(len(args))],
        out_specs=[hbm if i in far_outs else VMEM for i in range(len(outs))],
        scratch_shapes=[pltpu.VMEM(s, d) for s, d in scratch] + [pltpu.SemaphoreType.DMA(s) for s in sems],
        compiler_params=pltpu.CompilerParams(vmem_limit_bytes=24 << 20),
        cost_estimate=pl.CostEstimate(flops=1000000, bytes_accessed=1000000, transcendentals=0),
    )(*args)


EDGE_X = ((FIELDS, 2, NY, NZ), F32)
EDGE_Y = ((FIELDS, 2, NX, NZ), F32)
EDGE_Z = ((24, NZ), F32)
SENDS = [EDGE_X, EDGE_X, EDGE_Y, EDGE_Y, EDGE_Z]
FIELD = ((FIELDS, ROWS, NZ), F32)


def exchange(sends):
    x0, x1, y0, y1, zz = sends
    def swap(v, axis, odd):
        return lax.ppermute(v, axis, pairs(lax.axis_size(axis), odd))
    x = swap(x0, "gx", 0), swap(x1, "gx", 1)
    y = swap(y0, "gy", 0), swap(y1, "gy", 1)
    far = swap(zz, "wa", 1)
    zz, first = lax.optimization_barrier((zz, x[0]))
    x = first, x[1]
    z = swap(zz, "wa", 0), far
    return (*x, *y, *z)


def local(adjoint_init, objective_grad, diag_term, face_metric, flux_jacobian, wall_coef, ffd_ids, ffd_weight):
    psi = adjoint_init.reshape(FIELDS, ROWS, NZ)
    rhs = objective_grad.reshape(FIELDS, ROWS, NZ)
    diag = diag_term.reshape(ROWS, NZ)
    metric = face_metric.reshape(12, ROWS, NZ)
    jac = flux_jacobian.reshape(FIELDS * FIELDS, ROWS, NZ)
    *sends, packed_metric, psi, metric = run(
        first_body, (psi, metric), SENDS + [((24, NZ), F32), FIELD, ((12, ROWS, NZ), F32)], sems=[(4,)], far=(0, 1)
    )
    wall = run(
        wall_body,
        (wall_coef.reshape(30 * NX, NY), ffd_ids.reshape(4 * NX, NY), ffd_weight.reshape(4 * NX, NY)),
        [((3, 24, NZ), F32), ((8, NZ), F32), ((256, 512), jnp.bfloat16), ((8, NZ), jnp.int32)],
    )
    for step in range(SWEEPS):
        received = exchange(sends)
        (z,) = run(inner_body, (psi, metric), [FIELD])
        if step == 0:
            z, wall = lax.optimization_barrier((z, wall))
        if step < SWEEPS - 1:
            psi, *sends = run(
                middle_body, (psi, z, *received, diag, rhs, jac, metric, packed_metric), [FIELD] + SENDS, scratch=[FIELD]
            )
        else:
            psi, slots = run(
                last_body, (psi, z, *received, diag, rhs, jac, *wall), [FIELD, ((256, 48), F32)],
                scratch=[FIELD, FIELD, ((48, 512), jnp.bfloat16), ((48, 512), jnp.bfloat16)], sems=[()], far_outs=(0,),
            )
    got = lax.all_to_all(slots.reshape(256, 1, 48), AXES, 0, 0).reshape(256, 48)
    (grad,) = run(sum_body, (got,), [((3, 16), F32)])
    return psi.reshape(adjoint_init.shape), grad


def solution(mesh):
    in_specs = (
        P(None, "gx", "gy", "wa"),
        P(None, "gx", "gy", "wa"),
        P("gx", "gy", "wa"),
        P(None, "gx", "gy", "wa"),
        P(None, None, "gx", "gy", "wa"),
        P(None, None, "gx", "gy"),
        P(None, "gx", "gy"),
        P(None, "gx", "gy"),
    )
    out_specs = (P(None, "gx", "gy", "wa"), P(None, AXES))
    return jax.shard_map(local, mesh=mesh, in_specs=in_specs, out_specs=out_specs, check_vma=False)
```

```python
import jax
import jax.numpy as jnp
from jax import lax
from jax.experimental import pallas as pl
from jax.experimental.pallas import tpu as pltpu
from jax.sharding import PartitionSpec as P

SWEEPS = 4
OMEGA = 0.6
AXES = ("gx", "gy", "wa")
FIELDS, NX, NY, NZ = 5, 8, 16, 128
ROWS = NX * NY
SLOTS, SLOT = 128, 32
F32 = jnp.float32
VMEM = pl.BlockSpec(memory_space=pltpu.VMEM)


def pairs(count, odd):
    table = {}
    for i in range(0, count, 2):
        a, b = (i + odd) % count, (i + 1 + odd) % count
        table[a], table[b] = b, a
    return sorted(table.items())


def iota(shape, dim):
    return lax.broadcasted_iota(jnp.int32, shape, dim)


def lane_roll(v, shift):
    return pltpu.roll(v, shift % NZ, axis=1) if shift % NZ else v


def row_roll(v, shift):
    return pltpu.roll(v, shift % v.shape[0], axis=0)


def is_even(axis):
    return lax.axis_index(axis) % 2 == 0


def slab(x):
    return slice(NY * x, NY * (x + 1))


def edge_rows(y):
    return pl.ds(y, NX, stride=NY)


def tile_rows(x, t):
    return slice(NY * x + 8 * t, NY * x + 8 * t + 8)


def pack_edges(psi_ref):
    lane = iota((8, NZ), 1)
    edge = (lane < 2) | (lane >= NZ - 2)
    groups = []
    for g in range((FIELDS + 1) // 2):
        total = jnp.zeros((8, NZ), F32)
        for e in range(2 * g, min(2 * g + 2, FIELDS)):
            for x in range(NX):
                for t in range(2):
                    v = jnp.where(edge, psi_ref[e, tile_rows(x, t), :], 0.0)
                    total = total + lane_roll(v, 2 + 64 * (e % 2) + 4 * (2 * x + t))
        groups.append(total)
    return groups


def pack_metric(metric_ref, out_ref):
    lane = iota((8, NZ), 1)
    same = jnp.zeros((8, NZ), F32)
    after = jnp.zeros((8, NZ), F32)
    before = jnp.zeros((8, NZ), F32)
    for x in range(NX):
        for t in range(2):
            j, rows = 4 * (2 * x + t), tile_rows(x, t)
            v = jnp.where(lane >= NZ - 2, metric_ref[10, rows, :], jnp.where(lane < 2, metric_ref[11, rows, :], 0.0))
            same = same + lane_roll(v, 2 + j)
            after = after + lane_roll(jnp.where(lane == NZ - 1, metric_ref[8, rows, :], 0.0), 1 + j)
            before = before + lane_roll(jnp.where(lane == 0, metric_ref[9, rows, :], 0.0), 3 + j)
    for i, v in enumerate((same, after, before)):
        out_ref[8 * i : 8 * i + 8, :] = v + lane_roll(v, 64)


def emit_sends(psi_ref, metric_ref, packed_metric, groups, sends):
    x0, x1, y0, y1, zz = sends
    lane = iota((8, NZ), 1)
    same, after, before = (packed_metric[8 * i : 8 * i + 8, :] for i in range(3))
    for g, p in enumerate(groups):
        v = same * p + after * lane_roll(p, -1) + before * lane_roll(p, 1)
        zz[8 * g : 8 * g + 8, :] = jnp.where(lane % 4 < 2, lane_roll(v, -2), lane_roll(v, 2))
    even = is_even("gy")
    m4, m6a, m6b = metric_ref[4, edge_rows(15), :], metric_ref[6, edge_rows(14), :], metric_ref[6, edge_rows(15), :]
    m5, m7a, m7b = metric_ref[5, edge_rows(0), :], metric_ref[7, edge_rows(0), :], metric_ref[7, edge_rows(1), :]
    for e in range(FIELDS):
        q14, q15 = psi_ref[e, edge_rows(14), :], psi_ref[e, edge_rows(15), :]
        q0, q1 = psi_ref[e, edge_rows(0), :], psi_ref[e, edge_rows(1), :]
        high = (m4 * q15 + m6a * q14, m6b * q15)
        low = (m7a * q0, m5 * q0 + m7b * q1)
        for r in range(2):
            y0[e, r] = jnp.where(even, high[r], low[r])
            y1[e, r] = jnp.where(even, low[r], high[r])
    even = is_even("gx")
    last, near = slab(NX - 1), slab(NX - 2)
    m0, m2a, m2b = metric_ref[0, last, :], metric_ref[2, near, :], metric_ref[2, last, :]
    m1, m3a, m3b = metric_ref[1, slab(0), :], metric_ref[3, slab(0), :], metric_ref[3, slab(1), :]
    for e in range(FIELDS):
        q6, q7, q0, q1 = psi_ref[e, near, :], psi_ref[e, last, :], psi_ref[e, slab(0), :], psi_ref[e, slab(1), :]
        high = (m0 * q7 + m2a * q6, m2b * q7)
        low = (m3a * q0, m1 * q0 + m3b * q1)
        for r in range(2):
            x0[e, r] = jnp.where(even, high[r], low[r])
            x1[e, r] = jnp.where(even, low[r], high[r])


def first_body(psi_hbm, metric_hbm, x0, x1, y0, y1, zz, packed_metric, psi_ref, metric_ref, sems):
    copies = [
        pltpu.make_async_copy(metric_hbm.at[8:12], metric_ref.at[8:12], sems.at[0]),
        pltpu.make_async_copy(psi_hbm, psi_ref, sems.at[1]),
        pltpu.make_async_copy(metric_hbm.at[4:8], metric_ref.at[4:8], sems.at[2]),
        pltpu.make_async_copy(metric_hbm.at[0:4], metric_ref.at[0:4], sems.at[3]),
    ]
    for copy in copies:
        copy.start()
    copies[0].wait()
    pack_metric(metric_ref, packed_metric)
    copies[1].wait()
    groups = pack_edges(psi_ref)
    copies[2].wait()
    copies[3].wait()
    emit_sends(psi_ref, metric_ref, packed_metric, groups, (x0, x1, y0, y1, zz))


def inner_body(psi_ref, metric_ref, z_ref):
    lane, row = iota((NY, NZ), 1), iota((NY, NZ), 0)
    for x in range(NX):
        s = slab(x)
        ms = []
        for o, keep in (
            (4, row < NY - 1), (5, row >= 1), (6, row < NY - 2), (7, row >= 2),
            (8, lane < NZ - 1), (9, lane >= 1), (10, lane < NZ - 2), (11, lane >= 2),
        ):
            ms.append(jnp.where(keep, metric_ref[o, s, :], 0.0))
        for e in range(FIELDS):
            q = psi_ref[e, s, :]
            total = row_roll(ms[0] * q, 1) + row_roll(ms[1] * q, -1)
            total = total + (row_roll(ms[2] * q, 2) + row_roll(ms[3] * q, -2))
            total = total + (lane_roll(ms[4] * q, 1) + lane_roll(ms[5] * q, -1))
            total = total + (lane_roll(ms[6] * q, 2) + lane_roll(ms[7] * q, -2))
            for o, step in enumerate((1, -1, 2, -2)):
                if 0 <= x - step < NX:
                    total = total + metric_ref[o, slab(x - step), :] * psi_ref[e, slab(x - step), :]
            z_ref[e, s, :] = total


def from_sides(axis, first, second):
    index = lax.axis_index(axis)
    even = index % 2 == 0
    below = jnp.where(even, second, first)
    above = jnp.where(even, first, second)
    return jnp.where(index > 0, below, 0.0), jnp.where(index < lax.axis_size(axis) - 1, above, 0.0)


def update(psi_ref, z_ref, received, diag_ref, rhs_ref, jac_ref, new_ref, total_ref):
    x0, x1, y0, y1, z0, z1 = received
    lane8 = iota((8, NZ), 1)
    edge = (lane8 < 2) | (lane8 >= NZ - 2)
    for g in range((FIELDS + 1) // 2):
        rows = slice(8 * g, 8 * g + 8)
        below, above = from_sides("wa", z0[rows, :], z1[rows, :])
        both = jnp.where(lane8 % 4 >= 2, below, above)
        for e in range(2 * g, min(2 * g + 2, FIELDS)):
            for x in range(NX):
                for t in range(2):
                    shift = -(2 + 64 * (e % 2) + 4 * (2 * x + t))
                    total_ref[e, tile_rows(x, t), :] = z_ref[e, tile_rows(x, t), :] + jnp.where(edge, lane_roll(both, shift), 0.0)
    for e in range(FIELDS):
        for r in range(2):
            below, above = from_sides("gx", x0[e, r], x1[e, r])
            total_ref[e, slab(r), :] += below
            total_ref[e, slab(NX - 2 + r), :] += above
        for r in range(2):
            below, above = from_sides("gy", y0[e, r], y1[e, r])
            total_ref[e, edge_rows(r), :] += below
            total_ref[e, edge_rows(NY - 2 + r), :] += above
    for x in range(NX):
        s = slab(x)
        d = diag_ref[s, :]
        scale = OMEGA / d
        zs = [total_ref[e, s, :] for e in range(FIELDS)]
        for f in range(FIELDS):
            c = jac_ref[f, s, :].astype(F32) * zs[0]
            for e in range(1, FIELDS):
                c = c + jac_ref[FIELDS * e + f, s, :].astype(F32) * zs[e]
            q = psi_ref[f, s, :]
            new_ref[f, s, :] = q + (rhs_ref[f, s, :] - d * q + c) * scale


def middle_body(psi_ref, z_ref, r0, r1, r2, r3, r4, r5, diag_ref, rhs_ref, jac_ref, metric_ref, packed_metric,
                new_ref, x0, x1, y0, y1, zz, total_ref):
    update(psi_ref, z_ref, (r0, r1, r2, r3, r4, r5), diag_ref, rhs_ref, jac_ref, new_ref, total_ref)
    emit_sends(new_ref, metric_ref, packed_metric, pack_edges(new_ref), (x0, x1, y0, y1, zz))


def wall_body(coef_ref, ids_ref, weight_ref, coef_out, weight_out, hot_out, low_out):
    def spread(rows, place):
        at = lax.broadcasted_iota(jnp.int32, (rows, 2 * NZ), 1)
        r = lax.broadcasted_iota(jnp.int32, (rows, 2 * NZ), 0)
        return (at % NZ == place(r) + 4 * (at // NZ)).astype(F32)

    def packed(table, chooser):
        v = lax.dot_general(table, chooser, (((0,), (0,)), ((), ())), precision=lax.Precision.HIGHEST,
                            preferred_element_type=F32)
        return v[:8, :NZ] + v[8:, NZ:]

    chooser = spread(4 * NX, lambda r: 64 * (r // 16) + 8 * (r % NX) + 2 + (r // NX) % 2)
    for c in range(3):
        for g in range((FIELDS + 1) // 2):
            count = 4 * NX if g < FIELDS // 2 else 2 * NX
            start = c * 10 * NX + g * 4 * NX
            coef_out[c, 8 * g : 8 * g + 8, :] = packed(coef_ref[start : start + count, :], chooser[:count])
    chooser = spread(4 * NX, lambda r: 8 * (r % NX) + r // NX)
    lane, row = iota((8, NZ), 1), iota((8, NZ), 0)

    def halves(v):
        return jnp.where(lane < 64, v, lane_roll(row_roll(v, 4), 64))

    on = jnp.where(lax.axis_index("wa") == 0, 1.0, 0.0)
    weight_out[...] = halves(packed(weight_ref[...], chooser)) * on
    ids = halves(packed(ids_ref[...].astype(F32), chooser)).astype(jnp.int32)
    low_out[...] = ids % SLOT
    owner = ids // SLOT
    slot = iota((SLOTS, NZ), 0)
    for s in range(4):
        hit = slot == jnp.broadcast_to(owner[s : s + 1, :], (SLOTS, NZ))
        hot_out[:, NZ * s : NZ * s + NZ] = jnp.where(hit, 1.0, 0.0).astype(jnp.bfloat16)


def last_body(psi_ref, z_ref, r0, r1, r2, r3, r4, r5, diag_ref, rhs_ref, jac_ref, coef_ref, weight_ref, hot_ref, low_ref,
              out_hbm, slots_ref, new_ref, total_ref, high_part, low_part, sem):
    update(psi_ref, z_ref, (r0, r1, r2, r3, r4, r5), diag_ref, rhs_ref, jac_ref, new_ref, total_ref)
    copy = pltpu.make_async_copy(new_ref, out_hbm, sem)
    copy.start()
    lane = iota((8, NZ), 1)
    groups = pack_edges(new_ref)
    low = low_ref[...]
    point = iota((SLOT, NZ), 0)
    for c in range(3):
        v = coef_ref[c, 0:8, :] * groups[0]
        for g in range(1, len(groups)):
            v = v + coef_ref[c, 8 * g : 8 * g + 8, :] * groups[g]
        v = v + lane_roll(v, 64)
        v = jnp.where(lane % 4 == 3, v + lane_roll(v, 1), 0.0)
        v = v + lane_roll(v, -1)
        v = v + lane_roll(v, -2)
        v = jnp.where(lane < 64, v, row_roll(v, 4)) * weight_ref[...]
        for s in range(4):
            here = point == jnp.broadcast_to(low[s : s + 1, :], (SLOT, NZ))
            w = jnp.where(here, jnp.broadcast_to(v[s : s + 1, :], (SLOT, NZ)), 0.0)
            top = w.astype(jnp.bfloat16)
            at = (slice(SLOT * c, SLOT * c + SLOT), slice(NZ * s, NZ * s + NZ))
            high_part[at] = top
            low_part[at] = (w - top.astype(F32)).astype(jnp.bfloat16)
    hot = hot_ref[...]
    dims = (((1,), (1,)), ((), ()))
    slots_ref[...] = lax.dot_general(hot, high_part[...], dims, preferred_element_type=F32) + lax.dot_general(
        hot, low_part[...], dims, preferred_element_type=F32
    )
    copy.wait()


def sum_body(got_ref, out_ref):
    out_ref[...] = jnp.broadcast_to(got_ref[...].sum(axis=0, keepdims=True), out_ref.shape)


def pick_body(own_ref, other_ref, out_ref):
    own, other = own_ref[0:1, :], other_ref[0:1, :]
    even = is_even("wa")
    for c in range(3):
        at = SLOT * c
        out_ref[c : c + 1, :] = jnp.where(even, own[:, at : at + SLOT // 2], other[:, at + SLOT // 2 : at + SLOT])


def run(body, args, outs, scratch=(), sems=(), far=(), far_outs=()):
    hbm = pl.BlockSpec(memory_space=pltpu.HBM)
    args = [pltpu.with_memory_space_constraint(v, pltpu.HBM) if i in far else v for i, v in enumerate(args)]
    return pl.pallas_call(
        body,
        out_shape=[jax.ShapeDtypeStruct(s, d) for s, d in outs],
        in_specs=[hbm if i in far else VMEM for i in range(len(args))],
        out_specs=[hbm if i in far_outs else VMEM for i in range(len(outs))],
        scratch_shapes=[pltpu.VMEM(s, d) for s, d in scratch] + [pltpu.SemaphoreType.DMA(s) for s in sems],
        compiler_params=pltpu.CompilerParams(vmem_limit_bytes=24 << 20),
        cost_estimate=pl.CostEstimate(flops=1000000, bytes_accessed=1000000, transcendentals=0),
    )(*args)


EDGE_X = ((FIELDS, 2, NY, NZ), F32)
EDGE_Y = ((FIELDS, 2, NX, NZ), F32)
EDGE_Z = ((24, NZ), F32)
SENDS = [EDGE_X, EDGE_X, EDGE_Y, EDGE_Y, EDGE_Z]
FIELD = ((FIELDS, ROWS, NZ), F32)


def exchange(sends):
    x0, x1, y0, y1, zz = sends
    def swap(v, axis, odd):
        return lax.ppermute(v, axis, pairs(lax.axis_size(axis), odd))
    x = swap(x0, "gx", 0), swap(x1, "gx", 1)
    y = swap(y0, "gy", 0), swap(y1, "gy", 1)
    far = swap(zz, "wa", 1)
    zz, first = lax.optimization_barrier((zz, x[0]))
    x = first, x[1]
    z = swap(zz, "wa", 0), far
    return (*x, *y, *z)


def local(adjoint_init, objective_grad, diag_term, face_metric, flux_jacobian, wall_coef, ffd_ids, ffd_weight):
    psi = adjoint_init.reshape(FIELDS, ROWS, NZ)
    rhs = objective_grad.reshape(FIELDS, ROWS, NZ)
    diag = diag_term.reshape(ROWS, NZ)
    metric = face_metric.reshape(12, ROWS, NZ)
    jac = flux_jacobian.reshape(FIELDS * FIELDS, ROWS, NZ)
    *sends, packed_metric, psi, metric = run(
        first_body, (psi, metric), SENDS + [((24, NZ), F32), FIELD, ((12, ROWS, NZ), F32)], sems=[(4,)], far=(0, 1)
    )
    wall = run(
        wall_body,
        (wall_coef.reshape(30 * NX, NY), ffd_ids.reshape(4 * NX, NY), ffd_weight.reshape(4 * NX, NY)),
        [((3, 24, NZ), F32), ((8, NZ), F32), ((SLOTS, 512), jnp.bfloat16), ((8, NZ), jnp.int32)],
    )
    for step in range(SWEEPS):
        received = exchange(sends)
        (z,) = run(inner_body, (psi, metric), [FIELD])
        if step == 0:
            z, wall = lax.optimization_barrier((z, wall))
        if step < SWEEPS - 1:
            psi, *sends = run(
                middle_body, (psi, z, *received, diag, rhs, jac, metric, packed_metric), [FIELD] + SENDS, scratch=[FIELD]
            )
        else:
            psi, slots = run(
                last_body, (psi, z, *received, diag, rhs, jac, *wall), [FIELD, ((SLOTS, 3 * SLOT), F32)],
                scratch=[FIELD, FIELD, ((3 * SLOT, 512), jnp.bfloat16), ((3 * SLOT, 512), jnp.bfloat16)], sems=[()], far_outs=(0,),
            )
    columns = lax.axis_size("gx") * lax.axis_size("gy")
    groups = [[4 * i + w for i in range(columns) for w in (core, core + 2)] for core in range(2)]
    got = lax.all_to_all(slots.reshape(SLOTS, 1, 3 * SLOT), AXES, 0, 0, axis_index_groups=groups).reshape(SLOTS, 3 * SLOT)
    (own,) = run(sum_body, (got,), [((8, 3 * SLOT), F32)])
    other = lax.ppermute(own, "wa", pairs(lax.axis_size("wa"), 0))
    (grad,) = run(pick_body, (own, other), [((3, 16), F32)])
    return psi.reshape(adjoint_init.shape), grad


def solution(mesh):
    in_specs = (
        P(None, "gx", "gy", "wa"),
        P(None, "gx", "gy", "wa"),
        P("gx", "gy", "wa"),
        P(None, "gx", "gy", "wa"),
        P(None, None, "gx", "gy", "wa"),
        P(None, None, "gx", "gy"),
        P(None, "gx", "gy"),
        P(None, "gx", "gy"),
    )
    out_specs = (P(None, "gx", "gy", "wa"), P(None, AXES))
    return jax.shard_map(local, mesh=mesh, in_specs=in_specs, out_specs=out_specs, check_vma=False)
```

```python
import jax
import jax.numpy as jnp
from jax import lax
from jax.experimental import pallas as pl
from jax.experimental.pallas import tpu as pltpu
from jax.sharding import PartitionSpec as P

SWEEPS = 4
OMEGA = 0.6
AXES = ("gx", "gy", "wa")
FIELDS, NX, NY, NZ = 5, 8, 16, 128
ROWS = NX * NY
F32 = jnp.float32
VMEM = pl.BlockSpec(memory_space=pltpu.VMEM)


def pairs(count, odd):
    table = {i: i for i in range(count)}
    for i in range(odd, count - 1, 2):
        table[i], table[i + 1] = i + 1, i
    return sorted(table.items())


def iota(shape, dim):
    return lax.broadcasted_iota(jnp.int32, shape, dim)


def lane_roll(v, shift):
    return pltpu.roll(v, shift % NZ, axis=1) if shift % NZ else v


def row_roll(v, shift):
    return pltpu.roll(v, shift % v.shape[0], axis=0)


def is_even(axis):
    return lax.axis_index(axis) % 2 == 0


def slab(x):
    return slice(NY * x, NY * (x + 1))


def edge_rows(y):
    return pl.ds(y, NX, stride=NY)


def tile_rows(x, t):
    return slice(NY * x + 8 * t, NY * x + 8 * t + 8)


def pack_edges(psi_ref):
    lane = iota((8, NZ), 1)
    edge = (lane < 2) | (lane >= NZ - 2)
    groups = []
    for g in range((FIELDS + 1) // 2):
        total = jnp.zeros((8, NZ), F32)
        for e in range(2 * g, min(2 * g + 2, FIELDS)):
            for x in range(NX):
                for t in range(2):
                    v = jnp.where(edge, psi_ref[e, tile_rows(x, t), :], 0.0)
                    total = total + lane_roll(v, 2 + 64 * (e % 2) + 4 * (2 * x + t))
        groups.append(total)
    return groups


def pack_metric(metric_ref, out_ref):
    lane = iota((8, NZ), 1)
    same = jnp.zeros((8, NZ), F32)
    after = jnp.zeros((8, NZ), F32)
    before = jnp.zeros((8, NZ), F32)
    for x in range(NX):
        for t in range(2):
            j, rows = 4 * (2 * x + t), tile_rows(x, t)
            v = jnp.where(lane >= NZ - 2, metric_ref[10, rows, :], jnp.where(lane < 2, metric_ref[11, rows, :], 0.0))
            same = same + lane_roll(v, 2 + j)
            after = after + lane_roll(jnp.where(lane == NZ - 1, metric_ref[8, rows, :], 0.0), 1 + j)
            before = before + lane_roll(jnp.where(lane == 0, metric_ref[9, rows, :], 0.0), 3 + j)
    for i, v in enumerate((same, after, before)):
        out_ref[8 * i : 8 * i + 8, :] = v + lane_roll(v, 64)


def emit_sends(psi_ref, metric_ref, packed_metric, groups, sends):
    x0, x1, y0, y1, zz = sends
    lane = iota((8, NZ), 1)
    same, after, before = (packed_metric[8 * i : 8 * i + 8, :] for i in range(3))
    for g, p in enumerate(groups):
        v = same * p + after * lane_roll(p, -1) + before * lane_roll(p, 1)
        zz[8 * g : 8 * g + 8, :] = jnp.where(lane % 4 < 2, lane_roll(v, -2), lane_roll(v, 2))
    even = is_even("gy")
    m4, m6a, m6b = metric_ref[4, edge_rows(15), :], metric_ref[6, edge_rows(14), :], metric_ref[6, edge_rows(15), :]
    m5, m7a, m7b = metric_ref[5, edge_rows(0), :], metric_ref[7, edge_rows(0), :], metric_ref[7, edge_rows(1), :]
    for e in range(FIELDS):
        q14, q15 = psi_ref[e, edge_rows(14), :], psi_ref[e, edge_rows(15), :]
        q0, q1 = psi_ref[e, edge_rows(0), :], psi_ref[e, edge_rows(1), :]
        high = (m4 * q15 + m6a * q14, m6b * q15)
        low = (m7a * q0, m5 * q0 + m7b * q1)
        for r in range(2):
            y0[e, r] = jnp.where(even, high[r], low[r])
            y1[e, r] = jnp.where(even, low[r], high[r])
    even = is_even("gx")
    last, near = slab(NX - 1), slab(NX - 2)
    m0, m2a, m2b = metric_ref[0, last, :], metric_ref[2, near, :], metric_ref[2, last, :]
    m1, m3a, m3b = metric_ref[1, slab(0), :], metric_ref[3, slab(0), :], metric_ref[3, slab(1), :]
    for e in range(FIELDS):
        q6, q7, q0, q1 = psi_ref[e, near, :], psi_ref[e, last, :], psi_ref[e, slab(0), :], psi_ref[e, slab(1), :]
        high = (m0 * q7 + m2a * q6, m2b * q7)
        low = (m3a * q0, m1 * q0 + m3b * q1)
        for r in range(2):
            x0[e, r] = jnp.where(even, high[r], low[r])
            x1[e, r] = jnp.where(even, low[r], high[r])


def first_body(psi_hbm, metric_hbm, x0, x1, y0, y1, zz, packed_metric, psi_ref, metric_ref, sems):
    copies = [
        pltpu.make_async_copy(metric_hbm.at[8:12], metric_ref.at[8:12], sems.at[0]),
        pltpu.make_async_copy(psi_hbm, psi_ref, sems.at[1]),
        pltpu.make_async_copy(metric_hbm.at[4:8], metric_ref.at[4:8], sems.at[2]),
        pltpu.make_async_copy(metric_hbm.at[0:4], metric_ref.at[0:4], sems.at[3]),
    ]
    for copy in copies:
        copy.start()
    copies[0].wait()
    pack_metric(metric_ref, packed_metric)
    copies[1].wait()
    groups = pack_edges(psi_ref)
    copies[2].wait()
    copies[3].wait()
    emit_sends(psi_ref, metric_ref, packed_metric, groups, (x0, x1, y0, y1, zz))


def inner_body(psi_ref, metric_ref, z_ref):
    lane, row = iota((NY, NZ), 1), iota((NY, NZ), 0)
    for x in range(NX):
        s = slab(x)
        ms = []
        for o, keep in (
            (4, row < NY - 1), (5, row >= 1), (6, row < NY - 2), (7, row >= 2),
            (8, lane < NZ - 1), (9, lane >= 1), (10, lane < NZ - 2), (11, lane >= 2),
        ):
            ms.append(jnp.where(keep, metric_ref[o, s, :], 0.0))
        for e in range(FIELDS):
            q = psi_ref[e, s, :]
            total = row_roll(ms[0] * q, 1) + row_roll(ms[1] * q, -1)
            total = total + (row_roll(ms[2] * q, 2) + row_roll(ms[3] * q, -2))
            total = total + (lane_roll(ms[4] * q, 1) + lane_roll(ms[5] * q, -1))
            total = total + (lane_roll(ms[6] * q, 2) + lane_roll(ms[7] * q, -2))
            for o, step in enumerate((1, -1, 2, -2)):
                if 0 <= x - step < NX:
                    total = total + metric_ref[o, slab(x - step), :] * psi_ref[e, slab(x - step), :]
            z_ref[e, s, :] = total


def from_sides(axis, first, second):
    index = lax.axis_index(axis)
    even = index % 2 == 0
    below = jnp.where(even, second, first)
    above = jnp.where(even, first, second)
    return jnp.where(index > 0, below, 0.0), jnp.where(index < lax.axis_size(axis) - 1, above, 0.0)


def update(psi_ref, z_ref, received, diag_ref, rhs_ref, jac_ref, new_ref, total_ref):
    x0, x1, y0, y1, z0, z1 = received
    lane8 = iota((8, NZ), 1)
    edge = (lane8 < 2) | (lane8 >= NZ - 2)
    for g in range((FIELDS + 1) // 2):
        rows = slice(8 * g, 8 * g + 8)
        below, above = from_sides("wa", z0[rows, :], z1[rows, :])
        both = jnp.where(lane8 % 4 >= 2, below, above)
        for e in range(2 * g, min(2 * g + 2, FIELDS)):
            for x in range(NX):
                for t in range(2):
                    shift = -(2 + 64 * (e % 2) + 4 * (2 * x + t))
                    total_ref[e, tile_rows(x, t), :] = z_ref[e, tile_rows(x, t), :] + jnp.where(edge, lane_roll(both, shift), 0.0)
    for e in range(FIELDS):
        for r in range(2):
            below, above = from_sides("gx", x0[e, r], x1[e, r])
            total_ref[e, slab(r), :] += below
            total_ref[e, slab(NX - 2 + r), :] += above
        for r in range(2):
            below, above = from_sides("gy", y0[e, r], y1[e, r])
            total_ref[e, edge_rows(r), :] += below
            total_ref[e, edge_rows(NY - 2 + r), :] += above
    for x in range(NX):
        s = slab(x)
        d = diag_ref[s, :]
        scale = OMEGA / d
        zs = [total_ref[e, s, :] for e in range(FIELDS)]
        for f in range(FIELDS):
            c = jac_ref[f, s, :].astype(F32) * zs[0]
            for e in range(1, FIELDS):
                c = c + jac_ref[FIELDS * e + f, s, :].astype(F32) * zs[e]
            q = psi_ref[f, s, :]
            new_ref[f, s, :] = q + (rhs_ref[f, s, :] - d * q + c) * scale


def middle_body(psi_ref, z_ref, r0, r1, r2, r3, r4, r5, diag_ref, rhs_ref, jac_ref, metric_ref, packed_metric,
                new_ref, x0, x1, y0, y1, zz, total_ref):
    update(psi_ref, z_ref, (r0, r1, r2, r3, r4, r5), diag_ref, rhs_ref, jac_ref, new_ref, total_ref)
    emit_sends(new_ref, metric_ref, packed_metric, pack_edges(new_ref), (x0, x1, y0, y1, zz))


def wall_body(coef_ref, ids_ref, weight_ref, coef_out, weight_out, hot_out, low_out):
    def spread(rows, place):
        at = lax.broadcasted_iota(jnp.int32, (rows, 2 * NZ), 1)
        r = lax.broadcasted_iota(jnp.int32, (rows, 2 * NZ), 0)
        return (at % NZ == place(r) + 4 * (at // NZ)).astype(F32)

    def packed(table, chooser):
        v = lax.dot_general(table, chooser, (((0,), (0,)), ((), ())), precision=lax.Precision.HIGHEST,
                            preferred_element_type=F32)
        return v[:8, :NZ] + v[8:, NZ:]

    chooser = spread(4 * NX, lambda r: 64 * (r // 16) + 8 * (r % NX) + 2 + (r // NX) % 2)
    for c in range(3):
        for g in range((FIELDS + 1) // 2):
            count = 4 * NX if g < FIELDS // 2 else 2 * NX
            start = c * 10 * NX + g * 4 * NX
            coef_out[c, 8 * g : 8 * g + 8, :] = packed(coef_ref[start : start + count, :], chooser[:count])
    chooser = spread(4 * NX, lambda r: 8 * (r % NX) + r // NX)
    lane, row = iota((8, NZ), 1), iota((8, NZ), 0)

    def halves(v):
        return jnp.where(lane < 64, v, lane_roll(row_roll(v, 4), 64))

    on = jnp.where(lax.axis_index("wa") == 0, 1.0, 0.0)
    weight_out[...] = halves(packed(weight_ref[...], chooser)) * on
    ids = halves(packed(ids_ref[...].astype(F32), chooser)).astype(jnp.int32)
    low_out[...] = ids % 16
    owner = ids // 16
    slot = iota((256, NZ), 0)
    for s in range(4):
        hit = slot == jnp.broadcast_to(owner[s : s + 1, :], (256, NZ))
        hot_out[:, NZ * s : NZ * s + NZ] = jnp.where(hit, 1.0, 0.0).astype(jnp.bfloat16)


def last_body(psi_ref, z_ref, r0, r1, r2, r3, r4, r5, diag_ref, rhs_ref, jac_ref, coef_ref, weight_ref, hot_ref, low_ref,
              out_hbm, slots_ref, new_ref, total_ref, high_part, low_part, sem):
    update(psi_ref, z_ref, (r0, r1, r2, r3, r4, r5), diag_ref, rhs_ref, jac_ref, new_ref, total_ref)
    copy = pltpu.make_async_copy(new_ref, out_hbm, sem)
    copy.start()
    lane = iota((8, NZ), 1)
    groups = pack_edges(new_ref)
    low = low_ref[...]
    point = iota((16, NZ), 0)
    for c in range(3):
        v = coef_ref[c, 0:8, :] * groups[0]
        for g in range(1, len(groups)):
            v = v + coef_ref[c, 8 * g : 8 * g + 8, :] * groups[g]
        v = v + lane_roll(v, 64)
        v = jnp.where(lane % 4 == 3, v + lane_roll(v, 1), 0.0)
        v = v + lane_roll(v, -1)
        v = v + lane_roll(v, -2)
        v = jnp.where(lane < 64, v, row_roll(v, 4)) * weight_ref[...]
        for s in range(4):
            here = point == jnp.broadcast_to(low[s : s + 1, :], (16, NZ))
            w = jnp.where(here, jnp.broadcast_to(v[s : s + 1, :], (16, NZ)), 0.0)
            top = w.astype(jnp.bfloat16)
            at = (slice(16 * c, 16 * c + 16), slice(NZ * s, NZ * s + NZ))
            high_part[at] = top
            low_part[at] = (w - top.astype(F32)).astype(jnp.bfloat16)
    hot = hot_ref[...]
    dims = (((1,), (1,)), ((), ()))
    slots_ref[...] = lax.dot_general(hot, high_part[...], dims, preferred_element_type=F32) + lax.dot_general(
        hot, low_part[...], dims, preferred_element_type=F32
    )
    copy.wait()


def sum_body(got_ref, out_ref):
    v = got_ref[...].sum(axis=0, keepdims=True)
    for c in range(3):
        out_ref[c : c + 1, :] = v[:, 16 * c : 16 * c + 16]


def run(body, args, outs, scratch=(), sems=(), far=(), far_outs=()):
    hbm = pl.BlockSpec(memory_space=pltpu.HBM)
    args = [pltpu.with_memory_space_constraint(v, pltpu.HBM) if i in far else v for i, v in enumerate(args)]
    return pl.pallas_call(
        body,
        out_shape=[jax.ShapeDtypeStruct(s, d) for s, d in outs],
        in_specs=[hbm if i in far else VMEM for i in range(len(args))],
        out_specs=[hbm if i in far_outs else VMEM for i in range(len(outs))],
        scratch_shapes=[pltpu.VMEM(s, d) for s, d in scratch] + [pltpu.SemaphoreType.DMA(s) for s in sems],
        compiler_params=pltpu.CompilerParams(vmem_limit_bytes=24 << 20),
        cost_estimate=pl.CostEstimate(flops=1000000, bytes_accessed=1000000, transcendentals=0),
    )(*args)


EDGE_X = ((FIELDS, 2, NY, NZ), F32)
EDGE_Y = ((FIELDS, 2, NX, NZ), F32)
EDGE_Z = ((24, NZ), F32)
SENDS = [EDGE_X, EDGE_X, EDGE_Y, EDGE_Y, EDGE_Z]
FIELD = ((FIELDS, ROWS, NZ), F32)


def exchange(sends):
    x0, x1, y0, y1, zz = sends
    def swap(v, axis, odd):
        return lax.ppermute(v, axis, pairs(lax.axis_size(axis), odd))
    x = swap(x0, "gx", 0), swap(x1, "gx", 1)
    y = swap(y0, "gy", 0), swap(y1, "gy", 1)
    far = swap(zz, "wa", 1)
    zz, first = lax.optimization_barrier((zz, x[0]))
    x = first, x[1]
    z = swap(zz, "wa", 0), far
    return (*x, *y, *z)


def local(adjoint_init, objective_grad, diag_term, face_metric, flux_jacobian, wall_coef, ffd_ids, ffd_weight):
    psi = adjoint_init.reshape(FIELDS, ROWS, NZ)
    rhs = objective_grad.reshape(FIELDS, ROWS, NZ)
    diag = diag_term.reshape(ROWS, NZ)
    metric = face_metric.reshape(12, ROWS, NZ)
    jac = flux_jacobian.reshape(FIELDS * FIELDS, ROWS, NZ)
    *sends, packed_metric, psi, metric = run(
        first_body, (psi, metric), SENDS + [((24, NZ), F32), FIELD, ((12, ROWS, NZ), F32)], sems=[(4,)], far=(0, 1)
    )
    wall = run(
        wall_body,
        (wall_coef.reshape(30 * NX, NY), ffd_ids.reshape(4 * NX, NY), ffd_weight.reshape(4 * NX, NY)),
        [((3, 24, NZ), F32), ((8, NZ), F32), ((256, 512), jnp.bfloat16), ((8, NZ), jnp.int32)],
    )
    for step in range(SWEEPS):
        received = exchange(sends)
        (z,) = run(inner_body, (psi, metric), [FIELD])
        if step == 0:
            z, wall = lax.optimization_barrier((z, wall))
        if step < SWEEPS - 1:
            psi, *sends = run(
                middle_body, (psi, z, *received, diag, rhs, jac, metric, packed_metric), [FIELD] + SENDS, scratch=[FIELD]
            )
        else:
            psi, slots = run(
                last_body, (psi, z, *received, diag, rhs, jac, *wall), [FIELD, ((256, 48), F32)],
                scratch=[FIELD, FIELD, ((48, 512), jnp.bfloat16), ((48, 512), jnp.bfloat16)], sems=[()], far_outs=(0,),
            )
    got = lax.all_to_all(slots.reshape(256, 1, 48), AXES, 0, 0).reshape(256, 48)
    (grad,) = run(sum_body, (got,), [((3, 16), F32)])
    return psi.reshape(adjoint_init.shape), grad


def solution(mesh):
    in_specs = (
        P(None, "gx", "gy", "wa"),
        P(None, "gx", "gy", "wa"),
        P("gx", "gy", "wa"),
        P(None, "gx", "gy", "wa"),
        P(None, None, "gx", "gy", "wa"),
        P(None, None, "gx", "gy"),
        P(None, "gx", "gy"),
        P(None, "gx", "gy"),
    )
    out_specs = (P(None, "gx", "gy", "wa"), P(None, AXES))
    return jax.shard_map(local, mesh=mesh, in_specs=in_specs, out_specs=out_specs, check_vma=False)
```

```python
import jax
import jax.numpy as jnp
from jax import lax
from jax.experimental import pallas as pl
from jax.experimental.pallas import tpu as pltpu
from jax.sharding import PartitionSpec as P

SWEEPS = 4
OMEGA = 0.6
AXES = ("gx", "gy", "wa")
FIELDS, NX, NY, NZ = 5, 8, 16, 128
ROWS = NX * NY
FAR_ROWS = 96
F32 = jnp.float32
VMEM = pl.BlockSpec(memory_space=pltpu.VMEM)


def pairs(count, odd):
    table = {}
    for i in range(0, count, 2):
        a, b = (i + odd) % count, (i + 1 + odd) % count
        table[a], table[b] = b, a
    return sorted(table.items())


def iota(shape, dim):
    return lax.broadcasted_iota(jnp.int32, shape, dim)


def lane_roll(v, shift):
    return pltpu.roll(v, shift % NZ, axis=1) if shift % NZ else v


def row_roll(v, shift):
    return pltpu.roll(v, shift % v.shape[0], axis=0)


def is_even(axis):
    return lax.axis_index(axis) % 2 == 0


def slab(x):
    return slice(NY * x, NY * (x + 1))


def edge_rows(y):
    return pl.ds(y, NX, stride=NY)


def tile_rows(x, t):
    return slice(NY * x + 8 * t, NY * x + 8 * t + 8)


def pack_edges(psi_ref):
    lane = iota((8, NZ), 1)
    edge = (lane < 2) | (lane >= NZ - 2)
    groups = []
    for g in range((FIELDS + 1) // 2):
        total = jnp.zeros((8, NZ), F32)
        for e in range(2 * g, min(2 * g + 2, FIELDS)):
            for x in range(NX):
                for t in range(2):
                    v = jnp.where(edge, psi_ref[e, tile_rows(x, t), :], 0.0)
                    total = total + lane_roll(v, 2 + 64 * (e % 2) + 4 * (2 * x + t))
        groups.append(total)
    return groups


def pack_metric(metric_ref, out_ref):
    lane = iota((8, NZ), 1)
    same = jnp.zeros((8, NZ), F32)
    after = jnp.zeros((8, NZ), F32)
    before = jnp.zeros((8, NZ), F32)
    for x in range(NX):
        for t in range(2):
            j, rows = 4 * (2 * x + t), tile_rows(x, t)
            v = jnp.where(lane >= NZ - 2, metric_ref[10, rows, :], jnp.where(lane < 2, metric_ref[11, rows, :], 0.0))
            same = same + lane_roll(v, 2 + j)
            after = after + lane_roll(jnp.where(lane == NZ - 1, metric_ref[8, rows, :], 0.0), 1 + j)
            before = before + lane_roll(jnp.where(lane == 0, metric_ref[9, rows, :], 0.0), 3 + j)
    for i, v in enumerate((same, after, before)):
        out_ref[8 * i : 8 * i + 8, :] = v + lane_roll(v, 64)


def emit_sends(psi_ref, metric_ref, packed_metric, groups, sends):
    x0, x1, y0, y1, zz, far = sends
    lane = iota((8, NZ), 1)
    same, after, before = (packed_metric[8 * i : 8 * i + 8, :] for i in range(3))
    for g, p in enumerate(groups):
        v = same * p + after * lane_roll(p, -1) + before * lane_roll(p, 1)
        v = jnp.where(lane % 4 < 2, lane_roll(v, -2), lane_roll(v, 2))
        zz[8 * g : 8 * g + 8, :] = v
        far[8 * g : 8 * g + 8, :] = v
    far[24:, :] = jnp.zeros((FAR_ROWS - 24, NZ), F32)
    even = is_even("gy")
    m4, m6a, m6b = metric_ref[4, edge_rows(15), :], metric_ref[6, edge_rows(14), :], metric_ref[6, edge_rows(15), :]
    m5, m7a, m7b = metric_ref[5, edge_rows(0), :], metric_ref[7, edge_rows(0), :], metric_ref[7, edge_rows(1), :]
    for e in range(FIELDS):
        q14, q15 = psi_ref[e, edge_rows(14), :], psi_ref[e, edge_rows(15), :]
        q0, q1 = psi_ref[e, edge_rows(0), :], psi_ref[e, edge_rows(1), :]
        high = (m4 * q15 + m6a * q14, m6b * q15)
        low = (m7a * q0, m5 * q0 + m7b * q1)
        for r in range(2):
            y0[e, r] = jnp.where(even, high[r], low[r])
            y1[e, r] = jnp.where(even, low[r], high[r])
    even = is_even("gx")
    last, near = slab(NX - 1), slab(NX - 2)
    m0, m2a, m2b = metric_ref[0, last, :], metric_ref[2, near, :], metric_ref[2, last, :]
    m1, m3a, m3b = metric_ref[1, slab(0), :], metric_ref[3, slab(0), :], metric_ref[3, slab(1), :]
    for e in range(FIELDS):
        q6, q7, q0, q1 = psi_ref[e, near, :], psi_ref[e, last, :], psi_ref[e, slab(0), :], psi_ref[e, slab(1), :]
        high = (m0 * q7 + m2a * q6, m2b * q7)
        low = (m3a * q0, m1 * q0 + m3b * q1)
        for r in range(2):
            x0[e, r] = jnp.where(even, high[r], low[r])
            x1[e, r] = jnp.where(even, low[r], high[r])


def first_body(psi_hbm, metric_hbm, x0, x1, y0, y1, zz, far, packed_metric, psi_ref, metric_ref, sems):
    copies = [
        pltpu.make_async_copy(metric_hbm.at[8:12], metric_ref.at[8:12], sems.at[0]),
        pltpu.make_async_copy(psi_hbm, psi_ref, sems.at[1]),
        pltpu.make_async_copy(metric_hbm.at[4:8], metric_ref.at[4:8], sems.at[2]),
        pltpu.make_async_copy(metric_hbm.at[0:4], metric_ref.at[0:4], sems.at[3]),
    ]
    for copy in copies:
        copy.start()
    copies[0].wait()
    pack_metric(metric_ref, packed_metric)
    copies[1].wait()
    groups = pack_edges(psi_ref)
    copies[2].wait()
    copies[3].wait()
    emit_sends(psi_ref, metric_ref, packed_metric, groups, (x0, x1, y0, y1, zz, far))


def inner_body(psi_ref, metric_ref, z_ref):
    lane, row = iota((NY, NZ), 1), iota((NY, NZ), 0)
    for x in range(NX):
        s = slab(x)
        ms = []
        for o, keep in (
            (4, row < NY - 1), (5, row >= 1), (6, row < NY - 2), (7, row >= 2),
            (8, lane < NZ - 1), (9, lane >= 1), (10, lane < NZ - 2), (11, lane >= 2),
        ):
            ms.append(jnp.where(keep, metric_ref[o, s, :], 0.0))
        for e in range(FIELDS):
            q = psi_ref[e, s, :]
            total = row_roll(ms[0] * q, 1) + row_roll(ms[1] * q, -1)
            total = total + (row_roll(ms[2] * q, 2) + row_roll(ms[3] * q, -2))
            total = total + (lane_roll(ms[4] * q, 1) + lane_roll(ms[5] * q, -1))
            total = total + (lane_roll(ms[6] * q, 2) + lane_roll(ms[7] * q, -2))
            for o, step in enumerate((1, -1, 2, -2)):
                if 0 <= x - step < NX:
                    total = total + metric_ref[o, slab(x - step), :] * psi_ref[e, slab(x - step), :]
            z_ref[e, s, :] = total


def from_sides(axis, first, second):
    index = lax.axis_index(axis)
    even = index % 2 == 0
    below = jnp.where(even, second, first)
    above = jnp.where(even, first, second)
    return jnp.where(index > 0, below, 0.0), jnp.where(index < lax.axis_size(axis) - 1, above, 0.0)


def update(psi_ref, z_ref, received, diag_ref, rhs_ref, jac_ref, new_ref, total_ref):
    x0, x1, y0, y1, z0, z1 = received
    lane8 = iota((8, NZ), 1)
    edge = (lane8 < 2) | (lane8 >= NZ - 2)
    for g in range((FIELDS + 1) // 2):
        rows = slice(8 * g, 8 * g + 8)
        below, above = from_sides("wa", z0[rows, :], z1[rows, :])
        both = jnp.where(lane8 % 4 >= 2, below, above)
        for e in range(2 * g, min(2 * g + 2, FIELDS)):
            for x in range(NX):
                for t in range(2):
                    shift = -(2 + 64 * (e % 2) + 4 * (2 * x + t))
                    total_ref[e, tile_rows(x, t), :] = z_ref[e, tile_rows(x, t), :] + jnp.where(edge, lane_roll(both, shift), 0.0)
    for e in range(FIELDS):
        for r in range(2):
            below, above = from_sides("gx", x0[e, r], x1[e, r])
            total_ref[e, slab(r), :] += below
            total_ref[e, slab(NX - 2 + r), :] += above
        for r in range(2):
            below, above = from_sides("gy", y0[e, r], y1[e, r])
            total_ref[e, edge_rows(r), :] += below
            total_ref[e, edge_rows(NY - 2 + r), :] += above
    for x in range(NX):
        s = slab(x)
        d = diag_ref[s, :]
        scale = OMEGA / d
        zs = [total_ref[e, s, :] for e in range(FIELDS)]
        for f in range(FIELDS):
            c = jac_ref[f, s, :].astype(F32) * zs[0]
            for e in range(1, FIELDS):
                c = c + jac_ref[FIELDS * e + f, s, :].astype(F32) * zs[e]
            q = psi_ref[f, s, :]
            new_ref[f, s, :] = q + (rhs_ref[f, s, :] - d * q + c) * scale


def middle_body(psi_ref, z_ref, r0, r1, r2, r3, r4, r5, diag_ref, rhs_ref, jac_ref, metric_ref, packed_metric,
                new_ref, x0, x1, y0, y1, zz, far, total_ref):
    update(psi_ref, z_ref, (r0, r1, r2, r3, r4, r5), diag_ref, rhs_ref, jac_ref, new_ref, total_ref)
    emit_sends(new_ref, metric_ref, packed_metric, pack_edges(new_ref), (x0, x1, y0, y1, zz, far))


def wall_body(coef_ref, ids_ref, weight_ref, coef_out, weight_out, hot_out, low_out):
    def spread(rows, place):
        at = lax.broadcasted_iota(jnp.int32, (rows, 2 * NZ), 1)
        r = lax.broadcasted_iota(jnp.int32, (rows, 2 * NZ), 0)
        return (at % NZ == place(r) + 4 * (at // NZ)).astype(F32)

    def packed(table, chooser):
        v = lax.dot_general(table, chooser, (((0,), (0,)), ((), ())), precision=lax.Precision.HIGHEST,
                            preferred_element_type=F32)
        return v[:8, :NZ] + v[8:, NZ:]

    chooser = spread(4 * NX, lambda r: 64 * (r // 16) + 8 * (r % NX) + 2 + (r // NX) % 2)
    for c in range(3):
        for g in range((FIELDS + 1) // 2):
            count = 4 * NX if g < FIELDS // 2 else 2 * NX
            start = c * 10 * NX + g * 4 * NX
            coef_out[c, 8 * g : 8 * g + 8, :] = packed(coef_ref[start : start + count, :], chooser[:count])
    chooser = spread(4 * NX, lambda r: 8 * (r % NX) + r // NX)
    lane, row = iota((8, NZ), 1), iota((8, NZ), 0)

    def halves(v):
        return jnp.where(lane < 64, v, lane_roll(row_roll(v, 4), 64))

    on = jnp.where(lax.axis_index("wa") == 0, 1.0, 0.0)
    weight_out[...] = halves(packed(weight_ref[...], chooser)) * on
    ids = halves(packed(ids_ref[...].astype(F32), chooser)).astype(jnp.int32)
    low_out[...] = ids % 16
    owner = ids // 16
    slot = iota((256, NZ), 0)
    for s in range(4):
        hit = slot == jnp.broadcast_to(owner[s : s + 1, :], (256, NZ))
        hot_out[:, NZ * s : NZ * s + NZ] = jnp.where(hit, 1.0, 0.0).astype(jnp.bfloat16)


def last_body(psi_ref, z_ref, r0, r1, r2, r3, r4, r5, diag_ref, rhs_ref, jac_ref, coef_ref, weight_ref, hot_ref, low_ref,
              out_hbm, slots_ref, new_ref, total_ref, high_part, low_part, sem):
    update(psi_ref, z_ref, (r0, r1, r2, r3, r4, r5), diag_ref, rhs_ref, jac_ref, new_ref, total_ref)
    copy = pltpu.make_async_copy(new_ref, out_hbm, sem)
    copy.start()
    lane = iota((8, NZ), 1)
    groups = pack_edges(new_ref)
    low = low_ref[...]
    point = iota((16, NZ), 0)
    for c in range(3):
        v = coef_ref[c, 0:8, :] * groups[0]
        for g in range(1, len(groups)):
            v = v + coef_ref[c, 8 * g : 8 * g + 8, :] * groups[g]
        v = v + lane_roll(v, 64)
        v = jnp.where(lane % 4 == 3, v + lane_roll(v, 1), 0.0)
        v = v + lane_roll(v, -1)
        v = v + lane_roll(v, -2)
        v = jnp.where(lane < 64, v, row_roll(v, 4)) * weight_ref[...]
        for s in range(4):
            here = point == jnp.broadcast_to(low[s : s + 1, :], (16, NZ))
            w = jnp.where(here, jnp.broadcast_to(v[s : s + 1, :], (16, NZ)), 0.0)
            top = w.astype(jnp.bfloat16)
            at = (slice(16 * c, 16 * c + 16), slice(NZ * s, NZ * s + NZ))
            high_part[at] = top
            low_part[at] = (w - top.astype(F32)).astype(jnp.bfloat16)
    hot = hot_ref[...]
    dims = (((1,), (1,)), ((), ()))
    slots_ref[...] = lax.dot_general(hot, high_part[...], dims, preferred_element_type=F32) + lax.dot_general(
        hot, low_part[...], dims, preferred_element_type=F32
    )
    copy.wait()


def sum_body(got_ref, out_ref):
    v = got_ref[...].sum(axis=0, keepdims=True)
    for c in range(3):
        out_ref[c : c + 1, :] = v[:, 16 * c : 16 * c + 16]


def run(body, args, outs, scratch=(), sems=(), far=(), far_outs=()):
    hbm = pl.BlockSpec(memory_space=pltpu.HBM)
    args = [pltpu.with_memory_space_constraint(v, pltpu.HBM) if i in far else v for i, v in enumerate(args)]
    return pl.pallas_call(
        body,
        out_shape=[jax.ShapeDtypeStruct(s, d) for s, d in outs],
        in_specs=[hbm if i in far else VMEM for i in range(len(args))],
        out_specs=[hbm if i in far_outs else VMEM for i in range(len(outs))],
        scratch_shapes=[pltpu.VMEM(s, d) for s, d in scratch] + [pltpu.SemaphoreType.DMA(s) for s in sems],
        compiler_params=pltpu.CompilerParams(vmem_limit_bytes=24 << 20),
        cost_estimate=pl.CostEstimate(flops=1000000, bytes_accessed=1000000, transcendentals=0),
    )(*args)


EDGE_X = ((FIELDS, 2, NY, NZ), F32)
EDGE_Y = ((FIELDS, 2, NX, NZ), F32)
EDGE_Z = ((24, NZ), F32)
EDGE_FAR = ((FAR_ROWS, NZ), F32)
SENDS = [EDGE_X, EDGE_X, EDGE_Y, EDGE_Y, EDGE_Z, EDGE_FAR]
FIELD = ((FIELDS, ROWS, NZ), F32)


def exchange(sends):
    x0, x1, y0, y1, zz, far = sends
    def swap(v, axis, odd):
        return lax.ppermute(v, axis, pairs(lax.axis_size(axis), odd))
    two_hops = swap(x1, "gx", 1)
    x = swap(x0, "gx", 0), two_hops
    far = swap(far, "wa", 1)
    y = swap(y0, "gy", 0), swap(y1, "gy", 1)
    zz, two_hops = lax.optimization_barrier((zz, two_hops))
    x = x[0], two_hops
    z = swap(zz, "wa", 0), far
    return (*x, *y, *z)


def local(adjoint_init, objective_grad, diag_term, face_metric, flux_jacobian, wall_coef, ffd_ids, ffd_weight):
    psi = adjoint_init.reshape(FIELDS, ROWS, NZ)
    rhs = objective_grad.reshape(FIELDS, ROWS, NZ)
    diag = diag_term.reshape(ROWS, NZ)
    metric = face_metric.reshape(12, ROWS, NZ)
    jac = flux_jacobian.reshape(FIELDS * FIELDS, ROWS, NZ)
    *sends, packed_metric, psi, metric = run(
        first_body, (psi, metric), SENDS + [((24, NZ), F32), FIELD, ((12, ROWS, NZ), F32)], sems=[(4,)], far=(0, 1)
    )
    wall = run(
        wall_body,
        (wall_coef.reshape(30 * NX, NY), ffd_ids.reshape(4 * NX, NY), ffd_weight.reshape(4 * NX, NY)),
        [((3, 24, NZ), F32), ((8, NZ), F32), ((256, 512), jnp.bfloat16), ((8, NZ), jnp.int32)],
    )
    for step in range(SWEEPS):
        received = exchange(sends)
        (z,) = run(inner_body, (psi, metric), [FIELD])
        if step == 0:
            z, wall = lax.optimization_barrier((z, wall))
        if step < SWEEPS - 1:
            psi, *sends = run(
                middle_body, (psi, z, *received, diag, rhs, jac, metric, packed_metric), [FIELD] + SENDS, scratch=[FIELD]
            )
        else:
            psi, slots = run(
                last_body, (psi, z, *received, diag, rhs, jac, *wall), [FIELD, ((256, 48), F32)],
                scratch=[FIELD, FIELD, ((48, 512), jnp.bfloat16), ((48, 512), jnp.bfloat16)], sems=[()], far_outs=(0,),
            )
    got = lax.all_to_all(slots.reshape(256, 1, 48), AXES, 0, 0).reshape(256, 48)
    (grad,) = run(sum_body, (got,), [((3, 16), F32)])
    return psi.reshape(adjoint_init.shape), grad


def solution(mesh):
    in_specs = (
        P(None, "gx", "gy", "wa"),
        P(None, "gx", "gy", "wa"),
        P("gx", "gy", "wa"),
        P(None, "gx", "gy", "wa"),
        P(None, None, "gx", "gy", "wa"),
        P(None, None, "gx", "gy"),
        P(None, "gx", "gy"),
        P(None, "gx", "gy"),
    )
    out_specs = (P(None, "gx", "gy", "wa"), P(None, AXES))
    return jax.shard_map(local, mesh=mesh, in_specs=in_specs, out_specs=out_specs, check_vma=False)
```

```python
import jax
import jax.numpy as jnp
from jax import lax
from jax.experimental import pallas as pl
from jax.experimental.pallas import tpu as pltpu
from jax.sharding import PartitionSpec as P

SWEEPS = 4
OMEGA = 0.6
AXES = ("gx", "gy", "wa")
FIELDS, NX, NY, NZ = 5, 8, 16, 128
ROWS = NX * NY
FAR_ROWS = 96
F32 = jnp.float32
VMEM = pl.BlockSpec(memory_space=pltpu.VMEM)


def pairs(count, odd):
    table = {}
    for i in range(0, count, 2):
        a, b = (i + odd) % count, (i + 1 + odd) % count
        table[a], table[b] = b, a
    return sorted(table.items())


def iota(shape, dim):
    return lax.broadcasted_iota(jnp.int32, shape, dim)


def lane_roll(v, shift):
    return pltpu.roll(v, shift % NZ, axis=1) if shift % NZ else v


def row_roll(v, shift):
    return pltpu.roll(v, shift % v.shape[0], axis=0)


def is_even(axis):
    return lax.axis_index(axis) % 2 == 0


def slab(x):
    return slice(NY * x, NY * (x + 1))


def edge_rows(y):
    return pl.ds(y, NX, stride=NY)


def tile_rows(x, t):
    return slice(NY * x + 8 * t, NY * x + 8 * t + 8)


def pack_edges(psi_ref):
    lane = iota((8, NZ), 1)
    edge = (lane < 2) | (lane >= NZ - 2)
    groups = []
    for g in range((FIELDS + 1) // 2):
        total = jnp.zeros((8, NZ), F32)
        for e in range(2 * g, min(2 * g + 2, FIELDS)):
            for x in range(NX):
                for t in range(2):
                    v = jnp.where(edge, psi_ref[e, tile_rows(x, t), :], 0.0)
                    total = total + lane_roll(v, 2 + 64 * (e % 2) + 4 * (2 * x + t))
        groups.append(total)
    return groups


def pack_metric(metric_ref, out_ref):
    lane = iota((8, NZ), 1)
    same = jnp.zeros((8, NZ), F32)
    after = jnp.zeros((8, NZ), F32)
    before = jnp.zeros((8, NZ), F32)
    for x in range(NX):
        for t in range(2):
            j, rows = 4 * (2 * x + t), tile_rows(x, t)
            v = jnp.where(lane >= NZ - 2, metric_ref[10, rows, :], jnp.where(lane < 2, metric_ref[11, rows, :], 0.0))
            same = same + lane_roll(v, 2 + j)
            after = after + lane_roll(jnp.where(lane == NZ - 1, metric_ref[8, rows, :], 0.0), 1 + j)
            before = before + lane_roll(jnp.where(lane == 0, metric_ref[9, rows, :], 0.0), 3 + j)
    for i, v in enumerate((same, after, before)):
        out_ref[8 * i : 8 * i + 8, :] = v + lane_roll(v, 64)


def emit_sends(psi_ref, metric_ref, packed_metric, groups, sends):
    x0, x1, y0, y1, zz, far = sends
    lane = iota((8, NZ), 1)
    same, after, before = (packed_metric[8 * i : 8 * i + 8, :] for i in range(3))
    for g, p in enumerate(groups):
        v = same * p + after * lane_roll(p, -1) + before * lane_roll(p, 1)
        v = jnp.where(lane % 4 < 2, lane_roll(v, -2), lane_roll(v, 2))
        zz[8 * g : 8 * g + 8, :] = v
        far[8 * g : 8 * g + 8, :] = v
    far[24:, :] = jnp.zeros((FAR_ROWS - 24, NZ), F32)
    even = is_even("gy")
    m4, m6a, m6b = metric_ref[4, edge_rows(15), :], metric_ref[6, edge_rows(14), :], metric_ref[6, edge_rows(15), :]
    m5, m7a, m7b = metric_ref[5, edge_rows(0), :], metric_ref[7, edge_rows(0), :], metric_ref[7, edge_rows(1), :]
    for e in range(FIELDS):
        q14, q15 = psi_ref[e, edge_rows(14), :], psi_ref[e, edge_rows(15), :]
        q0, q1 = psi_ref[e, edge_rows(0), :], psi_ref[e, edge_rows(1), :]
        high = (m4 * q15 + m6a * q14, m6b * q15)
        low = (m7a * q0, m5 * q0 + m7b * q1)
        for r in range(2):
            y0[e, r] = jnp.where(even, high[r], low[r])
            y1[e, r] = jnp.where(even, low[r], high[r])
    even = is_even("gx")
    last, near = slab(NX - 1), slab(NX - 2)
    m0, m2a, m2b = metric_ref[0, last, :], metric_ref[2, near, :], metric_ref[2, last, :]
    m1, m3a, m3b = metric_ref[1, slab(0), :], metric_ref[3, slab(0), :], metric_ref[3, slab(1), :]
    for e in range(FIELDS):
        q6, q7, q0, q1 = psi_ref[e, near, :], psi_ref[e, last, :], psi_ref[e, slab(0), :], psi_ref[e, slab(1), :]
        high = (m0 * q7 + m2a * q6, m2b * q7)
        low = (m3a * q0, m1 * q0 + m3b * q1)
        for r in range(2):
            x0[e, r] = jnp.where(even, high[r], low[r])
            x1[e, r] = jnp.where(even, low[r], high[r])


def first_body(psi_hbm, metric_hbm, x0, x1, y0, y1, zz, far, packed_metric, psi_ref, metric_ref, sems):
    copies = [
        pltpu.make_async_copy(metric_hbm.at[8:12], metric_ref.at[8:12], sems.at[0]),
        pltpu.make_async_copy(psi_hbm, psi_ref, sems.at[1]),
        pltpu.make_async_copy(metric_hbm.at[4:8], metric_ref.at[4:8], sems.at[2]),
        pltpu.make_async_copy(metric_hbm.at[0:4], metric_ref.at[0:4], sems.at[3]),
    ]
    for copy in copies:
        copy.start()
    copies[0].wait()
    pack_metric(metric_ref, packed_metric)
    copies[1].wait()
    groups = pack_edges(psi_ref)
    copies[2].wait()
    copies[3].wait()
    emit_sends(psi_ref, metric_ref, packed_metric, groups, (x0, x1, y0, y1, zz, far))


def coupled(jac_ref, s, zs):
    out = []
    for f in range(FIELDS):
        c = jac_ref[f, s, :].astype(F32) * zs[0]
        for e in range(1, FIELDS):
            c = c + jac_ref[FIELDS * e + f, s, :].astype(F32) * zs[e]
        out.append(c)
    return out


def inner_body(psi_ref, metric_ref, diag_ref, rhs_ref, jac_ref, base_ref):
    lane, row = iota((NY, NZ), 1), iota((NY, NZ), 0)
    for x in range(NX):
        s = slab(x)
        ms = []
        for o, keep in (
            (4, row < NY - 1), (5, row >= 1), (6, row < NY - 2), (7, row >= 2),
            (8, lane < NZ - 1), (9, lane >= 1), (10, lane < NZ - 2), (11, lane >= 2),
        ):
            ms.append(jnp.where(keep, metric_ref[o, s, :], 0.0))
        zs = []
        for e in range(FIELDS):
            q = psi_ref[e, s, :]
            total = row_roll(ms[0] * q, 1) + row_roll(ms[1] * q, -1)
            total = total + (row_roll(ms[2] * q, 2) + row_roll(ms[3] * q, -2))
            total = total + (lane_roll(ms[4] * q, 1) + lane_roll(ms[5] * q, -1))
            total = total + (lane_roll(ms[6] * q, 2) + lane_roll(ms[7] * q, -2))
            for o, step in enumerate((1, -1, 2, -2)):
                if 0 <= x - step < NX:
                    total = total + metric_ref[o, slab(x - step), :] * psi_ref[e, slab(x - step), :]
            zs.append(total)
        d = diag_ref[s, :]
        scale = OMEGA / d
        for f, c in enumerate(coupled(jac_ref, s, zs)):
            q = psi_ref[f, s, :]
            base_ref[f, s, :] = q + (rhs_ref[f, s, :] - d * q + c) * scale


def from_sides(axis, first, second):
    index = lax.axis_index(axis)
    even = index % 2 == 0
    below = jnp.where(even, second, first)
    above = jnp.where(even, first, second)
    return jnp.where(index > 0, below, 0.0), jnp.where(index < lax.axis_size(axis) - 1, above, 0.0)


def update(base_ref, received, diag_ref, jac_ref, new_ref, rows_ref):
    x0, x1, y0, y1, z0, z1 = received
    lane8 = iota((8, NZ), 1)
    edge = (lane8 < 2) | (lane8 >= NZ - 2)
    row = iota((NY, NZ), 0)
    outer = (row < 2) | (row >= NY - 2)
    walls = []
    for g in range((FIELDS + 1) // 2):
        below, above = from_sides("wa", z0[8 * g : 8 * g + 8, :], z1[8 * g : 8 * g + 8, :])
        walls.append(jnp.where(lane8 % 4 >= 2, below, above))
    for e in range(FIELDS):
        for r in range(2):
            below, above = from_sides("gy", y0[e, r], y1[e, r])
            rows_ref[e, edge_rows(r), :] = below
            rows_ref[e, edge_rows(NY - 2 + r), :] = above
    for x in range(NX):
        s = slab(x)
        zs = []
        for e in range(FIELDS):
            tiles = [
                jnp.where(edge, lane_roll(walls[e // 2], -(2 + 64 * (e % 2) + 4 * (2 * x + t))), 0.0) for t in range(2)
            ]
            total = jnp.concatenate(tiles, axis=0) + jnp.where(outer, rows_ref[e, s, :], 0.0)
            if x < 2:
                total = total + from_sides("gx", x0[e, x], x1[e, x])[0]
            if x >= NX - 2:
                total = total + from_sides("gx", x0[e, x - NX + 2], x1[e, x - NX + 2])[1]
            zs.append(total)
        scale = OMEGA / diag_ref[s, :]
        for f, c in enumerate(coupled(jac_ref, s, zs)):
            new_ref[f, s, :] = base_ref[f, s, :] + c * scale


def middle_body(base_ref, r0, r1, r2, r3, r4, r5, diag_ref, jac_ref, metric_ref, packed_metric,
                new_ref, x0, x1, y0, y1, zz, far, rows_ref):
    update(base_ref, (r0, r1, r2, r3, r4, r5), diag_ref, jac_ref, new_ref, rows_ref)
    emit_sends(new_ref, metric_ref, packed_metric, pack_edges(new_ref), (x0, x1, y0, y1, zz, far))


def wall_body(coef_ref, ids_ref, weight_ref, coef_out, weight_out, hot_out, low_out):
    def spread(rows, place):
        at = lax.broadcasted_iota(jnp.int32, (rows, 2 * NZ), 1)
        r = lax.broadcasted_iota(jnp.int32, (rows, 2 * NZ), 0)
        return (at % NZ == place(r) + 4 * (at // NZ)).astype(F32)

    def packed(table, chooser):
        v = lax.dot_general(table, chooser, (((0,), (0,)), ((), ())), precision=lax.Precision.HIGHEST,
                            preferred_element_type=F32)
        return v[:8, :NZ] + v[8:, NZ:]

    chooser = spread(4 * NX, lambda r: 64 * (r // 16) + 8 * (r % NX) + 2 + (r // NX) % 2)
    for c in range(3):
        for g in range((FIELDS + 1) // 2):
            count = 4 * NX if g < FIELDS // 2 else 2 * NX
            start = c * 10 * NX + g * 4 * NX
            coef_out[c, 8 * g : 8 * g + 8, :] = packed(coef_ref[start : start + count, :], chooser[:count])
    chooser = spread(4 * NX, lambda r: 8 * (r % NX) + r // NX)
    lane, row = iota((8, NZ), 1), iota((8, NZ), 0)

    def halves(v):
        return jnp.where(lane < 64, v, lane_roll(row_roll(v, 4), 64))

    on = jnp.where(lax.axis_index("wa") == 0, 1.0, 0.0)
    weight_out[...] = halves(packed(weight_ref[...], chooser)) * on
    ids = halves(packed(ids_ref[...].astype(F32), chooser)).astype(jnp.int32)
    low_out[...] = ids % 16
    owner = ids // 16
    slot = iota((256, NZ), 0)
    for s in range(4):
        hit = slot == jnp.broadcast_to(owner[s : s + 1, :], (256, NZ))
        hot_out[:, NZ * s : NZ * s + NZ] = jnp.where(hit, 1.0, 0.0).astype(jnp.bfloat16)


def last_body(base_ref, r0, r1, r2, r3, r4, r5, diag_ref, jac_ref, coef_ref, weight_ref, hot_ref, low_ref,
              out_hbm, slots_ref, new_ref, rows_ref, high_part, low_part, sem):
    update(base_ref, (r0, r1, r2, r3, r4, r5), diag_ref, jac_ref, new_ref, rows_ref)
    copy = pltpu.make_async_copy(new_ref, out_hbm, sem)
    copy.start()
    lane = iota((8, NZ), 1)
    groups = pack_edges(new_ref)
    low = low_ref[...]
    point = iota((16, NZ), 0)
    for c in range(3):
        v = coef_ref[c, 0:8, :] * groups[0]
        for g in range(1, len(groups)):
            v = v + coef_ref[c, 8 * g : 8 * g + 8, :] * groups[g]
        v = v + lane_roll(v, 64)
        v = jnp.where(lane % 4 == 3, v + lane_roll(v, 1), 0.0)
        v = v + lane_roll(v, -1)
        v = v + lane_roll(v, -2)
        v = jnp.where(lane < 64, v, row_roll(v, 4)) * weight_ref[...]
        for s in range(4):
            here = point == jnp.broadcast_to(low[s : s + 1, :], (16, NZ))
            w = jnp.where(here, jnp.broadcast_to(v[s : s + 1, :], (16, NZ)), 0.0)
            top = w.astype(jnp.bfloat16)
            at = (slice(16 * c, 16 * c + 16), slice(NZ * s, NZ * s + NZ))
            high_part[at] = top
            low_part[at] = (w - top.astype(F32)).astype(jnp.bfloat16)
    hot = hot_ref[...]
    dims = (((1,), (1,)), ((), ()))
    slots_ref[...] = lax.dot_general(hot, high_part[...], dims, preferred_element_type=F32) + lax.dot_general(
        hot, low_part[...], dims, preferred_element_type=F32
    )
    copy.wait()


def sum_body(got_ref, out_ref):
    v = got_ref[...].sum(axis=0, keepdims=True)
    for c in range(3):
        out_ref[c : c + 1, :] = v[:, 16 * c : 16 * c + 16]


def run(body, args, outs, scratch=(), sems=(), far=(), far_outs=()):
    hbm = pl.BlockSpec(memory_space=pltpu.HBM)
    args = [pltpu.with_memory_space_constraint(v, pltpu.HBM) if i in far else v for i, v in enumerate(args)]
    return pl.pallas_call(
        body,
        out_shape=[jax.ShapeDtypeStruct(s, d) for s, d in outs],
        in_specs=[hbm if i in far else VMEM for i in range(len(args))],
        out_specs=[hbm if i in far_outs else VMEM for i in range(len(outs))],
        scratch_shapes=[pltpu.VMEM(s, d) for s, d in scratch] + [pltpu.SemaphoreType.DMA(s) for s in sems],
        compiler_params=pltpu.CompilerParams(vmem_limit_bytes=24 << 20),
        cost_estimate=pl.CostEstimate(flops=1000000, bytes_accessed=1000000, transcendentals=0),
    )(*args)


EDGE_X = ((FIELDS, 2, NY, NZ), F32)
EDGE_Y = ((FIELDS, 2, NX, NZ), F32)
EDGE_Z = ((24, NZ), F32)
EDGE_FAR = ((FAR_ROWS, NZ), F32)
SENDS = [EDGE_X, EDGE_X, EDGE_Y, EDGE_Y, EDGE_Z, EDGE_FAR]
FIELD = ((FIELDS, ROWS, NZ), F32)


def exchange(sends):
    x0, x1, y0, y1, zz, far = sends
    def swap(v, axis, odd):
        return lax.ppermute(v, axis, pairs(lax.axis_size(axis), odd))
    two_hops = swap(x1, "gx", 1)
    x = swap(x0, "gx", 0), two_hops
    far = swap(far, "wa", 1)
    y = swap(y0, "gy", 0), swap(y1, "gy", 1)
    zz, two_hops = lax.optimization_barrier((zz, two_hops))
    x = x[0], two_hops
    z = swap(zz, "wa", 0), far
    return (*x, *y, *z)


def local(adjoint_init, objective_grad, diag_term, face_metric, flux_jacobian, wall_coef, ffd_ids, ffd_weight):
    psi = adjoint_init.reshape(FIELDS, ROWS, NZ)
    rhs = objective_grad.reshape(FIELDS, ROWS, NZ)
    diag = diag_term.reshape(ROWS, NZ)
    metric = face_metric.reshape(12, ROWS, NZ)
    jac = flux_jacobian.reshape(FIELDS * FIELDS, ROWS, NZ)
    *sends, packed_metric, psi, metric = run(
        first_body, (psi, metric), SENDS + [((24, NZ), F32), FIELD, ((12, ROWS, NZ), F32)], sems=[(4,)], far=(0, 1)
    )
    jac, rhs, diag, packed_metric = lax.optimization_barrier((jac, rhs, diag, packed_metric))
    wall = run(
        wall_body,
        (wall_coef.reshape(30 * NX, NY), ffd_ids.reshape(4 * NX, NY), ffd_weight.reshape(4 * NX, NY)),
        [((3, 24, NZ), F32), ((8, NZ), F32), ((256, 512), jnp.bfloat16), ((8, NZ), jnp.int32)],
    )
    for step in range(SWEEPS):
        received = exchange(sends)
        (base,) = run(inner_body, (psi, metric, diag, rhs, jac), [FIELD])
        if step == 1:
            base, wall = lax.optimization_barrier((base, wall))
        if step < SWEEPS - 1:
            psi, *sends = run(
                middle_body, (base, *received, diag, jac, metric, packed_metric), [FIELD] + SENDS, scratch=[FIELD]
            )
        else:
            psi, slots = run(
                last_body, (base, *received, diag, jac, *wall), [FIELD, ((256, 48), F32)],
                scratch=[FIELD, FIELD, ((48, 512), jnp.bfloat16), ((48, 512), jnp.bfloat16)], sems=[()], far_outs=(0,),
            )
    got = lax.all_to_all(slots.reshape(256, 1, 48), AXES, 0, 0).reshape(256, 48)
    (grad,) = run(sum_body, (got,), [((3, 16), F32)])
    return psi.reshape(adjoint_init.shape), grad


def solution(mesh):
    in_specs = (
        P(None, "gx", "gy", "wa"),
        P(None, "gx", "gy", "wa"),
        P("gx", "gy", "wa"),
        P(None, "gx", "gy", "wa"),
        P(None, None, "gx", "gy", "wa"),
        P(None, None, "gx", "gy"),
        P(None, "gx", "gy"),
        P(None, "gx", "gy"),
    )
    out_specs = (P(None, "gx", "gy", "wa"), P(None, AXES))
    return jax.shard_map(local, mesh=mesh, in_specs=in_specs, out_specs=out_specs, check_vma=False)
```

```python
import jax
import jax.numpy as jnp
from jax import lax
from jax.experimental import pallas as pl
from jax.experimental.pallas import tpu as pltpu
from jax.sharding import PartitionSpec as P

SWEEPS = 4
OMEGA = 0.6
AXES = ("gx", "gy", "wa")
FIELDS, NX, NY, NZ = 5, 8, 16, 128
ROWS = NX * NY
FAR_ROWS = 88
F32 = jnp.float32
VMEM = pl.BlockSpec(memory_space=pltpu.VMEM)


def pairs(count, odd):
    table = {}
    for i in range(0, count, 2):
        a, b = (i + odd) % count, (i + 1 + odd) % count
        table[a], table[b] = b, a
    return sorted(table.items())


def iota(shape, dim):
    return lax.broadcasted_iota(jnp.int32, shape, dim)


def lane_roll(v, shift):
    return pltpu.roll(v, shift % NZ, axis=1) if shift % NZ else v


def row_roll(v, shift):
    return pltpu.roll(v, shift % v.shape[0], axis=0)


def is_even(axis):
    return lax.axis_index(axis) % 2 == 0


def slab(x):
    return slice(NY * x, NY * (x + 1))


def edge_rows(y):
    return pl.ds(y, NX, stride=NY)


def tile_rows(x, t):
    return slice(NY * x + 8 * t, NY * x + 8 * t + 8)


def pack_edges(psi_ref):
    lane = iota((8, NZ), 1)
    edge = (lane < 2) | (lane >= NZ - 2)
    groups = []
    for g in range((FIELDS + 1) // 2):
        total = jnp.zeros((8, NZ), F32)
        for e in range(2 * g, min(2 * g + 2, FIELDS)):
            for x in range(NX):
                for t in range(2):
                    v = jnp.where(edge, psi_ref[e, tile_rows(x, t), :], 0.0)
                    total = total + lane_roll(v, 2 + 64 * (e % 2) + 4 * (2 * x + t))
        groups.append(total)
    return groups


def pack_metric(metric_ref, out_ref):
    lane = iota((8, NZ), 1)
    same = jnp.zeros((8, NZ), F32)
    after = jnp.zeros((8, NZ), F32)
    before = jnp.zeros((8, NZ), F32)
    for x in range(NX):
        for t in range(2):
            j, rows = 4 * (2 * x + t), tile_rows(x, t)
            v = jnp.where(lane >= NZ - 2, metric_ref[10, rows, :], jnp.where(lane < 2, metric_ref[11, rows, :], 0.0))
            same = same + lane_roll(v, 2 + j)
            after = after + lane_roll(jnp.where(lane == NZ - 1, metric_ref[8, rows, :], 0.0), 1 + j)
            before = before + lane_roll(jnp.where(lane == 0, metric_ref[9, rows, :], 0.0), 3 + j)
    for i, v in enumerate((same, after, before)):
        out_ref[8 * i : 8 * i + 8, :] = v + lane_roll(v, 64)


def emit_sends(psi_ref, metric_ref, packed_metric, groups, sends):
    x0, x1, y0, y1, zz, far = sends
    lane = iota((8, NZ), 1)
    same, after, before = (packed_metric[8 * i : 8 * i + 8, :] for i in range(3))
    for g, p in enumerate(groups):
        v = same * p + after * lane_roll(p, -1) + before * lane_roll(p, 1)
        v = jnp.where(lane % 4 < 2, lane_roll(v, -2), lane_roll(v, 2))
        zz[8 * g : 8 * g + 8, :] = v
        far[8 * g : 8 * g + 8, :] = v
    far[24:, :] = jnp.zeros((FAR_ROWS - 24, NZ), F32)
    even = is_even("gy")
    m4, m6a, m6b = metric_ref[4, edge_rows(15), :], metric_ref[6, edge_rows(14), :], metric_ref[6, edge_rows(15), :]
    m5, m7a, m7b = metric_ref[5, edge_rows(0), :], metric_ref[7, edge_rows(0), :], metric_ref[7, edge_rows(1), :]
    for e in range(FIELDS):
        q14, q15 = psi_ref[e, edge_rows(14), :], psi_ref[e, edge_rows(15), :]
        q0, q1 = psi_ref[e, edge_rows(0), :], psi_ref[e, edge_rows(1), :]
        high = (m4 * q15 + m6a * q14, m6b * q15)
        low = (m7a * q0, m5 * q0 + m7b * q1)
        for r in range(2):
            y0[e, r] = jnp.where(even, high[r], low[r])
            y1[e, r] = jnp.where(even, low[r], high[r])
    even = is_even("gx")
    last, near = slab(NX - 1), slab(NX - 2)
    m0, m2a, m2b = metric_ref[0, last, :], metric_ref[2, near, :], metric_ref[2, last, :]
    m1, m3a, m3b = metric_ref[1, slab(0), :], metric_ref[3, slab(0), :], metric_ref[3, slab(1), :]
    for e in range(FIELDS):
        q6, q7, q0, q1 = psi_ref[e, near, :], psi_ref[e, last, :], psi_ref[e, slab(0), :], psi_ref[e, slab(1), :]
        high = (m0 * q7 + m2a * q6, m2b * q7)
        low = (m3a * q0, m1 * q0 + m3b * q1)
        for r in range(2):
            x0[e, r] = jnp.where(even, high[r], low[r])
            x1[e, r] = jnp.where(even, low[r], high[r])


def first_body(psi_hbm, metric_hbm, x0, x1, y0, y1, zz, far, packed_metric, psi_ref, metric_ref, sems):
    copies = [
        pltpu.make_async_copy(metric_hbm.at[8:12], metric_ref.at[8:12], sems.at[0]),
        pltpu.make_async_copy(psi_hbm, psi_ref, sems.at[1]),
        pltpu.make_async_copy(metric_hbm.at[4:8], metric_ref.at[4:8], sems.at[2]),
        pltpu.make_async_copy(metric_hbm.at[0:4], metric_ref.at[0:4], sems.at[3]),
    ]
    for copy in copies:
        copy.start()
    copies[0].wait()
    pack_metric(metric_ref, packed_metric)
    copies[1].wait()
    groups = pack_edges(psi_ref)
    copies[2].wait()
    copies[3].wait()
    emit_sends(psi_ref, metric_ref, packed_metric, groups, (x0, x1, y0, y1, zz, far))


def inner_body(psi_ref, metric_ref, z_ref):
    lane, row = iota((NY, NZ), 1), iota((NY, NZ), 0)
    for x in range(NX):
        s = slab(x)
        ms = []
        for o, keep in (
            (4, row < NY - 1), (5, row >= 1), (6, row < NY - 2), (7, row >= 2),
            (8, lane < NZ - 1), (9, lane >= 1), (10, lane < NZ - 2), (11, lane >= 2),
        ):
            ms.append(jnp.where(keep, metric_ref[o, s, :], 0.0))
        for e in range(FIELDS):
            q = psi_ref[e, s, :]
            total = row_roll(ms[0] * q, 1) + row_roll(ms[1] * q, -1)
            total = total + (row_roll(ms[2] * q, 2) + row_roll(ms[3] * q, -2))
            total = total + (lane_roll(ms[4] * q, 1) + lane_roll(ms[5] * q, -1))
            total = total + (lane_roll(ms[6] * q, 2) + lane_roll(ms[7] * q, -2))
            for o, step in enumerate((1, -1, 2, -2)):
                if 0 <= x - step < NX:
                    total = total + metric_ref[o, slab(x - step), :] * psi_ref[e, slab(x - step), :]
            z_ref[e, s, :] = total


def from_sides(axis, first, second):
    index = lax.axis_index(axis)
    even = index % 2 == 0
    below = jnp.where(even, second, first)
    above = jnp.where(even, first, second)
    return jnp.where(index > 0, below, 0.0), jnp.where(index < lax.axis_size(axis) - 1, above, 0.0)


def update(psi_ref, z_ref, received, diag_ref, rhs_ref, jac_ref, new_ref, total_ref):
    x0, x1, y0, y1, z0, z1 = received
    lane8 = iota((8, NZ), 1)
    edge = (lane8 < 2) | (lane8 >= NZ - 2)
    for g in range((FIELDS + 1) // 2):
        rows = slice(8 * g, 8 * g + 8)
        below, above = from_sides("wa", z0[rows, :], z1[rows, :])
        both = jnp.where(lane8 % 4 >= 2, below, above)
        for e in range(2 * g, min(2 * g + 2, FIELDS)):
            for x in range(NX):
                for t in range(2):
                    shift = -(2 + 64 * (e % 2) + 4 * (2 * x + t))
                    total_ref[e, tile_rows(x, t), :] = z_ref[e, tile_rows(x, t), :] + jnp.where(edge, lane_roll(both, shift), 0.0)
    for e in range(FIELDS):
        for r in range(2):
            below, above = from_sides("gx", x0[e, r], x1[e, r])
            total_ref[e, slab(r), :] += below
            total_ref[e, slab(NX - 2 + r), :] += above
        for r in range(2):
            below, above = from_sides("gy", y0[e, r], y1[e, r])
            total_ref[e, edge_rows(r), :] += below
            total_ref[e, edge_rows(NY - 2 + r), :] += above
    for x in range(NX):
        s = slab(x)
        d = diag_ref[s, :]
        scale = OMEGA / d
        zs = [total_ref[e, s, :] for e in range(FIELDS)]
        for f in range(FIELDS):
            c = jac_ref[f, s, :].astype(F32) * zs[0]
            for e in range(1, FIELDS):
                c = c + jac_ref[FIELDS * e + f, s, :].astype(F32) * zs[e]
            q = psi_ref[f, s, :]
            new_ref[f, s, :] = q + (rhs_ref[f, s, :] - d * q + c) * scale


def middle_body(psi_ref, z_ref, r0, r1, r2, r3, r4, r5, diag_ref, rhs_ref, jac_ref, metric_ref, packed_metric,
                new_ref, x0, x1, y0, y1, zz, far, total_ref):
    update(psi_ref, z_ref, (r0, r1, r2, r3, r4, r5), diag_ref, rhs_ref, jac_ref, new_ref, total_ref)
    emit_sends(new_ref, metric_ref, packed_metric, pack_edges(new_ref), (x0, x1, y0, y1, zz, far))


def wall_body(coef_ref, ids_ref, weight_ref, coef_out, weight_out, hot_out, low_out):
    def spread(rows, place):
        at = lax.broadcasted_iota(jnp.int32, (rows, 2 * NZ), 1)
        r = lax.broadcasted_iota(jnp.int32, (rows, 2 * NZ), 0)
        return (at % NZ == place(r) + 4 * (at // NZ)).astype(F32)

    def packed(table, chooser):
        v = lax.dot_general(table, chooser, (((0,), (0,)), ((), ())), precision=lax.Precision.HIGHEST,
                            preferred_element_type=F32)
        return v[:8, :NZ] + v[8:, NZ:]

    chooser = spread(4 * NX, lambda r: 64 * (r // 16) + 8 * (r % NX) + 2 + (r // NX) % 2)
    for c in range(3):
        for g in range((FIELDS + 1) // 2):
            count = 4 * NX if g < FIELDS // 2 else 2 * NX
            start = c * 10 * NX + g * 4 * NX
            coef_out[c, 8 * g : 8 * g + 8, :] = packed(coef_ref[start : start + count, :], chooser[:count])
    chooser = spread(4 * NX, lambda r: 8 * (r % NX) + r // NX)
    lane, row = iota((8, NZ), 1), iota((8, NZ), 0)

    def halves(v):
        return jnp.where(lane < 64, v, lane_roll(row_roll(v, 4), 64))

    on = jnp.where(lax.axis_index("wa") == 0, 1.0, 0.0)
    weight_out[...] = halves(packed(weight_ref[...], chooser)) * on
    ids = halves(packed(ids_ref[...].astype(F32), chooser)).astype(jnp.int32)
    low_out[...] = ids % 16
    owner = ids // 16
    slot = iota((256, NZ), 0)
    for s in range(4):
        hit = slot == jnp.broadcast_to(owner[s : s + 1, :], (256, NZ))
        hot_out[:, NZ * s : NZ * s + NZ] = jnp.where(hit, 1.0, 0.0).astype(jnp.bfloat16)


def last_body(psi_ref, z_ref, r0, r1, r2, r3, r4, r5, diag_ref, rhs_ref, jac_ref, coef_ref, weight_ref, hot_ref, low_ref,
              out_hbm, slots_ref, new_ref, total_ref, high_part, low_part, sem):
    update(psi_ref, z_ref, (r0, r1, r2, r3, r4, r5), diag_ref, rhs_ref, jac_ref, new_ref, total_ref)
    copy = pltpu.make_async_copy(new_ref, out_hbm, sem)
    copy.start()
    lane = iota((8, NZ), 1)
    groups = pack_edges(new_ref)
    low = low_ref[...]
    point = iota((16, NZ), 0)
    for c in range(3):
        v = coef_ref[c, 0:8, :] * groups[0]
        for g in range(1, len(groups)):
            v = v + coef_ref[c, 8 * g : 8 * g + 8, :] * groups[g]
        v = v + lane_roll(v, 64)
        v = jnp.where(lane % 4 == 3, v + lane_roll(v, 1), 0.0)
        v = v + lane_roll(v, -1)
        v = v + lane_roll(v, -2)
        v = jnp.where(lane < 64, v, row_roll(v, 4)) * weight_ref[...]
        for s in range(4):
            here = point == jnp.broadcast_to(low[s : s + 1, :], (16, NZ))
            w = jnp.where(here, jnp.broadcast_to(v[s : s + 1, :], (16, NZ)), 0.0)
            top = w.astype(jnp.bfloat16)
            at = (slice(16 * c, 16 * c + 16), slice(NZ * s, NZ * s + NZ))
            high_part[at] = top
            low_part[at] = (w - top.astype(F32)).astype(jnp.bfloat16)
    hot = hot_ref[...]
    dims = (((1,), (1,)), ((), ()))
    slots_ref[...] = lax.dot_general(hot, high_part[...], dims, preferred_element_type=F32) + lax.dot_general(
        hot, low_part[...], dims, preferred_element_type=F32
    )
    copy.wait()


def sum_body(got_ref, out_ref):
    v = got_ref[...].sum(axis=0, keepdims=True)
    for c in range(3):
        out_ref[c : c + 1, :] = v[:, 16 * c : 16 * c + 16]


def run(body, args, outs, scratch=(), sems=(), far=(), far_outs=()):
    hbm = pl.BlockSpec(memory_space=pltpu.HBM)
    args = [pltpu.with_memory_space_constraint(v, pltpu.HBM) if i in far else v for i, v in enumerate(args)]
    return pl.pallas_call(
        body,
        out_shape=[jax.ShapeDtypeStruct(s, d) for s, d in outs],
        in_specs=[hbm if i in far else VMEM for i in range(len(args))],
        out_specs=[hbm if i in far_outs else VMEM for i in range(len(outs))],
        scratch_shapes=[pltpu.VMEM(s, d) for s, d in scratch] + [pltpu.SemaphoreType.DMA(s) for s in sems],
        compiler_params=pltpu.CompilerParams(vmem_limit_bytes=24 << 20),
        cost_estimate=pl.CostEstimate(flops=1000000, bytes_accessed=1000000, transcendentals=0),
    )(*args)


EDGE_X = ((FIELDS, 2, NY, NZ), F32)
EDGE_Y = ((FIELDS, 2, NX, NZ), F32)
EDGE_Z = ((24, NZ), F32)
EDGE_FAR = ((FAR_ROWS, NZ), F32)
SENDS = [EDGE_X, EDGE_X, EDGE_Y, EDGE_Y, EDGE_Z, EDGE_FAR]
FIELD = ((FIELDS, ROWS, NZ), F32)


def exchange(sends):
    x0, x1, y0, y1, zz, far = sends
    def swap(v, axis, odd):
        return lax.ppermute(v, axis, pairs(lax.axis_size(axis), odd))
    two_hops = swap(x1, "gx", 1)
    one_hop = swap(x0, "gx", 0)
    far = swap(far, "wa", 1)
    y = swap(y0, "gy", 0), swap(y1, "gy", 1)
    zz, one_hop = lax.optimization_barrier((zz, one_hop))
    x = one_hop, two_hops
    z = swap(zz, "wa", 0), far
    return (*x, *y, *z)


def local(adjoint_init, objective_grad, diag_term, face_metric, flux_jacobian, wall_coef, ffd_ids, ffd_weight):
    psi = adjoint_init.reshape(FIELDS, ROWS, NZ)
    rhs = objective_grad.reshape(FIELDS, ROWS, NZ)
    diag = diag_term.reshape(ROWS, NZ)
    metric = face_metric.reshape(12, ROWS, NZ)
    jac = flux_jacobian.reshape(FIELDS * FIELDS, ROWS, NZ)
    *sends, packed_metric, psi, metric = run(
        first_body, (psi, metric), SENDS + [((24, NZ), F32), FIELD, ((12, ROWS, NZ), F32)], sems=[(4,)], far=(0, 1)
    )
    wall = run(
        wall_body,
        (wall_coef.reshape(30 * NX, NY), ffd_ids.reshape(4 * NX, NY), ffd_weight.reshape(4 * NX, NY)),
        [((3, 24, NZ), F32), ((8, NZ), F32), ((256, 512), jnp.bfloat16), ((8, NZ), jnp.int32)],
    )
    for step in range(SWEEPS):
        received = exchange(sends)
        (z,) = run(inner_body, (psi, metric), [FIELD])
        if step == 0:
            z, wall = lax.optimization_barrier((z, wall))
        if step < SWEEPS - 1:
            psi, *sends = run(
                middle_body, (psi, z, *received, diag, rhs, jac, metric, packed_metric), [FIELD] + SENDS, scratch=[FIELD]
            )
        else:
            psi, slots = run(
                last_body, (psi, z, *received, diag, rhs, jac, *wall), [FIELD, ((256, 48), F32)],
                scratch=[FIELD, FIELD, ((48, 512), jnp.bfloat16), ((48, 512), jnp.bfloat16)], sems=[()], far_outs=(0,),
            )
    got = lax.all_to_all(slots.reshape(256, 1, 48), AXES, 0, 0).reshape(256, 48)
    (grad,) = run(sum_body, (got,), [((3, 16), F32)])
    return psi.reshape(adjoint_init.shape), grad


def solution(mesh):
    in_specs = (
        P(None, "gx", "gy", "wa"),
        P(None, "gx", "gy", "wa"),
        P("gx", "gy", "wa"),
        P(None, "gx", "gy", "wa"),
        P(None, None, "gx", "gy", "wa"),
        P(None, None, "gx", "gy"),
        P(None, "gx", "gy"),
        P(None, "gx", "gy"),
    )
    out_specs = (P(None, "gx", "gy", "wa"), P(None, AXES))
    return jax.shard_map(local, mesh=mesh, in_specs=in_specs, out_specs=out_specs, check_vma=False)
```

```python
import jax
import jax.numpy as jnp
from jax import lax
from jax.experimental import pallas as pl
from jax.experimental.pallas import tpu as pltpu
from jax.sharding import PartitionSpec as P

SWEEPS = 4
OMEGA = 0.6
AXES = ("gx", "gy", "wa")
FIELDS, NX, NY, NZ = 5, 8, 16, 128
ROWS = NX * NY
FAR_ROWS = 88
OUTER_ROWS = (0, 1, NY - 2, NY - 1)
F32 = jnp.float32
VMEM = pl.BlockSpec(memory_space=pltpu.VMEM)


def pairs(count, odd):
    table = {}
    for i in range(0, count, 2):
        a, b = (i + odd) % count, (i + 1 + odd) % count
        table[a], table[b] = b, a
    return sorted(table.items())


def iota(shape, dim):
    return lax.broadcasted_iota(jnp.int32, shape, dim)


def lane_roll(v, shift):
    return pltpu.roll(v, shift % NZ, axis=1) if shift % NZ else v


def row_roll(v, shift):
    return pltpu.roll(v, shift % v.shape[0], axis=0)


def is_even(axis):
    return lax.axis_index(axis) % 2 == 0


def slab(x):
    return slice(NY * x, NY * (x + 1))


def edge_rows(y):
    return pl.ds(y, NX, stride=NY)


def tile_rows(x, t):
    return slice(NY * x + 8 * t, NY * x + 8 * t + 8)


def pack_edges(psi_ref):
    lane = iota((8, NZ), 1)
    edge = (lane < 2) | (lane >= NZ - 2)
    groups = []
    for g in range((FIELDS + 1) // 2):
        total = jnp.zeros((8, NZ), F32)
        for e in range(2 * g, min(2 * g + 2, FIELDS)):
            for x in range(NX):
                for t in range(2):
                    v = jnp.where(edge, psi_ref[e, tile_rows(x, t), :], 0.0)
                    total = total + lane_roll(v, 2 + 64 * (e % 2) + 4 * (2 * x + t))
        groups.append(total)
    return groups


def pack_metric(metric_ref, out_ref):
    lane = iota((8, NZ), 1)
    same = jnp.zeros((8, NZ), F32)
    after = jnp.zeros((8, NZ), F32)
    before = jnp.zeros((8, NZ), F32)
    for x in range(NX):
        for t in range(2):
            j, rows = 4 * (2 * x + t), tile_rows(x, t)
            v = jnp.where(lane >= NZ - 2, metric_ref[10, rows, :], jnp.where(lane < 2, metric_ref[11, rows, :], 0.0))
            same = same + lane_roll(v, 2 + j)
            after = after + lane_roll(jnp.where(lane == NZ - 1, metric_ref[8, rows, :], 0.0), 1 + j)
            before = before + lane_roll(jnp.where(lane == 0, metric_ref[9, rows, :], 0.0), 3 + j)
    for i, v in enumerate((same, after, before)):
        out_ref[8 * i : 8 * i + 8, :] = v + lane_roll(v, 64)


def emit_sends(psi_ref, metric_ref, packed_metric, groups, sends, rows=None):
    x0, x1, y0, y1, zz, far = sends
    lane = iota((8, NZ), 1)
    same, after, before = (packed_metric[8 * i : 8 * i + 8, :] for i in range(3))
    for g, p in enumerate(groups):
        v = same * p + after * lane_roll(p, -1) + before * lane_roll(p, 1)
        v = jnp.where(lane % 4 < 2, lane_roll(v, -2), lane_roll(v, 2))
        zz[8 * g : 8 * g + 8, :] = v
        far[8 * g : 8 * g + 8, :] = v
    far[24:, :] = jnp.zeros((FAR_ROWS - 24, NZ), F32)
    even = is_even("gy")
    m4, m6a, m6b = metric_ref[4, edge_rows(15), :], metric_ref[6, edge_rows(14), :], metric_ref[6, edge_rows(15), :]
    m5, m7a, m7b = metric_ref[5, edge_rows(0), :], metric_ref[7, edge_rows(0), :], metric_ref[7, edge_rows(1), :]
    for e in range(FIELDS):
        q0, q1, q14, q15 = rows[e] if rows else [psi_ref[e, edge_rows(y), :] for y in OUTER_ROWS]
        high = (m4 * q15 + m6a * q14, m6b * q15)
        low = (m7a * q0, m5 * q0 + m7b * q1)
        for r in range(2):
            y0[e, r] = jnp.where(even, high[r], low[r])
            y1[e, r] = jnp.where(even, low[r], high[r])
    even = is_even("gx")
    last, near = slab(NX - 1), slab(NX - 2)
    m0, m2a, m2b = metric_ref[0, last, :], metric_ref[2, near, :], metric_ref[2, last, :]
    m1, m3a, m3b = metric_ref[1, slab(0), :], metric_ref[3, slab(0), :], metric_ref[3, slab(1), :]
    for e in range(FIELDS):
        q6, q7, q0, q1 = psi_ref[e, near, :], psi_ref[e, last, :], psi_ref[e, slab(0), :], psi_ref[e, slab(1), :]
        high = (m0 * q7 + m2a * q6, m2b * q7)
        low = (m3a * q0, m1 * q0 + m3b * q1)
        for r in range(2):
            x0[e, r] = jnp.where(even, high[r], low[r])
            x1[e, r] = jnp.where(even, low[r], high[r])


def first_body(psi_hbm, metric_hbm, x0, x1, y0, y1, zz, far, packed_metric, psi_ref, metric_ref, sems):
    copies = [
        pltpu.make_async_copy(metric_hbm.at[8:12], metric_ref.at[8:12], sems.at[0]),
        pltpu.make_async_copy(psi_hbm, psi_ref, sems.at[1]),
        pltpu.make_async_copy(metric_hbm.at[4:8], metric_ref.at[4:8], sems.at[2]),
        pltpu.make_async_copy(metric_hbm.at[0:4], metric_ref.at[0:4], sems.at[3]),
    ]
    for copy in copies:
        copy.start()
    copies[0].wait()
    pack_metric(metric_ref, packed_metric)
    copies[1].wait()
    groups = pack_edges(psi_ref)
    copies[2].wait()
    copies[3].wait()
    emit_sends(psi_ref, metric_ref, packed_metric, groups, (x0, x1, y0, y1, zz, far))


def from_sides(axis, first, second):
    index = lax.axis_index(axis)
    even = index % 2 == 0
    below = jnp.where(even, second, first)
    above = jnp.where(even, first, second)
    return jnp.where(index > 0, below, 0.0), jnp.where(index < lax.axis_size(axis) - 1, above, 0.0)


def coupled(jac_ref, s, zs):
    out = []
    for f in range(FIELDS):
        c = jac_ref[f, s, :].astype(F32) * zs[0]
        for e in range(1, FIELDS):
            c = c + jac_ref[FIELDS * e + f, s, :].astype(F32) * zs[e]
        out.append(c)
    return out


def window_body(psi_ref, metric_ref, diag_ref, rhs_ref, jac_ref, x0, x1, z0, z1, base_ref):
    lane8 = iota((8, NZ), 1)
    edge = (lane8 < 2) | (lane8 >= NZ - 2)
    walls = []
    for g in range((FIELDS + 1) // 2):
        below, above = from_sides("wa", z0[8 * g : 8 * g + 8, :], z1[8 * g : 8 * g + 8, :])
        walls.append(jnp.where(lane8 % 4 >= 2, below, above))
    lane, row = iota((NY, NZ), 1), iota((NY, NZ), 0)
    for x in range(NX):
        s = slab(x)
        ms = []
        for o, keep in (
            (4, row < NY - 1), (5, row >= 1), (6, row < NY - 2), (7, row >= 2),
            (8, lane < NZ - 1), (9, lane >= 1), (10, lane < NZ - 2), (11, lane >= 2),
        ):
            ms.append(jnp.where(keep, metric_ref[o, s, :], 0.0))
        zs = []
        for e in range(FIELDS):
            q = psi_ref[e, s, :]
            total = row_roll(ms[0] * q, 1) + row_roll(ms[1] * q, -1)
            total = total + (row_roll(ms[2] * q, 2) + row_roll(ms[3] * q, -2))
            total = total + (lane_roll(ms[4] * q, 1) + lane_roll(ms[5] * q, -1))
            total = total + (lane_roll(ms[6] * q, 2) + lane_roll(ms[7] * q, -2))
            for o, step in enumerate((1, -1, 2, -2)):
                if 0 <= x - step < NX:
                    total = total + metric_ref[o, slab(x - step), :] * psi_ref[e, slab(x - step), :]
            tiles = [
                jnp.where(edge, lane_roll(walls[e // 2], -(2 + 64 * (e % 2) + 4 * (2 * x + t))), 0.0) for t in range(2)
            ]
            total = total + jnp.concatenate(tiles, axis=0)
            if x < 2:
                total = total + from_sides("gx", x0[e, x], x1[e, x])[0]
            if x >= NX - 2:
                total = total + from_sides("gx", x0[e, x - NX + 2], x1[e, x - NX + 2])[1]
            zs.append(total)
        d = diag_ref[s, :]
        scale = OMEGA / d
        for f, c in enumerate(coupled(jac_ref, s, zs)):
            q = psi_ref[f, s, :]
            base_ref[f, s, :] = q + (rhs_ref[f, s, :] - d * q + c) * scale


def rows_body(jac_ref, diag_ref, jac_rows, scale_rows, wide):
    for k in range(FIELDS * FIELDS):
        for x in range(NX):
            wide[k, slab(x), :] = jac_ref[k, slab(x), :].astype(F32)
    for i, y in enumerate(OUTER_ROWS):
        scale_rows[i] = OMEGA / diag_ref[edge_rows(y), :]
        for k in range(FIELDS * FIELDS):
            jac_rows[4 * k + i] = wide[k, edge_rows(y), :]


def finish(base_ref, y0, y1, jac_rows, scale_rows, new_ref):
    zs = []
    for e in range(FIELDS):
        sides = [from_sides("gy", y0[e, r], y1[e, r]) for r in range(2)]
        zs.append([sides[0][0], sides[1][0], sides[0][1], sides[1][1]])
    rows = []
    for f in range(FIELDS):
        new_ref[f] = base_ref[f]
        mine = []
        for i, y in enumerate(OUTER_ROWS):
            c = jac_rows[4 * f + i] * zs[0][i]
            for e in range(1, FIELDS):
                c = c + jac_rows[4 * (FIELDS * e + f) + i] * zs[e][i]
            mine.append(base_ref[f, edge_rows(y), :] + c * scale_rows[i])
        for i, y in enumerate(OUTER_ROWS):
            new_ref[f, edge_rows(y), :] = mine[i]
        rows.append(mine)
    return rows


def middle_body(base_ref, y_even, y_odd, jac_rows, scale_rows, metric_ref, packed_metric,
                new_ref, x0, x1, y0, y1, zz, far):
    rows = finish(base_ref, y_even, y_odd, jac_rows, scale_rows, new_ref)
    emit_sends(new_ref, metric_ref, packed_metric, pack_edges(new_ref), (x0, x1, y0, y1, zz, far), rows)


def wall_body(coef_ref, ids_ref, weight_ref, coef_out, weight_out, hot_out, low_out):
    def spread(rows, place):
        at = lax.broadcasted_iota(jnp.int32, (rows, 2 * NZ), 1)
        r = lax.broadcasted_iota(jnp.int32, (rows, 2 * NZ), 0)
        return (at % NZ == place(r) + 4 * (at // NZ)).astype(F32)

    def packed(table, chooser):
        v = lax.dot_general(table, chooser, (((0,), (0,)), ((), ())), precision=lax.Precision.HIGHEST,
                            preferred_element_type=F32)
        return v[:8, :NZ] + v[8:, NZ:]

    chooser = spread(4 * NX, lambda r: 64 * (r // 16) + 8 * (r % NX) + 2 + (r // NX) % 2)
    for c in range(3):
        for g in range((FIELDS + 1) // 2):
            count = 4 * NX if g < FIELDS // 2 else 2 * NX
            start = c * 10 * NX + g * 4 * NX
            coef_out[c, 8 * g : 8 * g + 8, :] = packed(coef_ref[start : start + count, :], chooser[:count])
    chooser = spread(4 * NX, lambda r: 8 * (r % NX) + r // NX)
    lane, row = iota((8, NZ), 1), iota((8, NZ), 0)

    def halves(v):
        return jnp.where(lane < 64, v, lane_roll(row_roll(v, 4), 64))

    on = jnp.where(lax.axis_index("wa") == 0, 1.0, 0.0)
    weight_out[...] = halves(packed(weight_ref[...], chooser)) * on
    ids = halves(packed(ids_ref[...].astype(F32), chooser)).astype(jnp.int32)
    low_out[...] = ids % 16
    owner = ids // 16
    slot = iota((256, NZ), 0)
    for s in range(4):
        hit = slot == jnp.broadcast_to(owner[s : s + 1, :], (256, NZ))
        hot_out[:, NZ * s : NZ * s + NZ] = jnp.where(hit, 1.0, 0.0).astype(jnp.bfloat16)


def last_body(base_ref, y_even, y_odd, jac_rows, scale_rows, coef_ref, weight_ref, hot_ref, low_ref,
              out_hbm, slots_ref, new_ref, high_part, low_part, sem):
    finish(base_ref, y_even, y_odd, jac_rows, scale_rows, new_ref)
    copy = pltpu.make_async_copy(new_ref, out_hbm, sem)
    copy.start()
    lane = iota((8, NZ), 1)
    groups = pack_edges(new_ref)
    low = low_ref[...]
    point = iota((16, NZ), 0)
    for c in range(3):
        v = coef_ref[c, 0:8, :] * groups[0]
        for g in range(1, len(groups)):
            v = v + coef_ref[c, 8 * g : 8 * g + 8, :] * groups[g]
        v = v + lane_roll(v, 64)
        v = jnp.where(lane % 4 == 3, v + lane_roll(v, 1), 0.0)
        v = v + lane_roll(v, -1)
        v = v + lane_roll(v, -2)
        v = jnp.where(lane < 64, v, row_roll(v, 4)) * weight_ref[...]
        for s in range(4):
            here = point == jnp.broadcast_to(low[s : s + 1, :], (16, NZ))
            w = jnp.where(here, jnp.broadcast_to(v[s : s + 1, :], (16, NZ)), 0.0)
            top = w.astype(jnp.bfloat16)
            at = (slice(16 * c, 16 * c + 16), slice(NZ * s, NZ * s + NZ))
            high_part[at] = top
            low_part[at] = (w - top.astype(F32)).astype(jnp.bfloat16)
    hot = hot_ref[...]
    dims = (((1,), (1,)), ((), ()))
    slots_ref[...] = lax.dot_general(hot, high_part[...], dims, preferred_element_type=F32) + lax.dot_general(
        hot, low_part[...], dims, preferred_element_type=F32
    )
    copy.wait()


def sum_body(got_ref, out_ref):
    v = got_ref[...].sum(axis=0, keepdims=True)
    for c in range(3):
        out_ref[c : c + 1, :] = v[:, 16 * c : 16 * c + 16]


def run(body, args, outs, scratch=(), sems=(), far=(), far_outs=()):
    hbm = pl.BlockSpec(memory_space=pltpu.HBM)
    args = [pltpu.with_memory_space_constraint(v, pltpu.HBM) if i in far else v for i, v in enumerate(args)]
    return pl.pallas_call(
        body,
        out_shape=[jax.ShapeDtypeStruct(s, d) for s, d in outs],
        in_specs=[hbm if i in far else VMEM for i in range(len(args))],
        out_specs=[hbm if i in far_outs else VMEM for i in range(len(outs))],
        scratch_shapes=[pltpu.VMEM(s, d) for s, d in scratch] + [pltpu.SemaphoreType.DMA(s) for s in sems],
        compiler_params=pltpu.CompilerParams(vmem_limit_bytes=24 << 20),
        cost_estimate=pl.CostEstimate(flops=1000000, bytes_accessed=1000000, transcendentals=0),
    )(*args)


EDGE_X = ((FIELDS, 2, NY, NZ), F32)
EDGE_Y = ((FIELDS, 2, NX, NZ), F32)
EDGE_Z = ((24, NZ), F32)
EDGE_FAR = ((FAR_ROWS, NZ), F32)
SENDS = [EDGE_X, EDGE_X, EDGE_Y, EDGE_Y, EDGE_Z, EDGE_FAR]
FIELD = ((FIELDS, ROWS, NZ), F32)


def exchange(sends):
    x0, x1, y0, y1, zz, far = sends
    def swap(v, axis, odd):
        return lax.ppermute(v, axis, pairs(lax.axis_size(axis), odd))
    two_hops = swap(x1, "gx", 1)
    one_hop = swap(x0, "gx", 0)
    far = swap(far, "wa", 1)
    y = swap(y0, "gy", 0), swap(y1, "gy", 1)
    zz, one_hop = lax.optimization_barrier((zz, one_hop))
    x = one_hop, two_hops
    z = swap(zz, "wa", 0), far
    return (*x, *y, *z)


def local(adjoint_init, objective_grad, diag_term, face_metric, flux_jacobian, wall_coef, ffd_ids, ffd_weight):
    psi = adjoint_init.reshape(FIELDS, ROWS, NZ)
    rhs = objective_grad.reshape(FIELDS, ROWS, NZ)
    diag = diag_term.reshape(ROWS, NZ)
    metric = face_metric.reshape(12, ROWS, NZ)
    jac = flux_jacobian.reshape(FIELDS * FIELDS, ROWS, NZ)
    *sends, packed_metric, psi, metric = run(
        first_body, (psi, metric), SENDS + [((24, NZ), F32), FIELD, ((12, ROWS, NZ), F32)], sems=[(4,)], far=(0, 1)
    )
    wall = run(
        wall_body,
        (wall_coef.reshape(30 * NX, NY), ffd_ids.reshape(4 * NX, NY), ffd_weight.reshape(4 * NX, NY)),
        [((3, 24, NZ), F32), ((8, NZ), F32), ((256, 512), jnp.bfloat16), ((8, NZ), jnp.int32)],
    )
    rows = run(
        rows_body, (jac, diag), [((4 * FIELDS * FIELDS, NX, NZ), F32), ((4, NX, NZ), F32)],
        scratch=[((FIELDS * FIELDS, ROWS, NZ), F32)],
    )
    for step in range(SWEEPS):
        x_even, x_odd, y_even, y_odd, z_even, z_odd = exchange(sends)
        (base,) = run(window_body, (psi, metric, diag, rhs, jac, x_even, x_odd, z_even, z_odd), [FIELD])
        if step == 1:
            base, wall = lax.optimization_barrier((base, wall))
        if step < SWEEPS - 1:
            psi, *sends = run(middle_body, (base, y_even, y_odd, *rows, metric, packed_metric), [FIELD] + SENDS)
        else:
            psi, slots = run(
                last_body, (base, y_even, y_odd, *rows, *wall), [FIELD, ((256, 48), F32)],
                scratch=[FIELD, ((48, 512), jnp.bfloat16), ((48, 512), jnp.bfloat16)], sems=[()], far_outs=(0,),
            )
    got = lax.all_to_all(slots.reshape(256, 1, 48), AXES, 0, 0).reshape(256, 48)
    (grad,) = run(sum_body, (got,), [((3, 16), F32)])
    return psi.reshape(adjoint_init.shape), grad


def solution(mesh):
    in_specs = (
        P(None, "gx", "gy", "wa"),
        P(None, "gx", "gy", "wa"),
        P("gx", "gy", "wa"),
        P(None, "gx", "gy", "wa"),
        P(None, None, "gx", "gy", "wa"),
        P(None, None, "gx", "gy"),
        P(None, "gx", "gy"),
        P(None, "gx", "gy"),
    )
    out_specs = (P(None, "gx", "gy", "wa"), P(None, AXES))
    return jax.shard_map(local, mesh=mesh, in_specs=in_specs, out_specs=out_specs, check_vma=False)
```

```python
import jax
import jax.numpy as jnp
from jax import lax
from jax.experimental import pallas as pl
from jax.experimental.pallas import tpu as pltpu
from jax.sharding import PartitionSpec as P

SWEEPS = 4
OMEGA = 0.6
AXES = ("gx", "gy", "wa")
FIELDS, NX, NY, NZ = 5, 8, 16, 128
ROWS = NX * NY
FAR_ROWS = 88
OUTER_ROWS = (0, 1, NY - 2, NY - 1)
F32 = jnp.float32
VMEM = pl.BlockSpec(memory_space=pltpu.VMEM)


def pairs(count, odd):
    table = {}
    for i in range(0, count, 2):
        a, b = (i + odd) % count, (i + 1 + odd) % count
        table[a], table[b] = b, a
    return sorted(table.items())


def iota(shape, dim):
    return lax.broadcasted_iota(jnp.int32, shape, dim)


def lane_roll(v, shift):
    return pltpu.roll(v, shift % NZ, axis=1) if shift % NZ else v


def row_roll(v, shift):
    return pltpu.roll(v, shift % v.shape[0], axis=0)


def is_even(axis):
    return lax.axis_index(axis) % 2 == 0


def slab(x):
    return slice(NY * x, NY * (x + 1))


def edge_rows(y):
    return pl.ds(y, NX, stride=NY)


def tile_rows(x, t):
    return slice(NY * x + 8 * t, NY * x + 8 * t + 8)


def pack_edges(psi_ref):
    lane = iota((8, NZ), 1)
    edge = (lane < 2) | (lane >= NZ - 2)
    groups = []
    for g in range((FIELDS + 1) // 2):
        total = jnp.zeros((8, NZ), F32)
        for e in range(2 * g, min(2 * g + 2, FIELDS)):
            for x in range(NX):
                for t in range(2):
                    v = jnp.where(edge, psi_ref[e, tile_rows(x, t), :], 0.0)
                    total = total + lane_roll(v, 2 + 64 * (e % 2) + 4 * (2 * x + t))
        groups.append(total)
    return groups


def pack_metric(metric_ref, out_ref):
    lane = iota((8, NZ), 1)
    same = jnp.zeros((8, NZ), F32)
    after = jnp.zeros((8, NZ), F32)
    before = jnp.zeros((8, NZ), F32)
    for x in range(NX):
        for t in range(2):
            j, rows = 4 * (2 * x + t), tile_rows(x, t)
            v = jnp.where(lane >= NZ - 2, metric_ref[10, rows, :], jnp.where(lane < 2, metric_ref[11, rows, :], 0.0))
            same = same + lane_roll(v, 2 + j)
            after = after + lane_roll(jnp.where(lane == NZ - 1, metric_ref[8, rows, :], 0.0), 1 + j)
            before = before + lane_roll(jnp.where(lane == 0, metric_ref[9, rows, :], 0.0), 3 + j)
    for i, v in enumerate((same, after, before)):
        out_ref[8 * i : 8 * i + 8, :] = v + lane_roll(v, 64)


def emit_sends(psi_ref, metric_ref, packed_metric, groups, sends, rows=None, loads=()):
    x0, x1, y0, y1, zz, far = sends
    lane = iota((8, NZ), 1)
    same, after, before = (packed_metric[8 * i : 8 * i + 8, :] for i in range(3))
    for g, p in enumerate(groups):
        v = same * p + after * lane_roll(p, -1) + before * lane_roll(p, 1)
        v = jnp.where(lane % 4 < 2, lane_roll(v, -2), lane_roll(v, 2))
        zz[8 * g : 8 * g + 8, :] = v
        far[8 * g : 8 * g + 8, :] = v
    far[24:, :] = jnp.zeros((FAR_ROWS - 24, NZ), F32)
    for copy in loads[:1]:
        copy.wait()
    even = is_even("gy")
    m4, m6a, m6b = metric_ref[4, edge_rows(15), :], metric_ref[6, edge_rows(14), :], metric_ref[6, edge_rows(15), :]
    m5, m7a, m7b = metric_ref[5, edge_rows(0), :], metric_ref[7, edge_rows(0), :], metric_ref[7, edge_rows(1), :]
    for e in range(FIELDS):
        q0, q1, q14, q15 = rows[e] if rows else [psi_ref[e, edge_rows(y), :] for y in OUTER_ROWS]
        high = (m4 * q15 + m6a * q14, m6b * q15)
        low = (m7a * q0, m5 * q0 + m7b * q1)
        for r in range(2):
            y0[e, r] = jnp.where(even, high[r], low[r])
            y1[e, r] = jnp.where(even, low[r], high[r])
    for copy in loads[1:]:
        copy.wait()
    even = is_even("gx")
    last, near = slab(NX - 1), slab(NX - 2)
    m0, m2a, m2b = metric_ref[0, last, :], metric_ref[2, near, :], metric_ref[2, last, :]
    m1, m3a, m3b = metric_ref[1, slab(0), :], metric_ref[3, slab(0), :], metric_ref[3, slab(1), :]
    for e in range(FIELDS):
        q6, q7, q0, q1 = psi_ref[e, near, :], psi_ref[e, last, :], psi_ref[e, slab(0), :], psi_ref[e, slab(1), :]
        high = (m0 * q7 + m2a * q6, m2b * q7)
        low = (m3a * q0, m1 * q0 + m3b * q1)
        for r in range(2):
            x0[e, r] = jnp.where(even, high[r], low[r])
            x1[e, r] = jnp.where(even, low[r], high[r])


def first_body(psi_hbm, metric_hbm, x0, x1, y0, y1, zz, far, packed_metric, psi_ref, metric_ref, sems):
    copies = [
        pltpu.make_async_copy(metric_hbm.at[8:12], metric_ref.at[8:12], sems.at[0]),
        pltpu.make_async_copy(psi_hbm, psi_ref, sems.at[1]),
        pltpu.make_async_copy(metric_hbm.at[4:8], metric_ref.at[4:8], sems.at[2]),
        pltpu.make_async_copy(metric_hbm.at[0:4], metric_ref.at[0:4], sems.at[3]),
    ]
    for copy in copies:
        copy.start()
    copies[0].wait()
    pack_metric(metric_ref, packed_metric)
    copies[1].wait()
    groups = pack_edges(psi_ref)
    emit_sends(psi_ref, metric_ref, packed_metric, groups, (x0, x1, y0, y1, zz, far), loads=copies[2:])


def from_sides(axis, first, second):
    index = lax.axis_index(axis)
    even = index % 2 == 0
    below = jnp.where(even, second, first)
    above = jnp.where(even, first, second)
    return jnp.where(index > 0, below, 0.0), jnp.where(index < lax.axis_size(axis) - 1, above, 0.0)


def coupled(jac_ref, s, zs):
    out = []
    for f in range(FIELDS):
        c = jac_ref[f, s, :].astype(F32) * zs[0]
        for e in range(1, FIELDS):
            c = c + jac_ref[FIELDS * e + f, s, :].astype(F32) * zs[e]
        out.append(c)
    return out


def window_body(psi_ref, metric_ref, diag_ref, rhs_ref, jac_ref, x0, x1, z0, z1, base_ref):
    lane8 = iota((8, NZ), 1)
    edge = (lane8 < 2) | (lane8 >= NZ - 2)
    walls = []
    for g in range((FIELDS + 1) // 2):
        below, above = from_sides("wa", z0[8 * g : 8 * g + 8, :], z1[8 * g : 8 * g + 8, :])
        walls.append(jnp.where(lane8 % 4 >= 2, below, above))
    lane, row = iota((NY, NZ), 1), iota((NY, NZ), 0)
    for x in range(NX):
        s = slab(x)
        ms = []
        for o, keep in (
            (4, row < NY - 1), (5, row >= 1), (6, row < NY - 2), (7, row >= 2),
            (8, lane < NZ - 1), (9, lane >= 1), (10, lane < NZ - 2), (11, lane >= 2),
        ):
            ms.append(jnp.where(keep, metric_ref[o, s, :], 0.0))
        zs = []
        for e in range(FIELDS):
            q = psi_ref[e, s, :]
            total = row_roll(ms[0] * q, 1) + row_roll(ms[1] * q, -1)
            total = total + (row_roll(ms[2] * q, 2) + row_roll(ms[3] * q, -2))
            total = total + (lane_roll(ms[4] * q, 1) + lane_roll(ms[5] * q, -1))
            total = total + (lane_roll(ms[6] * q, 2) + lane_roll(ms[7] * q, -2))
            for o, step in enumerate((1, -1, 2, -2)):
                if 0 <= x - step < NX:
                    total = total + metric_ref[o, slab(x - step), :] * psi_ref[e, slab(x - step), :]
            tiles = [
                jnp.where(edge, lane_roll(walls[e // 2], -(2 + 64 * (e % 2) + 4 * (2 * x + t))), 0.0) for t in range(2)
            ]
            total = total + jnp.concatenate(tiles, axis=0)
            if x < 2:
                total = total + from_sides("gx", x0[e, x], x1[e, x])[0]
            if x >= NX - 2:
                total = total + from_sides("gx", x0[e, x - NX + 2], x1[e, x - NX + 2])[1]
            zs.append(total)
        d = diag_ref[s, :]
        scale = OMEGA / d
        for f, c in enumerate(coupled(jac_ref, s, zs)):
            q = psi_ref[f, s, :]
            base_ref[f, s, :] = q + (rhs_ref[f, s, :] - d * q + c) * scale


def rows_body(jac_ref, diag_ref, jac_rows, scale_rows, wide):
    for k in range(FIELDS * FIELDS):
        for x in range(NX):
            wide[k, slab(x), :] = jac_ref[k, slab(x), :].astype(F32)
    for i, y in enumerate(OUTER_ROWS):
        scale_rows[i] = OMEGA / diag_ref[edge_rows(y), :]
        for k in range(FIELDS * FIELDS):
            jac_rows[4 * k + i] = wide[k, edge_rows(y), :]


def finish(base_ref, y0, y1, jac_rows, scale_rows, new_ref, in_place=True, out=()):
    zs = []
    for e in range(FIELDS):
        sides = [from_sides("gy", y0[e, r], y1[e, r]) for r in range(2)]
        zs.append([sides[0][0], sides[1][0], sides[0][1], sides[1][1]])
    rows = []
    for f in range(FIELDS):
        if not in_place:
            new_ref[f] = base_ref[f]
        mine = []
        for i, y in enumerate(OUTER_ROWS):
            c = jac_rows[4 * f + i] * zs[0][i]
            for e in range(1, FIELDS):
                c = c + jac_rows[4 * (FIELDS * e + f) + i] * zs[e][i]
            mine.append(base_ref[f, edge_rows(y), :] + c * scale_rows[i])
        for i, y in enumerate(OUTER_ROWS):
            new_ref[f, edge_rows(y), :] = mine[i]
        if out:
            out[f].start()
        rows.append(mine)
    return rows


def middle_body(base_ref, y_even, y_odd, jac_rows, scale_rows, metric_ref, packed_metric,
                new_ref, x0, x1, y0, y1, zz, far):
    rows = finish(base_ref, y_even, y_odd, jac_rows, scale_rows, new_ref)
    emit_sends(new_ref, metric_ref, packed_metric, pack_edges(new_ref), (x0, x1, y0, y1, zz, far), rows)


def wall_body(coef_ref, ids_ref, weight_ref, coef_out, weight_out, hot_out, low_out):
    def spread(rows, place):
        at = lax.broadcasted_iota(jnp.int32, (rows, 2 * NZ), 1)
        r = lax.broadcasted_iota(jnp.int32, (rows, 2 * NZ), 0)
        return (at % NZ == place(r) + 4 * (at // NZ)).astype(F32)

    def packed(table, chooser):
        v = lax.dot_general(table, chooser, (((0,), (0,)), ((), ())), precision=lax.Precision.HIGHEST,
                            preferred_element_type=F32)
        return v[:8, :NZ] + v[8:, NZ:]

    chooser = spread(4 * NX, lambda r: 64 * (r // 16) + 8 * (r % NX) + 2 + (r // NX) % 2)
    for c in range(3):
        for g in range((FIELDS + 1) // 2):
            count = 4 * NX if g < FIELDS // 2 else 2 * NX
            start = c * 10 * NX + g * 4 * NX
            coef_out[c, 8 * g : 8 * g + 8, :] = packed(coef_ref[start : start + count, :], chooser[:count])
    chooser = spread(4 * NX, lambda r: 8 * (r % NX) + r // NX)
    lane, row = iota((8, NZ), 1), iota((8, NZ), 0)

    def halves(v):
        return jnp.where(lane < 64, v, lane_roll(row_roll(v, 4), 64))

    on = jnp.where(lax.axis_index("wa") == 0, 1.0, 0.0)
    weight_out[...] = halves(packed(weight_ref[...], chooser)) * on
    ids = halves(packed(ids_ref[...].astype(F32), chooser)).astype(jnp.int32)
    low_out[...] = ids % 16
    owner = ids // 16
    slot = iota((256, NZ), 0)
    for s in range(4):
        hit = slot == jnp.broadcast_to(owner[s : s + 1, :], (256, NZ))
        hot_out[:, NZ * s : NZ * s + NZ] = jnp.where(hit, 1.0, 0.0).astype(jnp.bfloat16)


def last_body(base_ref, y_even, y_odd, jac_rows, scale_rows, coef_ref, weight_ref, hot_ref, low_ref,
              out_hbm, slots_ref, new_ref, high_part, low_part, sems):
    copies = [pltpu.make_async_copy(new_ref.at[f], out_hbm.at[f], sems.at[f]) for f in range(FIELDS)]
    finish(base_ref, y_even, y_odd, jac_rows, scale_rows, new_ref, in_place=False, out=copies)
    lane = iota((8, NZ), 1)
    groups = pack_edges(new_ref)
    low = low_ref[...]
    point = iota((16, NZ), 0)
    for c in range(3):
        v = coef_ref[c, 0:8, :] * groups[0]
        for g in range(1, len(groups)):
            v = v + coef_ref[c, 8 * g : 8 * g + 8, :] * groups[g]
        v = v + lane_roll(v, 64)
        v = jnp.where(lane % 4 == 3, v + lane_roll(v, 1), 0.0)
        v = v + lane_roll(v, -1)
        v = v + lane_roll(v, -2)
        v = jnp.where(lane < 64, v, row_roll(v, 4)) * weight_ref[...]
        for s in range(4):
            here = point == jnp.broadcast_to(low[s : s + 1, :], (16, NZ))
            w = jnp.where(here, jnp.broadcast_to(v[s : s + 1, :], (16, NZ)), 0.0)
            top = w.astype(jnp.bfloat16)
            at = (slice(16 * c, 16 * c + 16), slice(NZ * s, NZ * s + NZ))
            high_part[at] = top
            low_part[at] = (w - top.astype(F32)).astype(jnp.bfloat16)
    hot = hot_ref[...]
    dims = (((1,), (1,)), ((), ()))
    slots_ref[...] = lax.dot_general(hot, high_part[...], dims, preferred_element_type=F32) + lax.dot_general(
        hot, low_part[...], dims, preferred_element_type=F32
    )
    for copy in copies:
        copy.wait()


def sum_body(got_ref, out_ref):
    v = got_ref[...].sum(axis=0, keepdims=True)
    for c in range(3):
        out_ref[c : c + 1, :] = v[:, 16 * c : 16 * c + 16]


def run(body, args, outs, scratch=(), sems=(), far=(), far_outs=(), aliases=None):
    hbm = pl.BlockSpec(memory_space=pltpu.HBM)
    args = [pltpu.with_memory_space_constraint(v, pltpu.HBM) if i in far else v for i, v in enumerate(args)]
    return pl.pallas_call(
        body,
        out_shape=[jax.ShapeDtypeStruct(s, d) for s, d in outs],
        in_specs=[hbm if i in far else VMEM for i in range(len(args))],
        out_specs=[hbm if i in far_outs else VMEM for i in range(len(outs))],
        scratch_shapes=[pltpu.VMEM(s, d) for s, d in scratch] + [pltpu.SemaphoreType.DMA(s) for s in sems],
        input_output_aliases=aliases or {},
        compiler_params=pltpu.CompilerParams(vmem_limit_bytes=24 << 20),
        cost_estimate=pl.CostEstimate(flops=1000000, bytes_accessed=1000000, transcendentals=0),
    )(*args)


EDGE_X = ((FIELDS, 2, NY, NZ), F32)
EDGE_Y = ((FIELDS, 2, NX, NZ), F32)
EDGE_Z = ((24, NZ), F32)
EDGE_FAR = ((FAR_ROWS, NZ), F32)
SENDS = [EDGE_X, EDGE_X, EDGE_Y, EDGE_Y, EDGE_Z, EDGE_FAR]
FIELD = ((FIELDS, ROWS, NZ), F32)


def exchange(sends):
    x0, x1, y0, y1, zz, far = sends
    def swap(v, axis, odd):
        return lax.ppermute(v, axis, pairs(lax.axis_size(axis), odd))
    two_hops = swap(x1, "gx", 1)
    one_hop = swap(x0, "gx", 0)
    far = swap(far, "wa", 1)
    y = swap(y0, "gy", 0), swap(y1, "gy", 1)
    zz, one_hop = lax.optimization_barrier((zz, one_hop))
    x = one_hop, two_hops
    z = swap(zz, "wa", 0), far
    return (*x, *y, *z)


def local(adjoint_init, objective_grad, diag_term, face_metric, flux_jacobian, wall_coef, ffd_ids, ffd_weight):
    psi = adjoint_init.reshape(FIELDS, ROWS, NZ)
    rhs = objective_grad.reshape(FIELDS, ROWS, NZ)
    diag = diag_term.reshape(ROWS, NZ)
    metric = face_metric.reshape(12, ROWS, NZ)
    jac = flux_jacobian.reshape(FIELDS * FIELDS, ROWS, NZ)
    *sends, packed_metric, psi, metric = run(
        first_body, (psi, metric), SENDS + [((24, NZ), F32), FIELD, ((12, ROWS, NZ), F32)], sems=[(4,)], far=(0, 1)
    )
    wall = run(
        wall_body,
        (wall_coef.reshape(30 * NX, NY), ffd_ids.reshape(4 * NX, NY), ffd_weight.reshape(4 * NX, NY)),
        [((3, 24, NZ), F32), ((8, NZ), F32), ((256, 512), jnp.bfloat16), ((8, NZ), jnp.int32)],
    )
    rows = run(
        rows_body, (jac, diag), [((4 * FIELDS * FIELDS, NX, NZ), F32), ((4, NX, NZ), F32)],
        scratch=[((FIELDS * FIELDS, ROWS, NZ), F32)],
    )
    for step in range(SWEEPS):
        x_even, x_odd, y_even, y_odd, z_even, z_odd = exchange(sends)
        (base,) = run(window_body, (psi, metric, diag, rhs, jac, x_even, x_odd, z_even, z_odd), [FIELD])
        if step == 1:
            base, wall = lax.optimization_barrier((base, wall))
        if step < SWEEPS - 1:
            psi, *sends = run(
                middle_body, (base, y_even, y_odd, *rows, metric, packed_metric), [FIELD] + SENDS, aliases={0: 0}
            )
        else:
            psi, slots = run(
                last_body, (base, y_even, y_odd, *rows, *wall), [FIELD, ((256, 48), F32)],
                scratch=[FIELD, ((48, 512), jnp.bfloat16), ((48, 512), jnp.bfloat16)], sems=[(FIELDS,)], far_outs=(0,),
            )
    got = lax.all_to_all(slots.reshape(256, 1, 48), AXES, 0, 0).reshape(256, 48)
    (grad,) = run(sum_body, (got,), [((3, 16), F32)])
    return psi.reshape(adjoint_init.shape), grad


def solution(mesh):
    in_specs = (
        P(None, "gx", "gy", "wa"),
        P(None, "gx", "gy", "wa"),
        P("gx", "gy", "wa"),
        P(None, "gx", "gy", "wa"),
        P(None, None, "gx", "gy", "wa"),
        P(None, None, "gx", "gy"),
        P(None, "gx", "gy"),
        P(None, "gx", "gy"),
    )
    out_specs = (P(None, "gx", "gy", "wa"), P(None, AXES))
    return jax.shard_map(local, mesh=mesh, in_specs=in_specs, out_specs=out_specs, check_vma=False)
```

```python
import jax
import jax.numpy as jnp
from jax import lax
from jax.experimental import pallas as pl
from jax.experimental.pallas import tpu as pltpu
from jax.sharding import PartitionSpec as P

SWEEPS = 4
OMEGA = 0.6
AXES = ("gx", "gy", "wa")
FIELDS, NX, NY, NZ = 5, 8, 16, 128
ROWS = NX * NY
FAR_ROWS = 88
OUTER_ROWS = (0, 1, NY - 2, NY - 1)
SPAN_METRICS = ((4, NY - 1), (6, NY - 2), (6, NY - 1), (5, 0), (7, 0), (7, 1))
F32 = jnp.float32
VMEM = pl.BlockSpec(memory_space=pltpu.VMEM)


def pairs(count, odd):
    table = {}
    for i in range(0, count, 2):
        a, b = (i + odd) % count, (i + 1 + odd) % count
        table[a], table[b] = b, a
    return sorted(table.items())


def iota(shape, dim):
    return lax.broadcasted_iota(jnp.int32, shape, dim)


def lane_roll(v, shift):
    return pltpu.roll(v, shift % NZ, axis=1) if shift % NZ else v


def row_roll(v, shift):
    return pltpu.roll(v, shift % v.shape[0], axis=0)


def is_even(axis):
    return lax.axis_index(axis) % 2 == 0


def slab(x):
    return slice(NY * x, NY * (x + 1))


def edge_rows(y):
    return pl.ds(y, NX, stride=NY)


def tile_rows(x, t):
    return slice(NY * x + 8 * t, NY * x + 8 * t + 8)


def pack_edges(psi_ref):
    lane = iota((8, NZ), 1)
    edge = (lane < 2) | (lane >= NZ - 2)
    groups = []
    for g in range((FIELDS + 1) // 2):
        total = jnp.zeros((8, NZ), F32)
        for e in range(2 * g, min(2 * g + 2, FIELDS)):
            for x in range(NX):
                for t in range(2):
                    v = jnp.where(edge, psi_ref[e, tile_rows(x, t), :], 0.0)
                    total = total + lane_roll(v, 2 + 64 * (e % 2) + 4 * (2 * x + t))
        groups.append(total)
    return groups


def pack_metric(metric_ref, out_ref):
    lane = iota((8, NZ), 1)
    same = jnp.zeros((8, NZ), F32)
    after = jnp.zeros((8, NZ), F32)
    before = jnp.zeros((8, NZ), F32)
    for x in range(NX):
        for t in range(2):
            j, rows = 4 * (2 * x + t), tile_rows(x, t)
            v = jnp.where(lane >= NZ - 2, metric_ref[10, rows, :], jnp.where(lane < 2, metric_ref[11, rows, :], 0.0))
            same = same + lane_roll(v, 2 + j)
            after = after + lane_roll(jnp.where(lane == NZ - 1, metric_ref[8, rows, :], 0.0), 1 + j)
            before = before + lane_roll(jnp.where(lane == 0, metric_ref[9, rows, :], 0.0), 3 + j)
    for i, v in enumerate((same, after, before)):
        out_ref[8 * i : 8 * i + 8, :] = v + lane_roll(v, 64)


def emit_sends(psi_ref, metric_ref, packed_metric, groups, sends, rows=None, loads=(), metric_rows=None):
    x0, x1, y0, y1, zz, far = sends
    lane = iota((8, NZ), 1)
    same, after, before = (packed_metric[8 * i : 8 * i + 8, :] for i in range(3))
    for g, p in enumerate(groups):
        v = same * p + after * lane_roll(p, -1) + before * lane_roll(p, 1)
        v = jnp.where(lane % 4 < 2, lane_roll(v, -2), lane_roll(v, 2))
        zz[8 * g : 8 * g + 8, :] = v
        far[8 * g : 8 * g + 8, :] = v
    far[24:, :] = jnp.zeros((FAR_ROWS - 24, NZ), F32)
    for copy in loads[:1]:
        copy.wait()
    even = is_even("gy")
    if metric_rows is None:
        m4, m6a, m6b, m5, m7a, m7b = (metric_ref[o, edge_rows(y), :] for o, y in SPAN_METRICS)
    else:
        m4, m6a, m6b, m5, m7a, m7b = (metric_rows[i] for i in range(6))
    for e in range(FIELDS):
        q0, q1, q14, q15 = rows[e] if rows else [psi_ref[e, edge_rows(y), :] for y in OUTER_ROWS]
        high = (m4 * q15 + m6a * q14, m6b * q15)
        low = (m7a * q0, m5 * q0 + m7b * q1)
        for r in range(2):
            y0[e, r] = jnp.where(even, high[r], low[r])
            y1[e, r] = jnp.where(even, low[r], high[r])
    for copy in loads[1:]:
        copy.wait()
    even = is_even("gx")
    last, near = slab(NX - 1), slab(NX - 2)
    m0, m2a, m2b = metric_ref[0, last, :], metric_ref[2, near, :], metric_ref[2, last, :]
    m1, m3a, m3b = metric_ref[1, slab(0), :], metric_ref[3, slab(0), :], metric_ref[3, slab(1), :]
    for e in range(FIELDS):
        q6, q7, q0, q1 = psi_ref[e, near, :], psi_ref[e, last, :], psi_ref[e, slab(0), :], psi_ref[e, slab(1), :]
        high = (m0 * q7 + m2a * q6, m2b * q7)
        low = (m3a * q0, m1 * q0 + m3b * q1)
        for r in range(2):
            x0[e, r] = jnp.where(even, high[r], low[r])
            x1[e, r] = jnp.where(even, low[r], high[r])


def first_body(psi_hbm, metric_hbm, x0, x1, y0, y1, zz, far, packed_metric, psi_ref, metric_ref, sems):
    copies = [
        pltpu.make_async_copy(metric_hbm.at[8:12], metric_ref.at[8:12], sems.at[0]),
        pltpu.make_async_copy(psi_hbm, psi_ref, sems.at[1]),
        pltpu.make_async_copy(metric_hbm.at[4:8], metric_ref.at[4:8], sems.at[2]),
        pltpu.make_async_copy(metric_hbm.at[0:4], metric_ref.at[0:4], sems.at[3]),
    ]
    for copy in copies:
        copy.start()
    copies[0].wait()
    pack_metric(metric_ref, packed_metric)
    copies[1].wait()
    groups = pack_edges(psi_ref)
    emit_sends(psi_ref, metric_ref, packed_metric, groups, (x0, x1, y0, y1, zz, far), loads=copies[2:])


def from_sides(axis, first, second):
    index = lax.axis_index(axis)
    even = index % 2 == 0
    below = jnp.where(even, second, first)
    above = jnp.where(even, first, second)
    return jnp.where(index > 0, below, 0.0), jnp.where(index < lax.axis_size(axis) - 1, above, 0.0)


def coupled(jac_ref, s, zs):
    out = []
    for f in range(FIELDS):
        c = jac_ref[f, s, :].astype(F32) * zs[0]
        for e in range(1, FIELDS):
            c = c + jac_ref[FIELDS * e + f, s, :].astype(F32) * zs[e]
        out.append(c)
    return out


def window_body(psi_ref, metric_ref, diag_ref, rhs_ref, jac_ref, x0, x1, z0, z1, base_ref, rows_ref):
    lane8 = iota((8, NZ), 1)
    edge = (lane8 < 2) | (lane8 >= NZ - 2)
    walls = []
    for g in range((FIELDS + 1) // 2):
        below, above = from_sides("wa", z0[8 * g : 8 * g + 8, :], z1[8 * g : 8 * g + 8, :])
        walls.append(jnp.where(lane8 % 4 >= 2, below, above))
    lane, row = iota((NY, NZ), 1), iota((NY, NZ), 0)
    for x in range(NX):
        s = slab(x)
        ms = []
        for o, keep in (
            (4, row < NY - 1), (5, row >= 1), (6, row < NY - 2), (7, row >= 2),
            (8, lane < NZ - 1), (9, lane >= 1), (10, lane < NZ - 2), (11, lane >= 2),
        ):
            ms.append(jnp.where(keep, metric_ref[o, s, :], 0.0))
        zs = []
        for e in range(FIELDS):
            q = psi_ref[e, s, :]
            total = row_roll(ms[0] * q, 1) + row_roll(ms[1] * q, -1)
            total = total + (row_roll(ms[2] * q, 2) + row_roll(ms[3] * q, -2))
            total = total + (lane_roll(ms[4] * q, 1) + lane_roll(ms[5] * q, -1))
            total = total + (lane_roll(ms[6] * q, 2) + lane_roll(ms[7] * q, -2))
            for o, step in enumerate((1, -1, 2, -2)):
                if 0 <= x - step < NX:
                    total = total + metric_ref[o, slab(x - step), :] * psi_ref[e, slab(x - step), :]
            tiles = [
                jnp.where(edge, lane_roll(walls[e // 2], -(2 + 64 * (e % 2) + 4 * (2 * x + t))), 0.0) for t in range(2)
            ]
            total = total + jnp.concatenate(tiles, axis=0)
            if x < 2:
                total = total + from_sides("gx", x0[e, x], x1[e, x])[0]
            if x >= NX - 2:
                total = total + from_sides("gx", x0[e, x - NX + 2], x1[e, x - NX + 2])[1]
            zs.append(total)
        d = diag_ref[s, :]
        scale = OMEGA / d
        for f, c in enumerate(coupled(jac_ref, s, zs)):
            q = psi_ref[f, s, :]
            base_ref[f, s, :] = q + (rhs_ref[f, s, :] - d * q + c) * scale
    for f in range(FIELDS):
        for i, y in enumerate(OUTER_ROWS):
            rows_ref[4 * f + i] = base_ref[f, edge_rows(y), :]


def rows_body(jac_ref, diag_ref, metric_ref, jac_rows, metric_rows, wide):
    for i, (o, y) in enumerate(SPAN_METRICS):
        metric_rows[i] = metric_ref[o, edge_rows(y), :]
    for k in range(FIELDS * FIELDS):
        for x in range(NX):
            wide[k, slab(x), :] = jac_ref[k, slab(x), :].astype(F32)
    for i, y in enumerate(OUTER_ROWS):
        scale = OMEGA / diag_ref[edge_rows(y), :]
        for k in range(FIELDS * FIELDS):
            jac_rows[4 * k + i] = wide[k, edge_rows(y), :] * scale


def finish(base_ref, base_rows, y0, y1, jac_rows, new_ref, in_place=True, out=()):
    zs = []
    for e in range(FIELDS):
        sides = [from_sides("gy", y0[e, r], y1[e, r]) for r in range(2)]
        zs.append([sides[0][0], sides[1][0], sides[0][1], sides[1][1]])
    rows = []
    for f in range(FIELDS):
        if not in_place:
            new_ref[f] = base_ref[f]
        mine = []
        for i, y in enumerate(OUTER_ROWS):
            c = base_rows[4 * f + i] + jac_rows[4 * f + i] * zs[0][i]
            for e in range(1, FIELDS):
                c = c + jac_rows[4 * (FIELDS * e + f) + i] * zs[e][i]
            mine.append(c)
        for i, y in enumerate(OUTER_ROWS):
            new_ref[f, edge_rows(y), :] = mine[i]
        if out:
            out[f].start()
        rows.append(mine)
    return rows


def middle_body(base_ref, base_rows, y_even, y_odd, jac_rows, metric_rows, metric_ref, packed_metric,
                new_ref, x0, x1, y0, y1, zz, far):
    rows = finish(base_ref, base_rows, y_even, y_odd, jac_rows, new_ref)
    sends = (x0, x1, y0, y1, zz, far)
    emit_sends(new_ref, metric_ref, packed_metric, pack_edges(new_ref), sends, rows, metric_rows=metric_rows)


def wall_body(coef_ref, ids_ref, weight_ref, coef_out, weight_out, hot_out, low_out):
    def spread(rows, place):
        at = lax.broadcasted_iota(jnp.int32, (rows, 2 * NZ), 1)
        r = lax.broadcasted_iota(jnp.int32, (rows, 2 * NZ), 0)
        return (at % NZ == place(r) + 4 * (at // NZ)).astype(F32)

    def packed(table, chooser):
        v = lax.dot_general(table, chooser, (((0,), (0,)), ((), ())), precision=lax.Precision.HIGHEST,
                            preferred_element_type=F32)
        return v[:8, :NZ] + v[8:, NZ:]

    chooser = spread(4 * NX, lambda r: 64 * (r // 16) + 8 * (r % NX) + 2 + (r // NX) % 2)
    for c in range(3):
        for g in range((FIELDS + 1) // 2):
            count = 4 * NX if g < FIELDS // 2 else 2 * NX
            start = c * 10 * NX + g * 4 * NX
            coef_out[c, 8 * g : 8 * g + 8, :] = packed(coef_ref[start : start + count, :], chooser[:count])
    chooser = spread(4 * NX, lambda r: 8 * (r % NX) + r // NX)
    lane, row = iota((8, NZ), 1), iota((8, NZ), 0)

    def halves(v):
        return jnp.where(lane < 64, v, lane_roll(row_roll(v, 4), 64))

    on = jnp.where(lax.axis_index("wa") == 0, 1.0, 0.0)
    weight_out[...] = halves(packed(weight_ref[...], chooser)) * on
    ids = halves(packed(ids_ref[...].astype(F32), chooser)).astype(jnp.int32)
    low_out[...] = ids % 16
    owner = ids // 16
    slot = iota((256, NZ), 0)
    for s in range(4):
        hit = slot == jnp.broadcast_to(owner[s : s + 1, :], (256, NZ))
        hot_out[:, NZ * s : NZ * s + NZ] = jnp.where(hit, 1.0, 0.0).astype(jnp.bfloat16)


def last_body(base_ref, base_rows, y_even, y_odd, jac_rows, coef_ref, weight_ref, hot_ref, low_ref,
              out_hbm, slots_ref, new_ref, high_part, low_part, sems):
    copies = [pltpu.make_async_copy(new_ref.at[f], out_hbm.at[f], sems.at[f]) for f in range(FIELDS)]
    finish(base_ref, base_rows, y_even, y_odd, jac_rows, new_ref, in_place=False, out=copies)
    lane = iota((8, NZ), 1)
    groups = pack_edges(new_ref)
    low = low_ref[...]
    point = iota((16, NZ), 0)
    for c in range(3):
        v = coef_ref[c, 0:8, :] * groups[0]
        for g in range(1, len(groups)):
            v = v + coef_ref[c, 8 * g : 8 * g + 8, :] * groups[g]
        v = v + lane_roll(v, 64)
        v = jnp.where(lane % 4 == 3, v + lane_roll(v, 1), 0.0)
        v = v + lane_roll(v, -1)
        v = v + lane_roll(v, -2)
        v = jnp.where(lane < 64, v, row_roll(v, 4)) * weight_ref[...]
        for s in range(4):
            here = point == jnp.broadcast_to(low[s : s + 1, :], (16, NZ))
            w = jnp.where(here, jnp.broadcast_to(v[s : s + 1, :], (16, NZ)), 0.0)
            top = w.astype(jnp.bfloat16)
            at = (slice(16 * c, 16 * c + 16), slice(NZ * s, NZ * s + NZ))
            high_part[at] = top
            low_part[at] = (w - top.astype(F32)).astype(jnp.bfloat16)
    hot = hot_ref[...]
    dims = (((1,), (1,)), ((), ()))
    slots_ref[...] = lax.dot_general(hot, high_part[...], dims, preferred_element_type=F32) + lax.dot_general(
        hot, low_part[...], dims, preferred_element_type=F32
    )
    for copy in copies:
        copy.wait()


def sum_body(got_ref, out_ref):
    v = got_ref[...].sum(axis=0, keepdims=True)
    for c in range(3):
        out_ref[c : c + 1, :] = v[:, 16 * c : 16 * c + 16]


def run(body, args, outs, scratch=(), sems=(), far=(), far_outs=(), aliases=None):
    hbm = pl.BlockSpec(memory_space=pltpu.HBM)
    args = [pltpu.with_memory_space_constraint(v, pltpu.HBM) if i in far else v for i, v in enumerate(args)]
    return pl.pallas_call(
        body,
        out_shape=[jax.ShapeDtypeStruct(s, d) for s, d in outs],
        in_specs=[hbm if i in far else VMEM for i in range(len(args))],
        out_specs=[hbm if i in far_outs else VMEM for i in range(len(outs))],
        scratch_shapes=[pltpu.VMEM(s, d) for s, d in scratch] + [pltpu.SemaphoreType.DMA(s) for s in sems],
        input_output_aliases=aliases or {},
        compiler_params=pltpu.CompilerParams(vmem_limit_bytes=24 << 20),
        cost_estimate=pl.CostEstimate(flops=1000000, bytes_accessed=1000000, transcendentals=0),
    )(*args)


EDGE_X = ((FIELDS, 2, NY, NZ), F32)
EDGE_Y = ((FIELDS, 2, NX, NZ), F32)
EDGE_Z = ((24, NZ), F32)
EDGE_FAR = ((FAR_ROWS, NZ), F32)
SENDS = [EDGE_X, EDGE_X, EDGE_Y, EDGE_Y, EDGE_Z, EDGE_FAR]
FIELD = ((FIELDS, ROWS, NZ), F32)


def exchange(sends):
    x0, x1, y0, y1, zz, far = sends
    def swap(v, axis, odd):
        return lax.ppermute(v, axis, pairs(lax.axis_size(axis), odd))
    two_hops = swap(x1, "gx", 1)
    one_hop = swap(x0, "gx", 0)
    far = swap(far, "wa", 1)
    y = swap(y0, "gy", 0), swap(y1, "gy", 1)
    zz, one_hop = lax.optimization_barrier((zz, one_hop))
    x = one_hop, two_hops
    z = swap(zz, "wa", 0), far
    return (*x, *y, *z)


def local(adjoint_init, objective_grad, diag_term, face_metric, flux_jacobian, wall_coef, ffd_ids, ffd_weight):
    psi = adjoint_init.reshape(FIELDS, ROWS, NZ)
    rhs = objective_grad.reshape(FIELDS, ROWS, NZ)
    diag = diag_term.reshape(ROWS, NZ)
    metric = face_metric.reshape(12, ROWS, NZ)
    jac = flux_jacobian.reshape(FIELDS * FIELDS, ROWS, NZ)
    *sends, packed_metric, psi, metric = run(
        first_body, (psi, metric), SENDS + [((24, NZ), F32), FIELD, ((12, ROWS, NZ), F32)], sems=[(4,)], far=(0, 1)
    )
    wall = run(
        wall_body,
        (wall_coef.reshape(30 * NX, NY), ffd_ids.reshape(4 * NX, NY), ffd_weight.reshape(4 * NX, NY)),
        [((3, 24, NZ), F32), ((8, NZ), F32), ((256, 512), jnp.bfloat16), ((8, NZ), jnp.int32)],
    )
    jac_rows, metric_rows = run(
        rows_body, (jac, diag, metric), [((4 * FIELDS * FIELDS, NX, NZ), F32), ((6, NX, NZ), F32)],
        scratch=[((FIELDS * FIELDS, ROWS, NZ), F32)],
    )
    for step in range(SWEEPS):
        x_even, x_odd, y_even, y_odd, z_even, z_odd = exchange(sends)
        base, rows = run(
            window_body, (psi, metric, diag, rhs, jac, x_even, x_odd, z_even, z_odd), [FIELD, ((4 * FIELDS, NX, NZ), F32)]
        )
        if step == 1:
            base, wall = lax.optimization_barrier((base, wall))
        if step < SWEEPS - 1:
            psi, *sends = run(
                middle_body, (base, rows, y_even, y_odd, jac_rows, metric_rows, metric, packed_metric), [FIELD] + SENDS, aliases={0: 0}
            )
        else:
            psi, slots = run(
                last_body, (base, rows, y_even, y_odd, jac_rows, *wall), [FIELD, ((256, 48), F32)],
                scratch=[FIELD, ((48, 512), jnp.bfloat16), ((48, 512), jnp.bfloat16)], sems=[(FIELDS,)], far_outs=(0,),
            )
    got = lax.all_to_all(slots.reshape(256, 1, 48), AXES, 0, 0).reshape(256, 48)
    (grad,) = run(sum_body, (got,), [((3, 16), F32)])
    return psi.reshape(adjoint_init.shape), grad


def solution(mesh):
    in_specs = (
        P(None, "gx", "gy", "wa"),
        P(None, "gx", "gy", "wa"),
        P("gx", "gy", "wa"),
        P(None, "gx", "gy", "wa"),
        P(None, None, "gx", "gy", "wa"),
        P(None, None, "gx", "gy"),
        P(None, "gx", "gy"),
        P(None, "gx", "gy"),
    )
    out_specs = (P(None, "gx", "gy", "wa"), P(None, AXES))
    return jax.shard_map(local, mesh=mesh, in_specs=in_specs, out_specs=out_specs, check_vma=False)
```

```python
import jax
import jax.numpy as jnp
from jax import lax
from jax.experimental import pallas as pl
from jax.experimental.pallas import tpu as pltpu
from jax.sharding import PartitionSpec as P

SWEEPS = 4
OMEGA = 0.6
AXES = ("gx", "gy", "wa")
FIELDS, NX, NY, NZ = 5, 8, 16, 128
ROWS = NX * NY
FAR_ROWS = 88
OUTER_ROWS = (0, 1, NY - 2, NY - 1)
SPAN_METRICS = ((4, NY - 1), (6, NY - 2), (6, NY - 1), (5, 0), (7, 0), (7, 1))
F32 = jnp.float32
VMEM = pl.BlockSpec(memory_space=pltpu.VMEM)


def pairs(count, odd):
    table = {}
    for i in range(0, count, 2):
        a, b = (i + odd) % count, (i + 1 + odd) % count
        table[a], table[b] = b, a
    return sorted(table.items())


def iota(shape, dim):
    return lax.broadcasted_iota(jnp.int32, shape, dim)


def lane_roll(v, shift):
    return pltpu.roll(v, shift % NZ, axis=1) if shift % NZ else v


def row_roll(v, shift):
    return pltpu.roll(v, shift % v.shape[0], axis=0)


def is_even(axis):
    return lax.axis_index(axis) % 2 == 0


def slab(x):
    return slice(NY * x, NY * (x + 1))


def edge_rows(y):
    return pl.ds(y, NX, stride=NY)


def tile_rows(x, t):
    return slice(NY * x + 8 * t, NY * x + 8 * t + 8)


def pack_edges(psi_ref):
    lane = iota((8, NZ), 1)
    edge = (lane < 2) | (lane >= NZ - 2)
    groups = []
    for g in range((FIELDS + 1) // 2):
        total = jnp.zeros((8, NZ), F32)
        for e in range(2 * g, min(2 * g + 2, FIELDS)):
            for x in range(NX):
                for t in range(2):
                    v = jnp.where(edge, psi_ref[e, tile_rows(x, t), :], 0.0)
                    total = total + lane_roll(v, 2 + 64 * (e % 2) + 4 * (2 * x + t))
        groups.append(total)
    return groups


def pack_metric(metric_ref, out_ref):
    lane = iota((8, NZ), 1)
    same = jnp.zeros((8, NZ), F32)
    near = jnp.zeros((8, NZ), F32)
    for x in range(NX):
        for t in range(2):
            j, rows = 4 * (2 * x + t), tile_rows(x, t)
            v = jnp.where(lane >= NZ - 2, metric_ref[10, rows, :], jnp.where(lane < 2, metric_ref[11, rows, :], 0.0))
            same = same + lane_roll(v, 2 + j)
            v = jnp.where(lane == NZ - 1, metric_ref[8, rows, :], jnp.where(lane == 0, metric_ref[9, rows, :], 0.0))
            near = near + lane_roll(v, 2 + j)
    after = jnp.where(lane % 4 == 0, lane_roll(near, -1), 0.0)
    before = jnp.where(lane % 4 == 3, lane_roll(near, 1), 0.0)
    for i, v in enumerate((same, after, before)):
        out_ref[8 * i : 8 * i + 8, :] = v + lane_roll(v, 64)


def emit_sends(psi_ref, metric_ref, packed_metric, groups, sends, rows=None, loads=(), metric_rows=None):
    x0, x1, y0, y1, zz, far = sends
    lane = iota((8, NZ), 1)
    same, after, before = (packed_metric[8 * i : 8 * i + 8, :] for i in range(3))
    for g, p in enumerate(groups):
        v = same * p + after * lane_roll(p, -1) + before * lane_roll(p, 1)
        v = jnp.where(lane % 4 < 2, lane_roll(v, -2), lane_roll(v, 2))
        zz[8 * g : 8 * g + 8, :] = v
        far[8 * g : 8 * g + 8, :] = v
    far[24:, :] = jnp.zeros((FAR_ROWS - 24, NZ), F32)
    for copy in loads[:1]:
        copy.wait()
    even = is_even("gy")
    if metric_rows is None:
        m4, m6a, m6b, m5, m7a, m7b = (metric_ref[o, edge_rows(y), :] for o, y in SPAN_METRICS)
    else:
        m4, m6a, m6b, m5, m7a, m7b = (metric_rows[i] for i in range(6))
    for e in range(FIELDS):
        q0, q1, q14, q15 = rows[e] if rows else [psi_ref[e, edge_rows(y), :] for y in OUTER_ROWS]
        high = (m4 * q15 + m6a * q14, m6b * q15)
        low = (m7a * q0, m5 * q0 + m7b * q1)
        for r in range(2):
            y0[e, r] = jnp.where(even, high[r], low[r])
            y1[e, r] = jnp.where(even, low[r], high[r])
    for copy in loads[1:]:
        copy.wait()
    even = is_even("gx")
    last, near = slab(NX - 1), slab(NX - 2)
    m0, m2a, m2b = metric_ref[0, last, :], metric_ref[2, near, :], metric_ref[2, last, :]
    m1, m3a, m3b = metric_ref[1, slab(0), :], metric_ref[3, slab(0), :], metric_ref[3, slab(1), :]
    for e in range(FIELDS):
        q6, q7, q0, q1 = psi_ref[e, near, :], psi_ref[e, last, :], psi_ref[e, slab(0), :], psi_ref[e, slab(1), :]
        high = (m0 * q7 + m2a * q6, m2b * q7)
        low = (m3a * q0, m1 * q0 + m3b * q1)
        for r in range(2):
            x0[e, r] = jnp.where(even, high[r], low[r])
            x1[e, r] = jnp.where(even, low[r], high[r])


def first_body(psi_hbm, metric_hbm, x0, x1, y0, y1, zz, far, packed_metric, psi_ref, metric_ref, sems):
    copies = [
        pltpu.make_async_copy(metric_hbm.at[8:12], metric_ref.at[8:12], sems.at[0]),
        pltpu.make_async_copy(psi_hbm, psi_ref, sems.at[1]),
        pltpu.make_async_copy(metric_hbm.at[4:8], metric_ref.at[4:8], sems.at[2]),
        pltpu.make_async_copy(metric_hbm.at[0:4], metric_ref.at[0:4], sems.at[3]),
    ]
    for copy in copies:
        copy.start()
    copies[0].wait()
    pack_metric(metric_ref, packed_metric)
    copies[1].wait()
    groups = pack_edges(psi_ref)
    emit_sends(psi_ref, metric_ref, packed_metric, groups, (x0, x1, y0, y1, zz, far), loads=copies[2:])


def from_sides(axis, first, second):
    index = lax.axis_index(axis)
    even = index % 2 == 0
    below = jnp.where(even, second, first)
    above = jnp.where(even, first, second)
    return jnp.where(index > 0, below, 0.0), jnp.where(index < lax.axis_size(axis) - 1, above, 0.0)


def coupled(jac_ref, s, zs):
    out = []
    for f in range(FIELDS):
        c = jac_ref[f, s, :].astype(F32) * zs[0]
        for e in range(1, FIELDS):
            c = c + jac_ref[FIELDS * e + f, s, :].astype(F32) * zs[e]
        out.append(c)
    return out


def window_body(psi_ref, metric_ref, diag_ref, rhs_ref, jac_ref, x0, x1, z0, z1, base_ref, rows_ref):
    lane8 = iota((8, NZ), 1)
    edge = (lane8 < 2) | (lane8 >= NZ - 2)
    walls = []
    for g in range((FIELDS + 1) // 2):
        below, above = from_sides("wa", z0[8 * g : 8 * g + 8, :], z1[8 * g : 8 * g + 8, :])
        walls.append(jnp.where(lane8 % 4 >= 2, below, above))
    lane, row = iota((NY, NZ), 1), iota((NY, NZ), 0)
    for x in range(NX):
        s = slab(x)
        ms = []
        for o, keep in (
            (4, row < NY - 1), (5, row >= 1), (6, row < NY - 2), (7, row >= 2),
            (8, lane < NZ - 1), (9, lane >= 1), (10, lane < NZ - 2), (11, lane >= 2),
        ):
            ms.append(jnp.where(keep, metric_ref[o, s, :], 0.0))
        zs = []
        for e in range(FIELDS):
            q = psi_ref[e, s, :]
            total = row_roll(ms[0] * q, 1) + row_roll(ms[1] * q, -1)
            total = total + (row_roll(ms[2] * q, 2) + row_roll(ms[3] * q, -2))
            total = total + (lane_roll(ms[4] * q, 1) + lane_roll(ms[5] * q, -1))
            total = total + (lane_roll(ms[6] * q, 2) + lane_roll(ms[7] * q, -2))
            for o, step in enumerate((1, -1, 2, -2)):
                if 0 <= x - step < NX:
                    total = total + metric_ref[o, slab(x - step), :] * psi_ref[e, slab(x - step), :]
            tiles = [
                jnp.where(edge, lane_roll(walls[e // 2], -(2 + 64 * (e % 2) + 4 * (2 * x + t))), 0.0) for t in range(2)
            ]
            total = total + jnp.concatenate(tiles, axis=0)
            if x < 2:
                total = total + from_sides("gx", x0[e, x], x1[e, x])[0]
            if x >= NX - 2:
                total = total + from_sides("gx", x0[e, x - NX + 2], x1[e, x - NX + 2])[1]
            zs.append(total)
        d = diag_ref[s, :]
        scale = OMEGA / d
        for f, c in enumerate(coupled(jac_ref, s, zs)):
            q = psi_ref[f, s, :]
            base_ref[f, s, :] = q + (rhs_ref[f, s, :] - d * q + c) * scale
    for f in range(FIELDS):
        for i, y in enumerate(OUTER_ROWS):
            rows_ref[4 * f + i] = base_ref[f, edge_rows(y), :]


def rows_body(jac_ref, diag_ref, metric_ref, jac_rows, metric_rows, wide):
    for i, (o, y) in enumerate(SPAN_METRICS):
        metric_rows[i] = metric_ref[o, edge_rows(y), :]
    for k in range(FIELDS * FIELDS):
        for x in range(NX):
            wide[k, slab(x), :] = jac_ref[k, slab(x), :].astype(F32)
    for i, y in enumerate(OUTER_ROWS):
        scale = OMEGA / diag_ref[edge_rows(y), :]
        for k in range(FIELDS * FIELDS):
            jac_rows[4 * k + i] = wide[k, edge_rows(y), :] * scale


def finish(base_ref, base_rows, y0, y1, jac_rows, new_ref, in_place=True, out=()):
    zs = []
    for e in range(FIELDS):
        sides = [from_sides("gy", y0[e, r], y1[e, r]) for r in range(2)]
        zs.append([sides[0][0], sides[1][0], sides[0][1], sides[1][1]])
    rows = []
    for f in range(FIELDS):
        if not in_place:
            new_ref[f] = base_ref[f]
        mine = []
        for i, y in enumerate(OUTER_ROWS):
            c = base_rows[4 * f + i] + jac_rows[4 * f + i] * zs[0][i]
            for e in range(1, FIELDS):
                c = c + jac_rows[4 * (FIELDS * e + f) + i] * zs[e][i]
            mine.append(c)
        for i, y in enumerate(OUTER_ROWS):
            new_ref[f, edge_rows(y), :] = mine[i]
        if out:
            out[f].start()
        rows.append(mine)
    return rows


def middle_body(base_ref, base_rows, y_even, y_odd, jac_rows, metric_rows, metric_ref, packed_metric,
                new_ref, x0, x1, y0, y1, zz, far):
    rows = finish(base_ref, base_rows, y_even, y_odd, jac_rows, new_ref)
    sends = (x0, x1, y0, y1, zz, far)
    emit_sends(new_ref, metric_ref, packed_metric, pack_edges(new_ref), sends, rows, metric_rows=metric_rows)


def wall_body(coef_ref, ids_ref, weight_ref, coef_out, weight_out, hot_out, low_out):
    def spread(rows, place):
        at = lax.broadcasted_iota(jnp.int32, (rows, 2 * NZ), 1)
        r = lax.broadcasted_iota(jnp.int32, (rows, 2 * NZ), 0)
        return (at % NZ == place(r) + 4 * (at // NZ)).astype(F32)

    def packed(table, chooser):
        v = lax.dot_general(table, chooser, (((0,), (0,)), ((), ())), precision=lax.Precision.HIGHEST,
                            preferred_element_type=F32)
        return v[:8, :NZ] + v[8:, NZ:]

    chooser = spread(4 * NX, lambda r: 64 * (r // 16) + 8 * (r % NX) + 2 + (r // NX) % 2)
    for c in range(3):
        for g in range((FIELDS + 1) // 2):
            count = 4 * NX if g < FIELDS // 2 else 2 * NX
            start = c * 10 * NX + g * 4 * NX
            coef_out[c, 8 * g : 8 * g + 8, :] = packed(coef_ref[start : start + count, :], chooser[:count])
    chooser = spread(4 * NX, lambda r: 8 * (r % NX) + r // NX)
    lane, row = iota((8, NZ), 1), iota((8, NZ), 0)

    def halves(v):
        return jnp.where(lane < 64, v, lane_roll(row_roll(v, 4), 64))

    on = jnp.where(lax.axis_index("wa") == 0, 1.0, 0.0)
    weight_out[...] = halves(packed(weight_ref[...], chooser)) * on
    ids = halves(packed(ids_ref[...].astype(F32), chooser)).astype(jnp.int32)
    low_out[...] = ids % 16
    owner = ids // 16
    slot = iota((256, NZ), 0)
    for s in range(4):
        hit = slot == jnp.broadcast_to(owner[s : s + 1, :], (256, NZ))
        hot_out[:, NZ * s : NZ * s + NZ] = jnp.where(hit, 1.0, 0.0).astype(jnp.bfloat16)


def last_body(base_ref, base_rows, y_even, y_odd, jac_rows, coef_ref, weight_ref, hot_ref, low_ref,
              out_hbm, slots_ref, new_ref, parts, sems):
    copies = [pltpu.make_async_copy(new_ref.at[f], out_hbm.at[f], sems.at[f]) for f in range(FIELDS)]
    finish(base_ref, base_rows, y_even, y_odd, jac_rows, new_ref, in_place=False, out=copies)
    lane = iota((8, NZ), 1)
    groups = pack_edges(new_ref)
    low = low_ref[...]
    point = iota((16, NZ), 0)
    for c in range(3):
        v = coef_ref[c, 0:8, :] * groups[0]
        for g in range(1, len(groups)):
            v = v + coef_ref[c, 8 * g : 8 * g + 8, :] * groups[g]
        v = v + lane_roll(v, 64)
        v = jnp.where(lane % 4 == 3, v + lane_roll(v, 1), 0.0)
        v = v + lane_roll(v, -1)
        v = v + lane_roll(v, -2)
        v = jnp.where(lane < 64, v, row_roll(v, 4)) * weight_ref[...]
        for s in range(4):
            here = point == jnp.broadcast_to(low[s : s + 1, :], (16, NZ))
            w = jnp.where(here, jnp.broadcast_to(v[s : s + 1, :], (16, NZ)), 0.0)
            top = w.astype(jnp.bfloat16)
            columns = slice(NZ * s, NZ * s + NZ)
            parts[16 * c : 16 * c + 16, columns] = top
            parts[NZ + 16 * c : NZ + 16 * c + 16, columns] = (w - top.astype(F32)).astype(jnp.bfloat16)
    parts[48:NZ, :] = jnp.zeros((NZ - 48, 512), jnp.bfloat16)
    both = lax.dot_general(hot_ref[...], parts[...], (((1,), (1,)), ((), ())), preferred_element_type=F32)
    slots_ref[...] = both[:, :48] + both[:, NZ : NZ + 48]
    for copy in copies:
        copy.wait()


def sum_body(got_ref, out_ref):
    v = got_ref[...].sum(axis=0, keepdims=True)
    for c in range(3):
        out_ref[c : c + 1, :] = v[:, 16 * c : 16 * c + 16]


def run(body, args, outs, scratch=(), sems=(), far=(), far_outs=(), aliases=None):
    hbm = pl.BlockSpec(memory_space=pltpu.HBM)
    args = [pltpu.with_memory_space_constraint(v, pltpu.HBM) if i in far else v for i, v in enumerate(args)]
    return pl.pallas_call(
        body,
        out_shape=[jax.ShapeDtypeStruct(s, d) for s, d in outs],
        in_specs=[hbm if i in far else VMEM for i in range(len(args))],
        out_specs=[hbm if i in far_outs else VMEM for i in range(len(outs))],
        scratch_shapes=[pltpu.VMEM(s, d) for s, d in scratch] + [pltpu.SemaphoreType.DMA(s) for s in sems],
        input_output_aliases=aliases or {},
        compiler_params=pltpu.CompilerParams(vmem_limit_bytes=24 << 20),
        cost_estimate=pl.CostEstimate(flops=1000000, bytes_accessed=1000000, transcendentals=0),
    )(*args)


EDGE_X = ((FIELDS, 2, NY, NZ), F32)
EDGE_Y = ((FIELDS, 2, NX, NZ), F32)
EDGE_Z = ((24, NZ), F32)
EDGE_FAR = ((FAR_ROWS, NZ), F32)
SENDS = [EDGE_X, EDGE_X, EDGE_Y, EDGE_Y, EDGE_Z, EDGE_FAR]
FIELD = ((FIELDS, ROWS, NZ), F32)


def exchange(sends):
    x0, x1, y0, y1, zz, far = sends
    def swap(v, axis, odd):
        return lax.ppermute(v, axis, pairs(lax.axis_size(axis), odd))
    two_hops = swap(x1, "gx", 1)
    one_hop = swap(x0, "gx", 0)
    far = swap(far, "wa", 1)
    y = swap(y0, "gy", 0), swap(y1, "gy", 1)
    zz, one_hop = lax.optimization_barrier((zz, one_hop))
    x = one_hop, two_hops
    z = swap(zz, "wa", 0), far
    return (*x, *y, *z)


def local(adjoint_init, objective_grad, diag_term, face_metric, flux_jacobian, wall_coef, ffd_ids, ffd_weight):
    psi = adjoint_init.reshape(FIELDS, ROWS, NZ)
    rhs = objective_grad.reshape(FIELDS, ROWS, NZ)
    diag = diag_term.reshape(ROWS, NZ)
    metric = face_metric.reshape(12, ROWS, NZ)
    jac = flux_jacobian.reshape(FIELDS * FIELDS, ROWS, NZ)
    *sends, packed_metric, psi, metric = run(
        first_body, (psi, metric), SENDS + [((24, NZ), F32), FIELD, ((12, ROWS, NZ), F32)], sems=[(4,)], far=(0, 1)
    )
    wall = run(
        wall_body,
        (wall_coef.reshape(30 * NX, NY), ffd_ids.reshape(4 * NX, NY), ffd_weight.reshape(4 * NX, NY)),
        [((3, 24, NZ), F32), ((8, NZ), F32), ((256, 512), jnp.bfloat16), ((8, NZ), jnp.int32)],
    )
    jac_rows, metric_rows = run(
        rows_body, (jac, diag, metric), [((4 * FIELDS * FIELDS, NX, NZ), F32), ((6, NX, NZ), F32)],
        scratch=[((FIELDS * FIELDS, ROWS, NZ), F32)],
    )
    for step in range(SWEEPS):
        x_even, x_odd, y_even, y_odd, z_even, z_odd = exchange(sends)
        base, rows = run(
            window_body, (psi, metric, diag, rhs, jac, x_even, x_odd, z_even, z_odd), [FIELD, ((4 * FIELDS, NX, NZ), F32)]
        )
        if step == 1:
            base, wall = lax.optimization_barrier((base, wall))
        if step < SWEEPS - 1:
            psi, *sends = run(
                middle_body, (base, rows, y_even, y_odd, jac_rows, metric_rows, metric, packed_metric), [FIELD] + SENDS, aliases={0: 0}
            )
        else:
            psi, slots = run(
                last_body, (base, rows, y_even, y_odd, jac_rows, *wall), [FIELD, ((256, 48), F32)],
                scratch=[FIELD, ((NZ + 48, 512), jnp.bfloat16)], sems=[(FIELDS,)], far_outs=(0,),
            )
    got = lax.all_to_all(slots.reshape(256, 1, 48), AXES, 0, 0).reshape(256, 48)
    (grad,) = run(sum_body, (got,), [((3, 16), F32)])
    return psi.reshape(adjoint_init.shape), grad


def solution(mesh):
    in_specs = (
        P(None, "gx", "gy", "wa"),
        P(None, "gx", "gy", "wa"),
        P("gx", "gy", "wa"),
        P(None, "gx", "gy", "wa"),
        P(None, None, "gx", "gy", "wa"),
        P(None, None, "gx", "gy"),
        P(None, "gx", "gy"),
        P(None, "gx", "gy"),
    )
    out_specs = (P(None, "gx", "gy", "wa"), P(None, AXES))
    return jax.shard_map(local, mesh=mesh, in_specs=in_specs, out_specs=out_specs, check_vma=False)
```

```python
import jax
import jax.numpy as jnp
from jax import lax
from jax.experimental import pallas as pl
from jax.experimental.pallas import tpu as pltpu
from jax.sharding import PartitionSpec as P

SWEEPS = 4
OMEGA = 0.6
AXES = ("gx", "gy", "wa")
FIELDS, NX, NY, NZ = 5, 8, 16, 128
ROWS = NX * NY
FAR_ROWS = 160
OUTER_ROWS = (0, 1, NY - 2, NY - 1)
SPAN_METRICS = ((4, NY - 1), (6, NY - 2), (6, NY - 1), (5, 0), (7, 0), (7, 1))
F32 = jnp.float32
VMEM = pl.BlockSpec(memory_space=pltpu.VMEM)


def pairs(count, odd):
    table = {}
    for i in range(0, count, 2):
        a, b = (i + odd) % count, (i + 1 + odd) % count
        table[a], table[b] = b, a
    return sorted(table.items())


def iota(shape, dim):
    return lax.broadcasted_iota(jnp.int32, shape, dim)


def lane_roll(v, shift):
    return pltpu.roll(v, shift % NZ, axis=1) if shift % NZ else v


def row_roll(v, shift):
    return pltpu.roll(v, shift % v.shape[0], axis=0)


def is_even(axis):
    return lax.axis_index(axis) % 2 == 0


def slab(x):
    return slice(NY * x, NY * (x + 1))


def edge_rows(y):
    return pl.ds(y, NX, stride=NY)


def tile_rows(x, t):
    return slice(NY * x + 8 * t, NY * x + 8 * t + 8)


def pack_edges(psi_ref):
    lane = iota((8, NZ), 1)
    edge = (lane < 2) | (lane >= NZ - 2)
    groups = []
    for g in range((FIELDS + 1) // 2):
        total = jnp.zeros((8, NZ), F32)
        for e in range(2 * g, min(2 * g + 2, FIELDS)):
            for x in range(NX):
                for t in range(2):
                    v = jnp.where(edge, psi_ref[e, tile_rows(x, t), :], 0.0)
                    total = total + lane_roll(v, 2 + 64 * (e % 2) + 4 * (2 * x + t))
        groups.append(total)
    return groups


def pack_metric(metric_ref, out_ref):
    lane = iota((8, NZ), 1)
    same = jnp.zeros((8, NZ), F32)
    after = jnp.zeros((8, NZ), F32)
    before = jnp.zeros((8, NZ), F32)
    for x in range(NX):
        for t in range(2):
            j, rows = 4 * (2 * x + t), tile_rows(x, t)
            v = jnp.where(lane >= NZ - 2, metric_ref[10, rows, :], jnp.where(lane < 2, metric_ref[11, rows, :], 0.0))
            same = same + lane_roll(v, 2 + j)
            after = after + lane_roll(jnp.where(lane == NZ - 1, metric_ref[8, rows, :], 0.0), 1 + j)
            before = before + lane_roll(jnp.where(lane == 0, metric_ref[9, rows, :], 0.0), 3 + j)
    for i, v in enumerate((same, after, before)):
        out_ref[8 * i : 8 * i + 8, :] = v + lane_roll(v, 64)


def emit_sends(psi_ref, metric_ref, packed_metric, groups, sends, rows=None, loads=(), metric_rows=None):
    x0, x1, y0, y1, zz, far = sends
    lane = iota((8, NZ), 1)
    same, after, before = (packed_metric[8 * i : 8 * i + 8, :] for i in range(3))
    for g, p in enumerate(groups):
        v = same * p + after * lane_roll(p, -1) + before * lane_roll(p, 1)
        v = jnp.where(lane % 4 < 2, lane_roll(v, -2), lane_roll(v, 2))
        zz[8 * g : 8 * g + 8, :] = v
        far[8 * g : 8 * g + 8, :] = v
    far[24:, :] = jnp.zeros((FAR_ROWS - 24, NZ), F32)
    for copy in loads[:1]:
        copy.wait()
    even = is_even("gy")
    if metric_rows is None:
        m4, m6a, m6b, m5, m7a, m7b = (metric_ref[o, edge_rows(y), :] for o, y in SPAN_METRICS)
    else:
        m4, m6a, m6b, m5, m7a, m7b = (metric_rows[i] for i in range(6))
    for e in range(FIELDS):
        q0, q1, q14, q15 = rows[e] if rows else [psi_ref[e, edge_rows(y), :] for y in OUTER_ROWS]
        high = (m4 * q15 + m6a * q14, m6b * q15)
        low = (m7a * q0, m5 * q0 + m7b * q1)
        for r in range(2):
            y0[e, r] = jnp.where(even, high[r], low[r])
            y1[e, r] = jnp.where(even, low[r], high[r])
    for copy in loads[1:]:
        copy.wait()
    even = is_even("gx")
    last, near = slab(NX - 1), slab(NX - 2)
    m0, m2a, m2b = metric_ref[0, last, :], metric_ref[2, near, :], metric_ref[2, last, :]
    m1, m3a, m3b = metric_ref[1, slab(0), :], metric_ref[3, slab(0), :], metric_ref[3, slab(1), :]
    for e in range(FIELDS):
        q6, q7, q0, q1 = psi_ref[e, near, :], psi_ref[e, last, :], psi_ref[e, slab(0), :], psi_ref[e, slab(1), :]
        high = (m0 * q7 + m2a * q6, m2b * q7)
        low = (m3a * q0, m1 * q0 + m3b * q1)
        for r in range(2):
            x0[e, r] = jnp.where(even, high[r], low[r])
            x1[e, r] = jnp.where(even, low[r], high[r])


def first_body(psi_hbm, metric_hbm, x0, x1, y0, y1, zz, far, packed_metric, psi_ref, metric_ref, sems):
    copies = [
        pltpu.make_async_copy(metric_hbm.at[8:12], metric_ref.at[8:12], sems.at[0]),
        pltpu.make_async_copy(psi_hbm, psi_ref, sems.at[1]),
        pltpu.make_async_copy(metric_hbm.at[4:8], metric_ref.at[4:8], sems.at[2]),
        pltpu.make_async_copy(metric_hbm.at[0:4], metric_ref.at[0:4], sems.at[3]),
    ]
    for copy in copies:
        copy.start()
    copies[0].wait()
    pack_metric(metric_ref, packed_metric)
    copies[1].wait()
    groups = pack_edges(psi_ref)
    emit_sends(psi_ref, metric_ref, packed_metric, groups, (x0, x1, y0, y1, zz, far), loads=copies[2:])


def from_sides(axis, first, second):
    index = lax.axis_index(axis)
    even = index % 2 == 0
    below = jnp.where(even, second, first)
    above = jnp.where(even, first, second)
    return jnp.where(index > 0, below, 0.0), jnp.where(index < lax.axis_size(axis) - 1, above, 0.0)


def coupled(jac_ref, s, zs):
    out = []
    for f in range(FIELDS):
        c = jac_ref[f, s, :].astype(F32) * zs[0]
        for e in range(1, FIELDS):
            c = c + jac_ref[FIELDS * e + f, s, :].astype(F32) * zs[e]
        out.append(c)
    return out


def window_body(psi_ref, metric_ref, diag_ref, rhs_ref, jac_ref, x0, x1, z0, z1, base_ref, rows_ref):
    lane8 = iota((8, NZ), 1)
    edge = (lane8 < 2) | (lane8 >= NZ - 2)
    walls = []
    for g in range((FIELDS + 1) // 2):
        below, above = from_sides("wa", z0[8 * g : 8 * g + 8, :], z1[8 * g : 8 * g + 8, :])
        walls.append(jnp.where(lane8 % 4 >= 2, below, above))
    lane, row = iota((NY, NZ), 1), iota((NY, NZ), 0)
    for x in range(NX):
        s = slab(x)
        ms = []
        for o, keep in (
            (4, row < NY - 1), (5, row >= 1), (6, row < NY - 2), (7, row >= 2),
            (8, lane < NZ - 1), (9, lane >= 1), (10, lane < NZ - 2), (11, lane >= 2),
        ):
            ms.append(jnp.where(keep, metric_ref[o, s, :], 0.0))
        zs = []
        for e in range(FIELDS):
            q = psi_ref[e, s, :]
            total = row_roll(ms[0] * q, 1) + row_roll(ms[1] * q, -1)
            total = total + (row_roll(ms[2] * q, 2) + row_roll(ms[3] * q, -2))
            total = total + (lane_roll(ms[4] * q, 1) + lane_roll(ms[5] * q, -1))
            total = total + (lane_roll(ms[6] * q, 2) + lane_roll(ms[7] * q, -2))
            for o, step in enumerate((1, -1, 2, -2)):
                if 0 <= x - step < NX:
                    total = total + metric_ref[o, slab(x - step), :] * psi_ref[e, slab(x - step), :]
            tiles = [
                jnp.where(edge, lane_roll(walls[e // 2], -(2 + 64 * (e % 2) + 4 * (2 * x + t))), 0.0) for t in range(2)
            ]
            total = total + jnp.concatenate(tiles, axis=0)
            if x < 2:
                total = total + from_sides("gx", x0[e, x], x1[e, x])[0]
            if x >= NX - 2:
                total = total + from_sides("gx", x0[e, x - NX + 2], x1[e, x - NX + 2])[1]
            zs.append(total)
        d = diag_ref[s, :]
        scale = OMEGA / d
        for f, c in enumerate(coupled(jac_ref, s, zs)):
            q = psi_ref[f, s, :]
            base_ref[f, s, :] = q + (rhs_ref[f, s, :] - d * q + c) * scale
    for f in range(FIELDS):
        for i, y in enumerate(OUTER_ROWS):
            rows_ref[4 * f + i] = base_ref[f, edge_rows(y), :]


def rows_body(jac_ref, diag_ref, metric_ref, jac_rows, metric_rows, wide):
    for i, (o, y) in enumerate(SPAN_METRICS):
        metric_rows[i] = metric_ref[o, edge_rows(y), :]
    for k in range(FIELDS * FIELDS):
        for x in range(NX):
            wide[k, slab(x), :] = jac_ref[k, slab(x), :].astype(F32)
    for i, y in enumerate(OUTER_ROWS):
        scale = OMEGA / diag_ref[edge_rows(y), :]
        for k in range(FIELDS * FIELDS):
            jac_rows[4 * k + i] = wide[k, edge_rows(y), :] * scale


def finish(base_ref, base_rows, y0, y1, jac_rows, new_ref, in_place=True, out=()):
    zs = []
    for e in range(FIELDS):
        sides = [from_sides("gy", y0[e, r], y1[e, r]) for r in range(2)]
        zs.append([sides[0][0], sides[1][0], sides[0][1], sides[1][1]])
    rows = []
    for f in range(FIELDS):
        if not in_place:
            new_ref[f] = base_ref[f]
        mine = []
        for i, y in enumerate(OUTER_ROWS):
            c = base_rows[4 * f + i] + jac_rows[4 * f + i] * zs[0][i]
            for e in range(1, FIELDS):
                c = c + jac_rows[4 * (FIELDS * e + f) + i] * zs[e][i]
            mine.append(c)
        for i, y in enumerate(OUTER_ROWS):
            new_ref[f, edge_rows(y), :] = mine[i]
        if out:
            out[f].start()
        rows.append(mine)
    return rows


def middle_body(base_ref, base_rows, y_even, y_odd, jac_rows, metric_rows, metric_ref, packed_metric,
                new_ref, x0, x1, y0, y1, zz, far):
    rows = finish(base_ref, base_rows, y_even, y_odd, jac_rows, new_ref)
    sends = (x0, x1, y0, y1, zz, far)
    emit_sends(new_ref, metric_ref, packed_metric, pack_edges(new_ref), sends, rows, metric_rows=metric_rows)


def wall_body(coef_ref, ids_ref, weight_ref, coef_out, weight_out, hot_out, low_out):
    def spread(rows, place):
        at = lax.broadcasted_iota(jnp.int32, (rows, 2 * NZ), 1)
        r = lax.broadcasted_iota(jnp.int32, (rows, 2 * NZ), 0)
        return (at % NZ == place(r) + 4 * (at // NZ)).astype(F32)

    def packed(table, chooser):
        v = lax.dot_general(table, chooser, (((0,), (0,)), ((), ())), precision=lax.Precision.HIGHEST,
                            preferred_element_type=F32)
        return v[:8, :NZ] + v[8:, NZ:]

    chooser = spread(4 * NX, lambda r: 64 * (r // 16) + 8 * (r % NX) + 2 + (r // NX) % 2)
    for c in range(3):
        for g in range((FIELDS + 1) // 2):
            count = 4 * NX if g < FIELDS // 2 else 2 * NX
            start = c * 10 * NX + g * 4 * NX
            coef_out[c, 8 * g : 8 * g + 8, :] = packed(coef_ref[start : start + count, :], chooser[:count])
    chooser = spread(4 * NX, lambda r: 8 * (r % NX) + r // NX)
    lane, row = iota((8, NZ), 1), iota((8, NZ), 0)

    def halves(v):
        return jnp.where(lane < 64, v, lane_roll(row_roll(v, 4), 64))

    on = jnp.where(lax.axis_index("wa") == 0, 1.0, 0.0)
    weight_out[...] = halves(packed(weight_ref[...], chooser)) * on
    ids = halves(packed(ids_ref[...].astype(F32), chooser)).astype(jnp.int32)
    low_out[...] = ids % 16
    owner = ids // 16
    slot = iota((256, NZ), 0)
    for s in range(4):
        hit = slot == jnp.broadcast_to(owner[s : s + 1, :], (256, NZ))
        hot_out[:, NZ * s : NZ * s + NZ] = jnp.where(hit, 1.0, 0.0).astype(jnp.bfloat16)


def last_body(base_ref, base_rows, y_even, y_odd, jac_rows, coef_ref, weight_ref, hot_ref, low_ref,
              out_hbm, slots_ref, new_ref, high_part, low_part, sems):
    copies = [pltpu.make_async_copy(new_ref.at[f], out_hbm.at[f], sems.at[f]) for f in range(FIELDS)]
    finish(base_ref, base_rows, y_even, y_odd, jac_rows, new_ref, in_place=False, out=copies)
    lane = iota((8, NZ), 1)
    groups = pack_edges(new_ref)
    low = low_ref[...]
    point = iota((16, NZ), 0)
    for c in range(3):
        v = coef_ref[c, 0:8, :] * groups[0]
        for g in range(1, len(groups)):
            v = v + coef_ref[c, 8 * g : 8 * g + 8, :] * groups[g]
        v = v + lane_roll(v, 64)
        v = jnp.where(lane % 4 == 3, v + lane_roll(v, 1), 0.0)
        v = v + lane_roll(v, -1)
        v = v + lane_roll(v, -2)
        v = jnp.where(lane < 64, v, row_roll(v, 4)) * weight_ref[...]
        for s in range(4):
            here = point == jnp.broadcast_to(low[s : s + 1, :], (16, NZ))
            w = jnp.where(here, jnp.broadcast_to(v[s : s + 1, :], (16, NZ)), 0.0)
            top = w.astype(jnp.bfloat16)
            at = (slice(16 * c, 16 * c + 16), slice(NZ * s, NZ * s + NZ))
            high_part[at] = top
            low_part[at] = (w - top.astype(F32)).astype(jnp.bfloat16)
    hot = hot_ref[...]
    dims = (((1,), (1,)), ((), ()))
    slots_ref[...] = lax.dot_general(hot, high_part[...], dims, preferred_element_type=F32) + lax.dot_general(
        hot, low_part[...], dims, preferred_element_type=F32
    )
    for copy in copies:
        copy.wait()


def sum_body(got_ref, out_ref):
    v = got_ref[...].sum(axis=0, keepdims=True)
    for c in range(3):
        out_ref[c : c + 1, :] = v[:, 16 * c : 16 * c + 16]


def run(body, args, outs, scratch=(), sems=(), far=(), far_outs=(), aliases=None):
    hbm = pl.BlockSpec(memory_space=pltpu.HBM)
    args = [pltpu.with_memory_space_constraint(v, pltpu.HBM) if i in far else v for i, v in enumerate(args)]
    return pl.pallas_call(
        body,
        out_shape=[jax.ShapeDtypeStruct(s, d) for s, d in outs],
        in_specs=[hbm if i in far else VMEM for i in range(len(args))],
        out_specs=[hbm if i in far_outs else VMEM for i in range(len(outs))],
        scratch_shapes=[pltpu.VMEM(s, d) for s, d in scratch] + [pltpu.SemaphoreType.DMA(s) for s in sems],
        input_output_aliases=aliases or {},
        compiler_params=pltpu.CompilerParams(vmem_limit_bytes=24 << 20),
        cost_estimate=pl.CostEstimate(flops=1000000, bytes_accessed=1000000, transcendentals=0),
    )(*args)


EDGE_X = ((FIELDS, 2, NY, NZ), F32)
EDGE_Y = ((FIELDS, 2, NX, NZ), F32)
EDGE_Z = ((24, NZ), F32)
EDGE_FAR = ((FAR_ROWS, NZ), F32)
SENDS = [EDGE_X, EDGE_X, EDGE_Y, EDGE_Y, EDGE_Z, EDGE_FAR]
FIELD = ((FIELDS, ROWS, NZ), F32)


def exchange(sends):
    x0, x1, y0, y1, zz, far = sends
    def swap(v, axis, odd):
        return lax.ppermute(v, axis, pairs(lax.axis_size(axis), odd))
    two_hops = swap(x1, "gx", 1)
    far = swap(far, "wa", 1)
    one_hop = swap(x0, "gx", 0)
    y = swap(y0, "gy", 0), swap(y1, "gy", 1)
    zz, two_hops = lax.optimization_barrier((zz, two_hops))
    x = one_hop, two_hops
    z = swap(zz, "wa", 0), far
    return (*x, *y, *z)


def local(adjoint_init, objective_grad, diag_term, face_metric, flux_jacobian, wall_coef, ffd_ids, ffd_weight):
    psi = adjoint_init.reshape(FIELDS, ROWS, NZ)
    rhs = objective_grad.reshape(FIELDS, ROWS, NZ)
    diag = diag_term.reshape(ROWS, NZ)
    metric = face_metric.reshape(12, ROWS, NZ)
    jac = flux_jacobian.reshape(FIELDS * FIELDS, ROWS, NZ)
    *sends, packed_metric, psi, metric = run(
        first_body, (psi, metric), SENDS + [((24, NZ), F32), FIELD, ((12, ROWS, NZ), F32)], sems=[(4,)], far=(0, 1)
    )
    wall = run(
        wall_body,
        (wall_coef.reshape(30 * NX, NY), ffd_ids.reshape(4 * NX, NY), ffd_weight.reshape(4 * NX, NY)),
        [((3, 24, NZ), F32), ((8, NZ), F32), ((256, 512), jnp.bfloat16), ((8, NZ), jnp.int32)],
    )
    jac_rows, metric_rows = run(
        rows_body, (jac, diag, metric), [((4 * FIELDS * FIELDS, NX, NZ), F32), ((6, NX, NZ), F32)],
        scratch=[((FIELDS * FIELDS, ROWS, NZ), F32)],
    )
    for step in range(SWEEPS):
        x_even, x_odd, y_even, y_odd, z_even, z_odd = exchange(sends)
        base, rows = run(
            window_body, (psi, metric, diag, rhs, jac, x_even, x_odd, z_even, z_odd), [FIELD, ((4 * FIELDS, NX, NZ), F32)]
        )
        if step == 1:
            base, wall = lax.optimization_barrier((base, wall))
        if step < SWEEPS - 1:
            psi, *sends = run(
                middle_body, (base, rows, y_even, y_odd, jac_rows, metric_rows, metric, packed_metric), [FIELD] + SENDS, aliases={0: 0}
            )
        else:
            psi, slots = run(
                last_body, (base, rows, y_even, y_odd, jac_rows, *wall), [FIELD, ((256, 48), F32)],
                scratch=[FIELD, ((48, 512), jnp.bfloat16), ((48, 512), jnp.bfloat16)], sems=[(FIELDS,)], far_outs=(0,),
            )
    got = lax.all_to_all(slots.reshape(256, 1, 48), AXES, 0, 0).reshape(256, 48)
    (grad,) = run(sum_body, (got,), [((3, 16), F32)])
    return psi.reshape(adjoint_init.shape), grad


def solution(mesh):
    in_specs = (
        P(None, "gx", "gy", "wa"),
        P(None, "gx", "gy", "wa"),
        P("gx", "gy", "wa"),
        P(None, "gx", "gy", "wa"),
        P(None, None, "gx", "gy", "wa"),
        P(None, None, "gx", "gy"),
        P(None, "gx", "gy"),
        P(None, "gx", "gy"),
    )
    out_specs = (P(None, "gx", "gy", "wa"), P(None, AXES))
    return jax.shard_map(local, mesh=mesh, in_specs=in_specs, out_specs=out_specs, check_vma=False)
```
